32 devices in a mesh: seq: 8 (over y, x, core), stream: 4 (over z).
Axes of the slice: x: 2, y: 2, z: 4, core: 2. Of those that a mesh axis runs over, the one named last changes fastest.
Arguments:
- inputs: bfloat16 [4, 8192, 768], P('stream', 'seq'), may hold values from -11 to 11
- resets: int32 [4, 8192], P('stream', 'seq'), may hold values 0 or 1
- norm_gains: bfloat16 [768, 2], P(('seq', 'stream')), may hold values from 0.5 to 1.5
- norm_biases: bfloat16 [768, 2], P(('seq', 'stream')), may hold values from -1.25 to 1.25
- w_qkv: bfloat16 [768, 2304], P(('seq', 'stream')), may hold values from -1 to 1
- w_feat: bfloat16 [768, 128], P(('seq', 'stream')), may hold values from -0.75 to 0.75
- w_out: bfloat16 [768, 768], P(('seq', 'stream')), may hold values from -0.875 to 0.875
- w_fc: bfloat16 [768, 3072], P(('seq', 'stream')), may hold values from -1 to 1
- w_proj: bfloat16 [3072, 768], P(('seq', 'stream')), may hold values from -0.109375 to 0.109375
- cotangent: bfloat16 [4, 8192, 768], P('stream', 'seq'), may hold values from -6 to 6
Outputs:
- outputs: bfloat16 [4, 8192, 768], P('stream', 'seq')
- input_grad: float32 [4, 8192, 768], P('stream', 'seq')
- grad_gains: float32 [768, 2], P(('seq', 'stream'))
- grad_biases: float32 [768, 2], P(('seq', 'stream'))
- grad_qkv: float32 [768, 2304], P(('seq', 'stream'))
- grad_feat: float32 [768, 128], P(('seq', 'stream'))
- grad_out: float32 [768, 768], P(('seq', 'stream'))
- grad_fc: float32 [768, 3072], P(('seq', 'stream'))
- grad_proj: float32 [3072, 768], P(('seq', 'stream'))
- branch_rms: float32 [4, 3], P('stream')
The draws below stay inside these ranges and needn't reach their ends.
Inputs may be any that keep to these rules, and one draw needn't show every extreme that they name: `resets`: A stream's first token starts a document whether it is marked or not.
All inputs are finite; a program needn't handle non-finite values. No bound on the sum of `resets` on one device may be relied on, other than what follows from the above.
Results may differ from the reference program's by a relative error of at most 0.015.
Values may be sent and summed in bfloat16 or wider, within the bound.
No kernel may reach another device: no remote copies, remote signals or barrier semaphores. Data moves between devices by JAX's collectives and lax.ppermute only.
A program may use at most 256 MiB of HBM per device.

```python
import jax
import jax.numpy as jnp
from jax import lax

D = 768
H = 12
HD = 64
FF = 3072
BLOCK = 64
TOK_DEV = 1024
LENGTH = 8192
STREAMS = 4


def draw_inputs(key, part):
    sample = jax.random.normal(key, (STREAMS, LENGTH, D), jnp.float32)
    sample = jnp.clip(sample, -6.0, 6.0)
    position = jnp.arange(LENGTH, dtype=jnp.float32) / LENGTH
    factor = 0.6 + 1.2 * position
    return (sample * factor[None, :, None]).astype(jnp.bfloat16)


def shared_columns(key, columns):
    entries = jnp.clip(jax.random.normal(jax.random.fold_in(key, 11), (D, columns), jnp.float32), -6.0, 6.0)
    common = jnp.clip(jax.random.normal(jax.random.fold_in(key, 23), (columns,), jnp.float32), -4.0, 4.0)
    return ((entries + 0.5 * common[None, :]) * D ** (-0.5)).astype(jnp.bfloat16)


def draw_w_qkv(key, part):
    return shared_columns(key, 3 * D)


def draw_w_fc(key, part):
    return shared_columns(key, FF)


def touch_ends(values, own_key, low, top_value):
    spot = [jax.random.randint(jax.random.fold_in(own_key, axis), (), 0, length) for axis, length in enumerate(values.shape)]
    widest = values.shape.index(max(values.shape))
    neighbour = spot[:widest] + [(spot[widest] + 1) % values.shape[widest]] + spot[widest + 1:]
    return values.at[tuple(spot)].set(low).at[tuple(neighbour)].set(top_value)


def shard_levels(key, shape, shards, least, high):
    def one(dim, shards_of):
        draws = jax.random.uniform(jax.random.fold_in(jax.random.fold_in(key, 6), dim), (shards_of,), jnp.float32, least / len(shards), high / len(shards))
        return jnp.repeat(jnp.exp(draws), shape[dim] // shards_of).reshape((-1,) + (1,) * (len(shape) - dim - 1))

    level = one(*shards[0])
    for cut in shards[1:]:
        level = level * one(*cut)
    return level


def bell_draw(own_key, shape, deviation, reach, shards=(), kind=jnp.bfloat16):
    values = deviation * jax.random.normal(own_key, shape, jnp.float32)
    if shards:
        values = values * shard_levels(own_key, shape, shards, -0.22, 0.18)
    return jnp.clip(values, -reach, reach).astype(kind)


def setup_inputs(seed: int = 0) -> dict:
    arg_keys = jax.random.split(jax.random.key(seed), 11)
    inputs = draw_inputs(jax.random.fold_in(arg_keys[10], 71), 0)
    resets = touch_ends((jax.random.randint(arg_keys[1], (STREAMS, LENGTH), 0, 2 * TOK_DEV) < 1).astype(jnp.int32), jax.random.fold_in(arg_keys[1], 1), 0, 1)
    norm_gains = jnp.clip(1.0 + 0.1 * jax.random.normal(arg_keys[2], (D, 2), jnp.float32), 0.5, 1.5).astype(jnp.bfloat16)
    norm_biases = bell_draw(arg_keys[3], (D, 2), 0.2, 1.25, ((0, 32),))
    w_qkv = draw_w_qkv(jax.random.fold_in(arg_keys[10], 71), 0)
    w_feat = bell_draw(arg_keys[5], (D, 2 * HD), HD ** -0.5, 0.75, ((0, 32),))
    w_out = bell_draw(arg_keys[6], (D, D), (D // 16) ** -0.5, 0.875, ((0, 32),))
    w_fc = draw_w_fc(jax.random.fold_in(arg_keys[10], 71), 0)
    w_proj = bell_draw(arg_keys[8], (FF, D), FF ** -0.5, 0.109375, ((0, 32),))
    cotangent = bell_draw(arg_keys[9], (STREAMS, LENGTH, D), 1.0, 6.0, ((0, 4), (1, 8)))
    return {"inputs": inputs, "resets": resets, "norm_gains": norm_gains, "norm_biases": norm_biases, "w_qkv": w_qkv, "w_feat": w_feat, "w_out": w_out, "w_fc": w_fc, "w_proj": w_proj, "cotangent": cotangent}


@jax.custom_vjp
def low(v):
    return lax.optimization_barrier(v.astype(jnp.bfloat16)).astype(jnp.float32)

@jax.custom_vjp
def low_back(v):
    return v

def low_keep(v):
    return (low(v), None)

def low_pass(kept, grad):
    return (grad,)

def back_keep(v):
    return (v, None)

def back_low(kept, grad):
    return (low(grad),)
low.defvjp(low_keep, low_pass)
low_back.defvjp(back_keep, back_low)
highest = lax.Precision.HIGHEST
epsilon = 1e-05

def layer_norm(values, gain_vec, bias_vec):
    row_mean = lax.optimization_barrier(jnp.mean(values, axis=-1, keepdims=True))
    centered = values - row_mean
    variance = lax.optimization_barrier(jnp.mean(centered * centered, axis=-1, keepdims=True))
    return centered * lax.rsqrt(variance + epsilon) * gain_vec + bias_vec

def feature(logits):
    return jnp.concatenate([jax.nn.softmax(logits, axis=-1), jax.nn.softmax(-logits, axis=-1)], axis=-1)

def block_step(carried, block_in):
    kv_state, norm_state = carried
    phi_q, phi_k, values, reset_rows = block_in
    counts = jnp.cumsum(reset_rows)
    row_ids = jnp.arange(BLOCK)
    doc_mask = ((row_ids[:, None] >= row_ids[None, :]) & (counts[:, None] == counts[None, :])).astype(jnp.float32)
    before = (counts == 0).astype(jnp.float32)
    after_last = (counts == counts[-1]).astype(jnp.float32)
    carry_on = (counts[-1] == 0).astype(jnp.float32)
    scores = jnp.einsum('thf,shf->hts', phi_q, phi_k, precision=highest) * doc_mask[None]
    scores = low_back(low(scores))
    numerator = jnp.einsum('hts,shd->thd', scores, values, precision=highest)
    numerator = numerator + before[:, None, None] * jnp.einsum('thf,hfd->thd', phi_q, kv_state, precision=highest)
    denominator = lax.optimization_barrier(jnp.sum(scores, axis=-1)).T + before[:, None] * jnp.einsum('thf,hf->th', phi_q, norm_state, precision=highest)
    attended = low_back(numerator) / denominator[:, :, None]
    keyed_phi = phi_k * after_last[:, None, None]
    kv_state = carry_on * kv_state + jnp.einsum('shf,shd->hfd', keyed_phi, values, precision=highest)
    norm_state = carry_on * norm_state + lax.optimization_barrier(jnp.sum(keyed_phi, axis=0))
    return ((kv_state, norm_state), attended)

def stream_forward(stream_in, stream_resets, gain_all, bias_all, qkv_w, feat_w, out_w, fc_w, proj_w):
    normed_one = low(layer_norm(stream_in, gain_all[:, 0], bias_all[:, 0]))
    qkv_rows = low_back(low(jnp.dot(normed_one, qkv_w, precision=highest)))
    queries = qkv_rows[:, :D].reshape(LENGTH, H, HD)
    keys_in = qkv_rows[:, D:2 * D].reshape(LENGTH, H, HD)
    values = qkv_rows[:, 2 * D:].reshape(LENGTH, H, HD)
    feature_maps = feat_w.reshape(H, HD, 2 * HD)
    q_logits = low_back(jnp.einsum('thi,hij->thj', queries, feature_maps[:, :, :HD], precision=highest))
    k_logits = low_back(jnp.einsum('thi,hij->thj', keys_in, feature_maps[:, :, HD:], precision=highest))
    phi_q = low(feature(q_logits))
    phi_k = low(feature(k_logits))
    nblocks = LENGTH // BLOCK
    zero_state = (jnp.zeros((H, 2 * HD, HD), jnp.float32), jnp.zeros((H, 2 * HD), jnp.float32))
    blocks_in = (phi_q.reshape(nblocks, BLOCK, H, 2 * HD), phi_k.reshape(nblocks, BLOCK, H, 2 * HD), values.reshape(nblocks, BLOCK, H, HD), stream_resets.reshape(nblocks, BLOCK))
    ignored, attended = lax.scan(jax.checkpoint(block_step), zero_state, blocks_in)
    attn_out = low_back(jnp.dot(low(attended.reshape(LENGTH, D)), out_w, precision=highest))
    middle = stream_in + attn_out
    normed_two = low(layer_norm(middle, gain_all[:, 1], bias_all[:, 1]))
    hidden = low(jax.nn.gelu(low_back(jnp.dot(normed_two, fc_w, precision=highest)), approximate=True))
    mlp_out = low_back(jnp.dot(hidden, proj_w, precision=highest))
    result = middle + mlp_out
    squares = jnp.stack([jnp.sum(attn_out * attn_out), jnp.sum(mlp_out * mlp_out), jnp.sum(result * result)])
    return (result, squares)

def reference(inputs, resets, norm_gains, norm_biases, w_qkv, w_feat, w_out, w_fc, w_proj, cotangent):
    floats = tuple((tensor.astype(jnp.float32) for tensor in (inputs, norm_gains, norm_biases, w_qkv, w_feat, w_out, w_fc, w_proj)))

    def forward(stream_all, gain_all, bias_all, qkv_w, feat_w, out_w, fc_w, proj_w):

        def one_stream(stream_pair):
            return stream_forward(stream_pair[0], stream_pair[1], gain_all, bias_all, qkv_w, feat_w, out_w, fc_w, proj_w)
        result, squares = lax.map(jax.checkpoint(one_stream), (stream_all, resets))
        return (result, squares)
    result, pullback, squares = jax.vjp(forward, *floats, has_aux=True)
    grads = pullback(cotangent.astype(jnp.float32))
    branch_rms = jnp.sqrt(squares / (LENGTH * D))
    return (result.astype(jnp.bfloat16), grads[0], grads[1], grads[2], grads[3], grads[4], grads[5], grads[6], grads[7], branch_rms)
```

```python
import functools

import jax
import jax.numpy as jnp
from jax import lax
from jax.experimental import pallas as pl
from jax.experimental.pallas import tpu as pltpu
from jax.sharding import PartitionSpec as P

BT = 128
TM = 256
epsilon = 1e-05
f32 = jnp.float32
bf16 = jnp.bfloat16
GC = 0.7978845608028654
GA = 0.044715


def mm(a, b):
    return jnp.dot(a, b, preferred_element_type=f32)


def mm_t(a, b):
    return lax.dot_general(a, b, (((1,), (1,)), ((), ())), preferred_element_type=f32)


def mm_f(a, b):
    return lax.dot_general(a, b, (((0,), (0,)), ((), ())), preferred_element_type=f32)


def xor_send(arr, size, mask):
    return lax.ppermute(arr, "seq", [(i, i ^ mask) for i in range(size)])


def stream_rows(shard, depth):
    pieces = [shard] + [
        lax.ppermute(shard, "stream", [(i, (i + d) % depth) for i in range(depth)])
        for d in range(1, depth)
    ]
    ring = pieces[::-1]
    place = lax.axis_index("stream")
    rows = shard.shape[0]
    both = jnp.concatenate(ring + ring, axis=0)
    return lax.dynamic_slice_in_dim(both, (depth - 1 - place) * rows, depth * rows, 0)


def seq_blocks(block, size, flip):
    bits = [1 << b for b in range(1, size.bit_length() - 1)]
    if flip:
        bits = bits[::-1]
    found = {0: block}
    for bit in bits:
        for r in list(found):
            found[r ^ bit] = xor_send(found[r], size, bit)
    for r in list(found):
        found[r ^ 1] = xor_send(found[r], size, 1)
    return [found[r] for r in range(size)]


def to_owner(grad, size, depth, flip):
    nbits = size.bit_length() - 1
    place = lax.axis_index("seq")
    rest = list(range(nbits))[::-1]
    cols = grad.shape[1]
    cur = grad.reshape([2] * nbits + [grad.shape[0] // size, cols])
    order = [0] + (list(range(1, nbits))[::-1] if flip else list(range(1, nbits)))
    for bit in order:
        axis = rest.index(bit)
        own = (place >> bit) & 1
        send = lax.dynamic_index_in_dim(cur, 1 - own, axis, False)
        keep = lax.dynamic_index_in_dim(cur, own, axis, False)
        got = xor_send(send, size, 1 << bit)
        cur = (keep.astype(f32) + got.astype(f32)).astype(bf16)
        rest.pop(axis)
    level = lax.axis_index("stream")
    cur = cur.reshape(depth, cur.shape[0] // depth, cols)
    total = lax.dynamic_index_in_dim(cur, level, 0, False).astype(f32)
    for d in range(1, depth):
        piece = lax.dynamic_index_in_dim(cur, (level + d) % depth, 0, False)
        total = total + lax.ppermute(
            piece, "stream", [(i, (i + d) % depth) for i in range(depth)]
        ).astype(f32)
    return total


def lanes(shape):
    return lax.broadcasted_iota(jnp.int32, shape, len(shape) - 1)


def block_ones(width, part):
    r = lax.broadcasted_iota(jnp.int32, (width, width), 0) // part
    c = lax.broadcasted_iota(jnp.int32, (width, width), 1) // part
    return jnp.where(r == c, 1.0, 0.0).astype(bf16)


def fetch_start(blocks, dest, me, sems, col=0, width=None):
    rows = dest.shape[0] // len(blocks)
    copies = []
    for r, ref in enumerate(blocks):
        off = pl.multiple_of((me ^ r) * rows, 8)
        src = ref if width is None else ref.at[:, pl.ds(col, width)]
        copy = pltpu.make_async_copy(src, dest.at[pl.ds(off, rows), :], sems.at[r])
        copy.start()
        copies.append(copy)
    return copies


def pair_maps(feat_ref, dest, pairs, which):
    width = 128
    lane = lanes((width, width))
    row = lax.broadcasted_iota(jnp.int32, (width, width), 0)
    for p in range(pairs):
        both = feat_ref[pl.ds(p * width, width), :].astype(f32)
        half = width // 2
        other = pltpu.roll(both, half, 1)
        if which == 0:
            signed = jnp.where(lane < half, both, -other)
        else:
            signed = jnp.where(lane < half, other, -both)
        dest[p, :, pl.ds(0, width)] = jnp.where(row < half, signed, 0.0).astype(bf16)
        dest[p, :, pl.ds(width, width)] = jnp.where(row >= half, signed, 0.0).astype(bf16)


def features(logits, ones):
    parts = []
    for j in range(2):
        one = logits[:, j * 128 : (j + 1) * 128]
        low = lanes(one.shape) < 64
        top_a = jnp.max(jnp.where(low, one, -jnp.inf), axis=1, keepdims=True)
        top_b = jnp.max(jnp.where(low, -jnp.inf, one), axis=1, keepdims=True)
        parts.append(jnp.exp(one - jnp.where(low, top_a, top_b)))
    exps = jnp.concatenate(parts, axis=1)
    return (exps / mm(exps.astype(bf16), ones)).astype(bf16)


def augmented(two):
    low = lanes(two.shape) < 64
    one = jnp.ones_like(two)
    return jnp.where(low, two, one), jnp.where(low, one, two)


def pack_states(get, dest, pairs, zsum):
    shape = (128, 128)
    lane = lanes(shape)
    low = lane < 64
    zt = jnp.zeros(shape, f32)
    for p in range(pairs):
        a, b = get(2 * p), get(2 * p + 1)
        dest[p] = jnp.where(low, a, b).astype(bf16)
        if zsum:
            za = jnp.sum(jnp.where(low, 0.0, a), axis=1, keepdims=True)
            zb = jnp.sum(jnp.where(low, b, 0.0), axis=1, keepdims=True)
        else:
            za, zb = a, b
        zt = jnp.where(lane == 64 + 2 * p, za, zt)
        zt = jnp.where(lane == 2 * p + 1, zb, zt)
    dest[pairs] = zt.astype(bf16)


def unpack_states(coef_ref, blocks, put, pairs, split):
    shape = (128, 128)
    lane = lanes(shape)
    low = lane < 64

    def total(i):
        acc = jnp.zeros(shape, f32)
        for r in range(1, len(blocks)):
            acc = acc + coef_ref[r] * blocks[r][i].astype(f32)
        return acc

    zt = total(pairs)
    for p in range(pairs):
        two = total(p)
        za = jnp.sum(jnp.where(lane == 64 + 2 * p, zt, 0.0), axis=1, keepdims=True)
        zb = jnp.sum(jnp.where(lane == 2 * p + 1, zt, 0.0), axis=1, keepdims=True)
        if split:
            put(2 * p, jnp.where(low, two, jnp.where(lane == 64, za, 0.0)))
            put(2 * p + 1, jnp.where(low, jnp.where(lane == 0, zb, 0.0), two))
        else:
            put(2 * p, jnp.where(low, two, za))
            put(2 * p + 1, jnp.where(low, zb, two))


def normed(values, gain, bias):
    mean = jnp.mean(values, axis=1, keepdims=True)
    cent = values - mean
    rstd = lax.rsqrt(jnp.mean(cent * cent, axis=1, keepdims=True) + epsilon)
    hat = cent * rstd
    return hat * gain + bias, hat, rstd


def normed_back(grad, hat, rstd, gain):
    dhat = grad * gain
    return rstd * (
        dhat
        - jnp.mean(dhat, axis=1, keepdims=True)
        - hat * jnp.mean(dhat * hat, axis=1, keepdims=True)
    )


def keys_body(n_seq, pairs, me_ref, cend_ref, x_ref, cnt_ref, *refs):
    width = x_ref.shape[1]
    wa, wb = refs[:n_seq], refs[n_seq : 2 * n_seq]
    (h_ref, k_ref, v_ref, phi_ref, st_ref, gb_ref, w1, w2, maps, state, sems) = refs[2 * n_seq :]
    step = pl.program_id(0)

    @pl.when(step == 0)
    def _():
        me = me_ref[0]
        copies = fetch_start(wa, w1, me, sems.at[0])
        copies += fetch_start(wb, w2, me, sems.at[1])
        for c in copies:
            c.wait()
        gb_ref[...] = w1[:, pl.ds(width + 128, 128)].astype(f32).T[:8]
        pair_maps(w1.at[:, pl.ds(width, 128)], maps, pairs, 1)
        state[...] = jnp.zeros_like(state)

    gb = gb_ref[...]
    out, _, _ = normed(x_ref[...].astype(f32), gb[0:1], gb[2:3])
    h1 = out.astype(bf16)
    h_ref[...] = h1
    keys = mm(h1, w1[:, pl.ds(0, width)]).astype(bf16)
    vals = mm(h1, w2[...]).astype(bf16)
    k_ref[...] = keys
    v_ref[...] = vals
    ones = block_ones(256, 64)
    last = cend_ref[cend_ref.shape[0] - 1]
    used = jnp.where(cnt_ref[...] == last, 1.0, 0.0).astype(bf16)
    for p in range(pairs):
        two = slice(p * 128, (p + 1) * 128)
        phi = features(mm(keys[:, two], maps[p]), ones)
        phi_ref[:, pl.ds(p * 256, 256)] = phi
        va, vb = augmented(vals[:, two])
        state[2 * p] += mm_f(phi[:, :128], va * used)
        state[2 * p + 1] += mm_f(phi[:, 128:], vb * used)

    @pl.when(step == pl.num_programs(0) - 1)
    def _():
        pack_states(lambda h: state[h], st_ref, pairs, False)


def local_body(n_seq, pairs, me_ref, cend_ref, h_ref, phik_ref, v_ref, cnt_ref, row_ref, feat_ref, *refs):
    wq = refs[:n_seq]
    (q_ref, phiq_ref, num_ref, den_ref, srel_ref, w1, maps, state, sems) = refs[n_seq:]
    step = pl.program_id(0)
    width = h_ref.shape[1]

    @pl.when(step == 0)
    def _():
        for c in fetch_start(wq, w1, me_ref[0], sems, 0, width):
            c.wait()
        pair_maps(feat_ref, maps, pairs, 0)
        state[...] = jnp.zeros_like(state)

    queries = mm(h_ref[...], w1[...]).astype(bf16)
    q_ref[...] = queries
    ones = block_ones(256, 64)
    size = h_ref.shape[0]
    cnt = cnt_ref[...]
    first, last = cend_ref[step], cend_ref[step + 1]
    row_id = lax.broadcasted_iota(jnp.int32, (size, size), 0)
    mask = (row_id >= lanes((size, size))) & (cnt == row_ref[...])
    before = jnp.where(cnt == first, 1.0, 0.0)
    after = jnp.where(cnt == last, 1.0, 0.0).astype(bf16)
    keep = jnp.where(first == last, 1.0, 0.0)
    low = lanes((size, 128)) < 64
    for p in range(pairs):
        two = slice(p * 128, (p + 1) * 128)
        phi = features(mm(queries[:, two], maps[p]), ones)
        phiq_ref[:, pl.ds(p * 256, 256)] = phi
        res = []
        for j, val in enumerate(augmented(v_ref[:, two])):
            h = 2 * p + j
            pq = phi[:, j * 128 : (j + 1) * 128]
            pk = phik_ref[:, pl.ds(h * 128, 128)]
            scores = jnp.where(mask, mm_t(pq, pk), 0.0).astype(bf16)
            st = state[h]
            st_b = st.astype(bf16)
            srel_ref[0, h] = st_b
            res.append(mm(scores, val) + before * mm(pq, st_b))
            state[h] = keep * st + mm_f(pk, val * after)
        num_ref[:, two] = jnp.where(low, res[0], res[1])
        den_ref[:, two] = pltpu.roll(jnp.where(low, res[1], res[0]), 64, 1)


def middle_body(
    n_seq, pairs, me_ref, coef_ref, x_ref, dy_ref, num_ref, den_ref, phiq_ref, cnt_ref, gb_ref, *refs
):
    width = x_ref.shape[1]
    wo, wf, wp, sts = (refs[i * n_seq : (i + 1) * n_seq] for i in range(4))
    (
        y_ref, o_ref, h_ref, a_ref, df_ref, dat_ref, dr_ref, dd_ref, sin_ref, gst_ref, sum_ref,
        w_out, w_fc, w_proj, rden, state, stv, sems,
    ) = refs[4 * n_seq :]
    step = pl.program_id(0)
    chunk = 768
    size = x_ref.shape[0]

    @pl.when(step == 0)
    def _():
        me = me_ref[0]
        st_copies = []
        for r in range(1, n_seq):
            c = pltpu.make_async_copy(sts[r], stv.at[r], sems.at[3, r])
            c.start()
            st_copies.append(c)
        copies = fetch_start(wo, w_out, me, sems.at[0], width, width)
        copies += fetch_start(wf, w_fc, me, sems.at[1])
        copies += fetch_start(wp, w_proj, me, sems.at[2])
        for c in st_copies:
            c.wait()

        def put(h, value):
            sin_ref[h] = value.astype(bf16)

        unpack_states(coef_ref, [stv.at[r] for r in range(n_seq)], put, pairs, False)
        state[...] = jnp.zeros_like(state)
        sum_ref[...] = jnp.zeros_like(sum_ref)
        for c in copies:
            c.wait()

    gb = gb_ref[...]
    low = lanes((size, 128)) < 64
    start = jnp.where(cnt_ref[...] == 0.0, 1.0, 0.0)
    start_b = start.astype(bf16)
    for p in range(pairs):
        two = pl.ds(p * 128, 128)
        ra = mm(phiq_ref[:, pl.ds(p * 256, 128)], sin_ref[2 * p])
        rb = mm(phiq_ref[:, pl.ds(p * 256 + 128, 128)], sin_ref[2 * p + 1])
        num = num_ref[:, two] + start * jnp.where(low, ra, rb)
        den = den_ref[:, two] + start * pltpu.roll(jnp.where(low, rb, ra), 64, 1)
        inv = 1.0 / den
        rden[:, two] = inv
        o_ref[:, two] = (num * inv).astype(bf16)
    x = x_ref[...].astype(f32)
    attn = mm(o_ref[...], w_out[...])
    mid = x + attn
    out, hat, rstd = normed(mid, gb[1:2], gb[3:4])
    h2 = out.astype(bf16)
    h_ref[...] = h2
    dy_b = dy_ref[...]
    branch = jnp.zeros((size, width), f32)
    dh2 = jnp.zeros((size, width), f32)
    for c in range(w_fc.shape[1] // chunk):
        cols = pl.ds(c * chunk, chunk)
        fc = mm(h2, w_fc[:, cols])
        square = fc * fc
        tan = jnp.tanh(fc * (GC + GC * GA * square))
        half = 0.5 + 0.5 * tan
        act = (fc * half).astype(bf16)
        a_ref[:, cols] = act
        branch = branch + mm(act, w_proj[cols, :])
        slope = half + fc * (1.0 - half) * half * (2.0 * GC + 6.0 * GC * GA * square)
        dfc = (mm_t(dy_b, w_proj[cols, :]) * slope).astype(bf16)
        df_ref[:, cols] = dfc
        dh2 = dh2 + mm_t(dfc, w_fc[:, cols])
    y = mid + branch
    y_ref[...] = y.astype(bf16)
    sum_ref[0:1] += jnp.sum(attn * attn, axis=0, keepdims=True)
    sum_ref[1:2] += jnp.sum(branch * branch, axis=0, keepdims=True)
    sum_ref[2:3] += jnp.sum(y * y, axis=0, keepdims=True)
    sum_ref[3:4] += jnp.sum(dh2 * hat, axis=0, keepdims=True)
    sum_ref[4:5] += jnp.sum(dh2, axis=0, keepdims=True)
    dr = dy_b.astype(f32) + normed_back(dh2, hat, rstd, gb[1:2])
    dr_ref[...] = dr
    dat = dr.astype(bf16)
    dat_ref[...] = dat
    d_o = mm_t(dat, w_out[...])
    ones = block_ones(256, 64)
    lane = lanes((size, 128))
    for q in range(pairs // 2):
        four = pl.ds(q * 256, 256)
        inv = rden[:, four]
        d_q = d_o[:, q * 256 : (q + 1) * 256]
        prod = d_q * o_ref[:, four].astype(f32)
        hi = prod.astype(bf16)
        lo = (prod - hi.astype(f32)).astype(bf16)
        dden = -(mm(hi, ones) + mm(lo, ones)) * inv
        dnum = (d_q * inv).astype(bf16)
        for i in range(2):
            p = 2 * q + i
            sub = slice(i * 128, (i + 1) * 128)
            dd = pltpu.roll(dden[:, sub], 64, 1)
            dhi = dd.astype(bf16)
            dlo = (dd - dhi.astype(f32)).astype(bf16)
            near = lane & 63
            aux = jnp.where(near == 0, dhi.astype(f32), jnp.where(near == 1, dlo.astype(f32), 0.0)).astype(bf16)
            dn = dnum[:, sub]
            for j, both in enumerate((jnp.where(low, dn, aux), jnp.where(low, aux, dn))):
                h = 2 * p + j
                dd_ref[:, pl.ds(h * 128, 128)] = both
                state[h] += mm_f(phiq_ref[:, pl.ds(h * 128, 128)], both * start_b)

    @pl.when(step == pl.num_programs(0) - 1)
    def _():
        pack_states(lambda h: state[h], gst_ref, pairs, True)


def back_body(
    n_seq, pairs, coef_ref, cend_ref, q_ref, k_ref, v_ref, phiq_ref, phik_ref, dd_ref, srel_ref, sin_ref,
    cnt_ref, row_ref, feat_ref, *refs
):
    sts = refs[:n_seq]
    (dqkv_ref, gfeat_ref, mapq, mapk, state, gq, gk, stv, sems) = refs[n_seq:]
    step = pl.program_id(0)
    nblk = pl.num_programs(0)
    here = nblk - 1 - step

    @pl.when(step == 0)
    def _():
        copies = []
        for r in range(1, n_seq):
            c = pltpu.make_async_copy(sts[r], stv.at[r], sems.at[r])
            c.start()
            copies.append(c)
        pair_maps(feat_ref, mapq, pairs, 0)
        pair_maps(feat_ref, mapk, pairs, 1)
        gq[...] = jnp.zeros_like(gq)
        gk[...] = jnp.zeros_like(gk)
        for c in copies:
            c.wait()

        def put(h, value):
            state[h] = value

        unpack_states(coef_ref, [stv.at[r] for r in range(n_seq)], put, pairs, True)

    size = q_ref.shape[0]
    width = q_ref.shape[1]
    cnt = cnt_ref[...]
    first, last = cend_ref[here], cend_ref[here + 1]
    row_id = lax.broadcasted_iota(jnp.int32, (size, size), 0)
    col_id = lanes((size, size))
    same = cnt == row_ref[...]
    mask = (row_id >= col_id) & same
    mask_t = (col_id >= row_id) & same
    before = jnp.where(cnt == first, 1.0, 0.0).astype(bf16)
    after = jnp.where(cnt == last, 1.0, 0.0).astype(bf16)
    keep = jnp.where(first == last, 1.0, 0.0)
    opened = jnp.where(first == 0.0, 1.0, 0.0)
    ones = block_ones(256, 64)
    low = lanes((size, 128)) < 64
    for p in range(pairs):
        two = pl.ds(p * 128, 128)
        dphi_q, dphi_k, dvs = [], [], []
        for j, val in enumerate(augmented(v_ref[:, two])):
            h = 2 * p + j
            own = pl.ds(h * 128, 128)
            pq, pk, dd = phiq_ref[:, own], phik_ref[:, own], dd_ref[:, own]
            scores_t = jnp.where(mask_t, mm_t(pk, pq), 0.0).astype(bf16)
            dsc = jnp.where(mask, mm_t(dd, val), 0.0).astype(bf16)
            dsc_t = jnp.where(mask_t, mm_t(val, dd), 0.0).astype(bf16)
            st = (srel_ref[0, h].astype(f32) + opened * sin_ref[h].astype(f32)).astype(bf16)
            dst = state[h]
            dst_b = dst.astype(bf16)
            ddw = dd * before
            dphi_q.append(mm(dsc, pk) + mm_t(ddw, st))
            dphi_k.append(mm(dsc_t, pq) + mm_t(val * after, dst_b))
            dvs.append(mm(scores_t, dd) + mm(pk * after, dst_b))
            state[h] = keep * dst + mm_f(pq, ddw)
        dqkv_ref[:, pl.ds(2 * width + p * 128, 128)] = jnp.where(low, dvs[0], dvs[1]).astype(bf16)
        for phi_ref, dphi, rows_ref, maps, acc, base in (
            (phiq_ref, dphi_q, q_ref, mapq, gq, 0),
            (phik_ref, dphi_k, k_ref, mapk, gk, width),
        ):
            phi = phi_ref[:, pl.ds(p * 256, 256)].astype(f32)
            dphi = jnp.concatenate(dphi, axis=1)
            total = mm((phi * dphi).astype(bf16), ones)
            dlog = (phi * (dphi - total)).astype(bf16)
            dqkv_ref[:, pl.ds(base + p * 128, 128)] = mm_t(dlog, maps[p]).astype(bf16)
            acc[p] += mm_f(rows_ref[:, two], dlog)

    @pl.when(step == nblk - 1)
    def _():
        lane = lanes((128, 128))
        row = lax.broadcasted_iota(jnp.int32, (128, 128), 0)
        for p in range(pairs):
            outs = []
            for acc in (gq, gk):
                one = jnp.where(row < 64, acc[p, :, :128], acc[p, :, 128:])
                outs.append(one - pltpu.roll(one, 64, 1))
            gfeat_ref[pl.ds(p * 128, 128), :] = jnp.where(lane < 64, outs[0], -outs[1]).astype(bf16)


def enter_body(n_seq, me_ref, x_ref, dr_ref, dqkv_ref, gb_ref, *refs):
    width = x_ref.shape[1]
    wq, wk, wv = (refs[i * n_seq : (i + 1) * n_seq] for i in range(3))
    (dx_ref, sum_ref, w1, w2, w3, sems) = refs[3 * n_seq :]

    @pl.when(pl.program_id(0) == 0)
    def _():
        me = me_ref[0]
        copies = fetch_start(wq, w1, me, sems.at[0], 0, width)
        copies += fetch_start(wk, w2, me, sems.at[1], 0, width)
        copies += fetch_start(wv, w3, me, sems.at[2])
        sum_ref[...] = jnp.zeros_like(sum_ref)
        for c in copies:
            c.wait()

    gb = gb_ref[...]
    _, hat, rstd = normed(x_ref[...].astype(f32), gb[0:1], gb[2:3])
    dh = (
        mm_t(dqkv_ref[:, pl.ds(0, width)], w1[...])
        + mm_t(dqkv_ref[:, pl.ds(width, width)], w2[...])
        + mm_t(dqkv_ref[:, pl.ds(2 * width, width)], w3[...])
    )
    dx_ref[...] = dr_ref[...] + normed_back(dh, hat, rstd, gb[0:1])
    sum_ref[0:1] += jnp.sum(dh * hat, axis=0, keepdims=True)
    sum_ref[1:2] += jnp.sum(dh, axis=0, keepdims=True)


def whole(*_):
    return pl.BlockSpec(memory_space=pl.ANY)


def smem():
    return pl.BlockSpec(memory_space=pltpu.SMEM)


def rows_spec(size, cols, back=None):
    if back is None:
        return pl.BlockSpec((size, cols), lambda i: (i, 0))
    return pl.BlockSpec((size, cols), lambda i: (back - 1 - i, 0))


def full_spec(shape):
    zeros = (0,) * len(shape)
    return pl.BlockSpec(shape, lambda i: zeros)


def sds(shape, kind):
    return jax.ShapeDtypeStruct(shape, kind)


def cparams():
    return pltpu.CompilerParams(
        dimension_semantics=("arbitrary",), vmem_limit_bytes=58 * 1024 * 1024
    )


def dma(*shape):
    return pltpu.SemaphoreType.DMA(shape)


def shards(n_seq, depth, inputs, resets, norm_gains, norm_biases, w_qkv, w_feat, w_out, w_fc, w_proj, cotangent):
    tokens, width = inputs.shape[1], inputs.shape[2]
    hidden = w_fc.shape[1]
    head_dim = w_feat.shape[1] // 2
    heads = width // head_dim
    pairs = heads // 2
    rows = w_qkv.shape[0]
    nblk = tokens // BT
    x, dy = inputs[0], cotangent[0]
    me = lax.axis_index("seq")
    me_arr = me.reshape(1).astype(jnp.int32)

    norms = jnp.concatenate(
        [norm_gains, norm_biases, jnp.zeros((rows, 124), bf16)], axis=1
    )
    first = jnp.concatenate([w_qkv[:, width : 2 * width], w_feat, norms], axis=1)
    values_w = w_qkv[:, 2 * width :]
    second = jnp.concatenate([w_qkv[:, :width], w_out], axis=1)
    keys_blocks = seq_blocks(stream_rows(first, depth), n_seq, False)
    vals_blocks = seq_blocks(stream_rows(values_w, depth), n_seq, True)
    second_blocks = seq_blocks(stream_rows(second, depth), n_seq, False)
    fc_blocks = seq_blocks(stream_rows(w_fc, depth), n_seq, True)
    proj_blocks = seq_blocks(stream_rows(w_proj, depth), n_seq, False)

    marks = resets[0].reshape(nblk, BT).astype(bf16)
    upper = jnp.triu(jnp.ones((BT, BT), bf16))
    inner = jnp.dot(marks, upper, preferred_element_type=f32)
    ends = jnp.cumsum(inner[:, -1])
    cend = jnp.concatenate([jnp.zeros((1,), f32), ends])
    counts = inner + cend[:-1, None]
    cnt_col = counts.reshape(tokens, 1)
    cnt_row = counts.reshape(1, tokens)
    keep_dev = jnp.where(ends[-1] == 0.0, 1.0, 0.0).astype(f32)
    tile = jnp.full((8, 128), keep_dev, f32)
    keeps = jnp.stack([xor_send(tile, n_seq, r)[0, 0] if r else keep_dev for r in range(n_seq)])
    index = jnp.arange(n_seq) ^ me
    i_abs, j_abs = index[None, :], index[:, None]
    ahead = jnp.where((i_abs > j_abs) & (i_abs < me), keeps[None, :], 1.0)
    coef_f = jnp.where(index < me, jnp.prod(ahead, axis=1), 0.0)
    behind = jnp.where((i_abs < j_abs) & (i_abs > me), keeps[None, :], 1.0)
    coef_b = jnp.where(index > me, jnp.prod(behind, axis=1), 0.0)

    packed = (pairs + 1, 128, 128)
    full = (heads, 128, 128)
    h_one, keys, vals, phi_k, state, gb = pl.pallas_call(
        functools.partial(keys_body, n_seq, pairs),
        name="keys",
        grid=(tokens // TM,),
        in_specs=[smem(), smem(), rows_spec(TM, width), rows_spec(TM, 1)] + [whole()] * (2 * n_seq),
        out_specs=[rows_spec(TM, width)] * 3
        + [rows_spec(TM, 2 * width), full_spec(packed), full_spec((8, width))],
        out_shape=[sds((tokens, width), bf16)] * 3
        + [sds((tokens, 2 * width), bf16), sds(packed, bf16), sds((8, width), f32)],
        scratch_shapes=[
            pltpu.VMEM((width, width + 256), bf16),
            pltpu.VMEM((width, width), bf16),
            pltpu.VMEM((pairs, 128, 256), bf16),
            pltpu.VMEM(full, f32),
            dma(2, n_seq),
        ],
        compiler_params=cparams(),
    )(me_arr, cend, x, cnt_col, *keys_blocks, *vals_blocks)
    feat_full = assembled([b[:, width : width + 128] for b in keys_blocks], me)
    states = seq_blocks(state, n_seq, False)

    queries, phi_q, num, den, srel = pl.pallas_call(
        functools.partial(local_body, n_seq, pairs),
        name="local",
        grid=(nblk,),
        in_specs=[
            smem(), smem(), rows_spec(BT, width), rows_spec(BT, 2 * width), rows_spec(BT, width),
            rows_spec(BT, 1), pl.BlockSpec((1, BT), lambda i: (0, i)), full_spec((width, 128)),
        ]
        + [whole()] * n_seq,
        out_specs=[
            rows_spec(BT, width), rows_spec(BT, 2 * width), rows_spec(BT, width), rows_spec(BT, width),
            pl.BlockSpec((1,) + full, lambda i: (i, 0, 0, 0)),
        ],
        out_shape=[
            sds((tokens, width), bf16), sds((tokens, 2 * width), bf16), sds((tokens, width), f32),
            sds((tokens, width), f32), sds((nblk,) + full, bf16),
        ],
        scratch_shapes=[
            pltpu.VMEM((width, width), bf16),
            pltpu.VMEM((pairs, 128, 256), bf16),
            pltpu.VMEM(full, f32),
            dma(n_seq),
        ],
        compiler_params=cparams(),
    )(me_arr, cend, h_one, phi_k, vals, cnt_col, cnt_row, feat_full, *second_blocks)

    y, att, h_two, act, d_fc, d_att, d_mid, dd, s_in, g_state, sums = pl.pallas_call(
        functools.partial(middle_body, n_seq, pairs),
        name="middle",
        grid=(tokens // TM,),
        in_specs=[
            smem(), smem(), rows_spec(TM, width), rows_spec(TM, width), rows_spec(TM, width),
            rows_spec(TM, width), rows_spec(TM, 2 * width), rows_spec(TM, 1), full_spec((8, width)),
        ]
        + [whole()] * (4 * n_seq),
        out_specs=[
            rows_spec(TM, width), rows_spec(TM, width), rows_spec(TM, width), rows_spec(TM, hidden),
            rows_spec(TM, hidden), rows_spec(TM, width), rows_spec(TM, width), rows_spec(TM, 2 * width),
            full_spec(full), full_spec(packed), full_spec((8, width)),
        ],
        out_shape=[
            sds((tokens, width), bf16), sds((tokens, width), bf16), sds((tokens, width), bf16),
            sds((tokens, hidden), bf16), sds((tokens, hidden), bf16), sds((tokens, width), bf16),
            sds((tokens, width), f32), sds((tokens, 2 * width), bf16), sds(full, bf16), sds(packed, bf16),
            sds((8, width), f32),
        ],
        scratch_shapes=[
            pltpu.VMEM((width, width), bf16),
            pltpu.VMEM((width, hidden), bf16),
            pltpu.VMEM((hidden, width), bf16),
            pltpu.VMEM((TM, width), f32),
            pltpu.VMEM(full, f32),
            pltpu.VMEM((n_seq,) + packed, bf16),
            dma(4, n_seq),
        ],
        compiler_params=cparams(),
    )(
        me_arr, coef_f, x, dy, num, den, phi_q, cnt_col, gb,
        *second_blocks, *fc_blocks, *proj_blocks, *states,
    )

    g_states = seq_blocks(g_state, n_seq, True)
    squares = jnp.sum(sums[:3], axis=1)
    for b in range(n_seq.bit_length() - 1):
        squares = squares + xor_send(squares, n_seq, 1 << b)
    branch_rms = jnp.sqrt(squares / (tokens * n_seq * width)).reshape(1, 3)

    grad_proj = to_owner(mm_f(act, dy).astype(bf16), n_seq, depth, False)
    grad_fc = to_owner(mm_f(h_two, d_fc).astype(bf16), n_seq, depth, True)
    g_out = mm_f(att, d_att).astype(bf16)

    spec = functools.partial(rows_spec, BT, back=nblk)
    d_qkv, g_feat = pl.pallas_call(
        functools.partial(back_body, n_seq, pairs),
        name="back",
        grid=(nblk,),
        in_specs=[
            smem(), smem(), spec(width), spec(width), spec(width), spec(2 * width), spec(2 * width),
            spec(2 * width), pl.BlockSpec((1,) + full, lambda i: (nblk - 1 - i, 0, 0, 0)), full_spec(full),
            spec(1), pl.BlockSpec((1, BT), lambda i: (0, nblk - 1 - i)), full_spec((width, 128)),
        ]
        + [whole()] * n_seq,
        out_specs=[spec(3 * width), full_spec((width, 128))],
        out_shape=[sds((tokens, 3 * width), bf16), sds((width, 128), bf16)],
        scratch_shapes=[
            pltpu.VMEM((pairs, 128, 256), bf16),
            pltpu.VMEM((pairs, 128, 256), bf16),
            pltpu.VMEM(full, f32),
            pltpu.VMEM((pairs, 128, 256), f32),
            pltpu.VMEM((pairs, 128, 256), f32),
            pltpu.VMEM((n_seq,) + packed, bf16),
            dma(n_seq),
        ],
        compiler_params=cparams(),
    )(
        coef_b, cend, queries, keys, vals, phi_q, phi_k, dd, srel, s_in, cnt_col, cnt_row, feat_full,
        *g_states,
    )

    cut = 3 * width // 2
    grad_left = to_owner(mm_f(h_one, d_qkv[:, :cut]).astype(bf16), n_seq, depth, False)
    grad_right = to_owner(
        jnp.concatenate([mm_f(h_one, d_qkv[:, cut:]).astype(bf16), g_feat], axis=1), n_seq, depth, True
    )
    dx, sums_one = pl.pallas_call(
        functools.partial(enter_body, n_seq),
        name="enter",
        grid=(tokens // TM,),
        in_specs=[
            smem(), rows_spec(TM, width), rows_spec(TM, width), rows_spec(TM, 3 * width), full_spec((8, width)),
        ]
        + [whole()] * (3 * n_seq),
        out_specs=[rows_spec(TM, width), full_spec((8, width))],
        out_shape=[sds((tokens, width), f32), sds((8, width), f32)],
        scratch_shapes=[pltpu.VMEM((width, width), bf16)] * 3 + [dma(3, n_seq)],
        compiler_params=cparams(),
    )(me_arr, x, d_mid, d_qkv, gb, *second_blocks, *keys_blocks, *vals_blocks)
    norm_cols = jnp.stack([sums_one[0], sums[3], sums_one[1], sums[4]], axis=1).astype(bf16)
    last = to_owner(
        jnp.concatenate([g_out, norm_cols, jnp.zeros((width, 124), bf16)], axis=1), n_seq, depth, False
    )
    return (
        y[None],
        dx[None],
        last[:, width : width + 2],
        last[:, width + 2 : width + 4],
        jnp.concatenate([grad_left, grad_right[:, : 3 * width - cut]], axis=1),
        grad_right[:, 3 * width - cut :],
        last[:, :width],
        grad_fc,
        grad_proj,
        branch_rms,
    )


def assembled(blocks, me):
    size = len(blocks)
    rows = blocks[0].shape[0]
    out = jnp.zeros((size * rows, blocks[0].shape[1]), blocks[0].dtype)
    for r, block in enumerate(blocks):
        out = lax.dynamic_update_slice_in_dim(out, block, (me ^ r) * rows, 0)
    return out


def solution(mesh):
    both = P(("seq", "stream"), None)
    acts = P("stream", "seq", None)
    placed = (acts, P("stream", "seq"), both, both, both, both, both, both, both, acts)
    return jax.shard_map(
        functools.partial(shards, mesh.shape["seq"], mesh.shape["stream"]),
        mesh=mesh,
        in_specs=placed,
        out_specs=(acts, acts, both, both, both, both, both, both, both, P("stream", None)),
        check_vma=False,
    )
```

```python
import functools

import jax
import jax.numpy as jnp
from jax import lax
from jax.experimental import pallas as pl
from jax.experimental.pallas import tpu as pltpu
from jax.sharding import PartitionSpec as P

BT = 128
TM = 256
epsilon = 1e-05
f32 = jnp.float32
bf16 = jnp.bfloat16
GC = 0.7978845608028654
GA = 0.044715


def mm(a, b):
    return jnp.dot(a, b, preferred_element_type=f32)


def mm_t(a, b):
    return lax.dot_general(a, b, (((1,), (1,)), ((), ())), preferred_element_type=f32)


def mm_f(a, b):
    return lax.dot_general(a, b, (((0,), (0,)), ((), ())), preferred_element_type=f32)


def xor_send(arr, size, mask):
    return lax.ppermute(arr, "seq", [(i, i ^ mask) for i in range(size)])


def after(arr, *deps):
    return lax.optimization_barrier((arr,) + deps)[0]


def stream_send(shard, depth):
    return [shard] + [
        lax.ppermute(shard, "stream", [(i, (i + d) % depth) for i in range(depth)])
        for d in range(1, depth)
    ]


def stream_rows(pieces, depth):
    shard = pieces[0]
    ring = pieces[::-1]
    place = lax.axis_index("stream")
    rows = shard.shape[0]
    both = jnp.concatenate(ring + ring, axis=0)
    return lax.dynamic_slice_in_dim(both, (depth - 1 - place) * rows, depth * rows, 0)


class Spread:
    def __init__(self, block, size, flip):
        self.size = size
        bits = [1 << b for b in range(1, size.bit_length() - 1)]
        self.bits = bits[::-1] if flip else bits
        self.block = block
        self.found = {0: block}

    def near(self, *deps):
        block = after(self.block, *deps) if deps else self.block
        for bit in self.bits:
            self.found[bit] = xor_send(block, self.size, bit)
        return self

    def far(self, *deps):
        for bit in self.bits:
            for r in list(self.found):
                if r ^ bit not in self.found and r < 2 * max(self.bits):
                    src = self.found[r]
                    self.found[r ^ bit] = xor_send(after(src, *deps) if deps else src, self.size, bit)
        return self

    def far_halves(self):
        one, two = self.bits[:2]
        half = self.block.shape[1] // 2
        self.cuts = [self.found[one][:, :half], self.found[two][:, half:]]
        left = xor_send(self.cuts[0], self.size, two)
        right = xor_send(self.cuts[1], self.size, one)
        self.found[one ^ two] = jnp.concatenate([left, right], axis=1)
        return self.far()

    def cores(self, *deps):
        parts = [self.found[2 * r] for r in range(self.size // 2)]
        stack = jnp.stack(parts)
        if deps:
            stack = after(stack, *deps)
        return [stack, xor_send(stack, self.size, 1)]


def beside(parts):
    return parts[0] if len(parts) == 1 else jnp.concatenate(parts, axis=-1)


class Reduce:
    def __init__(self, grads, size, depth, order=None, rest=None):
        self.size, self.depth = size, depth
        nbits = size.bit_length() - 1
        self.rest = list(range(nbits))[::-1] if rest is None else list(rest)
        self.order = list(range(nbits)) if order is None else list(order)
        self.cur = [
            g.reshape([2] * len(self.rest) + [g.shape[0] // 2 ** len(self.rest), g.shape[1]])
            if g.ndim == 2
            else g
            for g in grads
        ]

    def send(self):
        place = lax.axis_index("seq")
        bit = self.order.pop(0)
        axis = self.rest.index(bit)
        own = (place >> bit) & 1
        self.out = beside([lax.dynamic_index_in_dim(c, 1 - own, axis, False) for c in self.cur])
        self.kept = [lax.dynamic_index_in_dim(c, own, axis, False) for c in self.cur]
        self.flight = xor_send(self.out, self.size, 1 << bit)
        self.rest.pop(axis)
        return self

    def add(self, *deps):
        got = after(self.flight, *deps) if deps else self.flight
        self.cur = [(beside(self.kept).astype(f32) + got.astype(f32)).astype(bf16)]
        return self

    def cut(self, at):
        (cur,) = self.cur
        parts = [
            Reduce([cur[..., :at]], self.size, self.depth, self.order, self.rest),
            Reduce([cur[..., at:]], self.size, self.depth, self.order[::-1], self.rest),
        ]
        return parts

    def send_stream(self):
        while self.order:
            self.send().add()
        depth = self.depth
        level = lax.axis_index("stream")
        cur = beside(self.cur)
        self.out = cur
        cur = cur.reshape(depth, cur.shape[0] // depth, cur.shape[1])
        self.total = lax.dynamic_index_in_dim(cur, level, 0, False).astype(f32)
        self.flights = []
        for d in range(1, depth):
            piece = lax.dynamic_index_in_dim(cur, (level + d) % depth, 0, False)
            self.flights.append(
                lax.ppermute(piece, "stream", [(i, (i + d) % depth) for i in range(depth)])
            )
        return self

    def done(self, *deps):
        total = self.total
        for f in self.flights:
            total = total + (after(f, *deps) if deps else f).astype(f32)
        return total


def lanes(shape):
    return lax.broadcasted_iota(jnp.int32, shape, len(shape) - 1)


def block_ones(width, part):
    r = lax.broadcasted_iota(jnp.int32, (width, width), 0) // part
    c = lax.broadcasted_iota(jnp.int32, (width, width), 1) // part
    return jnp.where(r == c, 1.0, 0.0).astype(bf16)


def fetch_start(stacks, dest, me, sems, col=0, width=None, at=0):
    half = stacks[0].shape[0]
    rows = dest.shape[0] // (2 * half)
    width = width or stacks[0].shape[2]
    copies = []
    for c, ref in enumerate(stacks):
        for r in range(half):
            off = pl.multiple_of((me ^ (2 * r + c)) * rows, 8)
            copy = pltpu.make_async_copy(
                ref.at[r, :, pl.ds(col, width)],
                dest.at[pl.ds(off, rows), pl.ds(at, width)],
                sems.at[2 * r + c],
            )
            copy.start()
            copies.append(copy)
    return copies


def pair_maps(feat_ref, dest, pairs, which):
    width = 128
    lane = lanes((width, width))
    row = lax.broadcasted_iota(jnp.int32, (width, width), 0)
    for p in range(pairs):
        both = feat_ref[pl.ds(p * width, width), :].astype(f32)
        half = width // 2
        other = pltpu.roll(both, half, 1)
        if which == 0:
            signed = jnp.where(lane < half, both, -other)
        else:
            signed = jnp.where(lane < half, other, -both)
        dest[p, :, pl.ds(0, width)] = jnp.where(row < half, signed, 0.0).astype(bf16)
        dest[p, :, pl.ds(width, width)] = jnp.where(row >= half, signed, 0.0).astype(bf16)


def features(logits, ones):
    parts = []
    for j in range(2):
        one = logits[:, j * 128 : (j + 1) * 128]
        low = lanes(one.shape) < 64
        top_a = jnp.max(jnp.where(low, one, -jnp.inf), axis=1, keepdims=True)
        top_b = jnp.max(jnp.where(low, -jnp.inf, one), axis=1, keepdims=True)
        parts.append(jnp.exp(one - jnp.where(low, top_a, top_b)))
    exps = jnp.concatenate(parts, axis=1)
    return (exps / mm(exps.astype(bf16), ones)).astype(bf16)


def augmented(two):
    low = lanes(two.shape) < 64
    one = jnp.ones_like(two)
    return jnp.where(low, two, one), jnp.where(low, one, two)


def pack_states(get, dest, pairs, zsum):
    shape = (128, 128)
    lane = lanes(shape)
    low = lane < 64
    zt = jnp.zeros(shape, f32)
    for p in range(pairs):
        a, b = get(2 * p), get(2 * p + 1)
        dest[p] = jnp.where(low, a, b).astype(bf16)
        if zsum:
            za = jnp.sum(jnp.where(low, 0.0, a), axis=1, keepdims=True)
            zb = jnp.sum(jnp.where(low, b, 0.0), axis=1, keepdims=True)
        else:
            za, zb = a, b
        zt = jnp.where(lane == 64 + 2 * p, za, zt)
        zt = jnp.where(lane == 2 * p + 1, zb, zt)
    dest[pairs] = zt.astype(bf16)


def unpack_states(me, keep_ref, blocks, put, base, count, pairs, back):
    shape = (128, 128)
    lane = lanes(shape)
    low = lane < 64
    size = 2 * blocks.shape[1]
    coefs = [None]
    for r in range(1, size):
        j = me ^ r
        c = jnp.where(j > me if back else j < me, 1.0, 0.0)
        for i in range(size):
            between = ((i > me) & (i < j)) if back else ((i > j) & (i < me))
            c = c * jnp.where(between, keep_ref[i], 1.0)
        coefs.append(c)

    def total(i):
        acc = jnp.zeros(shape, f32)
        for r in range(1, size):
            acc = acc + coefs[r] * blocks[r % 2, r // 2, i].astype(f32)
        return acc

    zt = total(pairs)
    for q in range(count):
        p = base + q
        two = total(p)
        za = jnp.sum(jnp.where(lane == 64 + 2 * p, zt, 0.0), axis=1, keepdims=True)
        zb = jnp.sum(jnp.where(lane == 2 * p + 1, zt, 0.0), axis=1, keepdims=True)
        if back:
            put(2 * q, jnp.where(low, two, jnp.where(lane == 64, za, 0.0)))
            put(2 * q + 1, jnp.where(low, jnp.where(lane == 0, zb, 0.0), two))
        else:
            put(2 * q, jnp.where(low, two, za))
            put(2 * q + 1, jnp.where(low, zb, two))


def normed(values, gain, bias):
    mean = jnp.mean(values, axis=1, keepdims=True)
    cent = values - mean
    rstd = lax.rsqrt(jnp.mean(cent * cent, axis=1, keepdims=True) + epsilon)
    hat = cent * rstd
    return hat * gain + bias, hat, rstd


def normed_back(grad, hat, rstd, gain):
    dhat = grad * gain
    return rstd * (
        dhat
        - jnp.mean(dhat, axis=1, keepdims=True)
        - hat * jnp.mean(dhat * hat, axis=1, keepdims=True)
    )


def keys_body(n_seq, pairs, me_ref, cend_ref, x_ref, cnt_ref, *refs):
    width = x_ref.shape[1]
    wl = refs[:2]
    (h_ref, k_ref, v_ref, phi_ref, st_ref, gb_ref, feat_ref, w1, maps, state, sems) = refs[2:]
    step = pl.program_id(0)

    @pl.when(step == 0)
    def _():
        me = me_ref[0]
        copies = fetch_start(wl, w1, me, sems.at[0], width, 2 * width + 256)
        for c in copies:
            c.wait()
        gb_ref[...] = w1[:, pl.ds(2 * width + 128, 128)].astype(f32).T[:8]
        feat_ref[...] = w1[:, pl.ds(2 * width, 128)]
        pair_maps(feat_ref, maps, pairs, 1)
        state[...] = jnp.zeros_like(state)

    gb = gb_ref[...]
    out, _, _ = normed(x_ref[...].astype(f32), gb[0:1], gb[2:3])
    h1 = out.astype(bf16)
    h_ref[...] = h1
    keys = mm(h1, w1[:, pl.ds(0, width)]).astype(bf16)
    vals = mm(h1, w1[:, pl.ds(width, width)]).astype(bf16)
    k_ref[...] = keys
    v_ref[...] = vals
    ones = block_ones(256, 64)
    last = cend_ref[cend_ref.shape[0] - 1]
    used = jnp.where(cnt_ref[...] == last, 1.0, 0.0).astype(bf16)
    for p in range(pairs):
        two = slice(p * 128, (p + 1) * 128)
        phi = features(mm(keys[:, two], maps[p]), ones)
        phi_ref[:, pl.ds(p * 256, 256)] = phi
        va, vb = augmented(vals[:, two])
        state[2 * p] += mm_f(phi[:, :128], va * used)
        state[2 * p + 1] += mm_f(phi[:, 128:], vb * used)

    @pl.when(step == pl.num_programs(0) - 1)
    def _():
        pack_states(lambda h: state[h], st_ref, pairs, False)


def local_body(base, pairs, me_ref, cend_ref, h_ref, phik_ref, v_ref, cnt_ref, row_ref, feat_ref, *refs):
    wq = refs[:2]
    (q_ref, phiq_ref, num_ref, den_ref, srel_ref, state, w1, maps, sems) = refs[-9:]
    step = pl.program_id(0)
    width = h_ref.shape[1]

    @pl.when(step == 0)
    def _():
        copies = fetch_start(wq, w1, me_ref[0], sems, 0, width)
        pair_maps(feat_ref, maps, pairs, 0)
        if base:
            state[...] = refs[2][...]
        else:
            state[...] = jnp.zeros_like(state)
        for c in copies:
            c.wait()

    queries = mm(h_ref[...], w1[...]).astype(bf16)
    q_ref[...] = queries
    ones = block_ones(256, 64)
    size = h_ref.shape[0]
    cnt = cnt_ref[...]
    first, last = cend_ref[base + step], cend_ref[base + step + 1]
    row_id = lax.broadcasted_iota(jnp.int32, (size, size), 0)
    mask = (row_id >= lanes((size, size))) & (cnt == row_ref[...])
    before = jnp.where(cnt == first, 1.0, 0.0)
    after = jnp.where(cnt == last, 1.0, 0.0).astype(bf16)
    keep = jnp.where(first == last, 1.0, 0.0)
    low = lanes((size, 128)) < 64
    for p in range(pairs):
        two = slice(p * 128, (p + 1) * 128)
        phi = features(mm(queries[:, two], maps[p]), ones)
        phiq_ref[:, pl.ds(p * 256, 256)] = phi
        res = []
        for j, val in enumerate(augmented(v_ref[:, two])):
            h = 2 * p + j
            pq = phi[:, j * 128 : (j + 1) * 128]
            pk = phik_ref[:, pl.ds(h * 128, 128)]
            scores = jnp.where(mask, mm_t(pq, pk), 0.0).astype(bf16)
            st = state[h]
            st_b = st.astype(bf16)
            srel_ref[0, h] = st_b
            res.append(mm(scores, val) + before * mm(pq, st_b))
            state[h] = keep * st + mm_f(pk, val * after)
        num_ref[:, two] = jnp.where(low, res[0], res[1])
        den_ref[:, two] = pltpu.roll(jnp.where(low, res[1], res[0]), 64, 1)


def middle_body(
    n_seq, pairs, me_ref, keep_ref, x_ref, dy_ref, num_ref, den_ref, phiq_ref, cnt_ref, gb_ref, *refs
):
    width = x_ref.shape[1]
    wf, wp, sts = (refs[2 * i : 2 * i + 2] for i in range(3))
    (
        y_ref, o_ref, h_ref, a_ref, df_ref, dat_ref, dr_ref, dd_ref, sin_ref, gst_ref, sum_ref,
        w_out, w_fc, w_proj, rden, state, stv, sems,
    ) = refs[6:]
    step = pl.program_id(0)
    chunk = 768
    hidden = w_fc.shape[1]
    size = x_ref.shape[0]

    @pl.when(step == 0)
    def _():
        me = me_ref[0]
        st_copies = []
        for c in range(2):
            st_copies.append(pltpu.make_async_copy(sts[c], stv.at[c], sems.at[3, c]))
            st_copies[c].start()
        copies = fetch_start(wf, w_out, me, sems.at[0], hidden, width)
        copies += fetch_start(wf, w_fc, me, sems.at[1], 0, hidden)
        copies += fetch_start(wp, w_proj, me, sems.at[2])
        for c in st_copies:
            c.wait()

        def put(h, value):
            sin_ref[h] = value.astype(bf16)

        unpack_states(me, keep_ref, stv, put, 0, pairs, pairs, False)
        state[...] = jnp.zeros_like(state)
        sum_ref[...] = jnp.zeros_like(sum_ref)
        for c in copies:
            c.wait()

    gb = gb_ref[...]
    low = lanes((size, 128)) < 64
    start = jnp.where(cnt_ref[...] == 0.0, 1.0, 0.0)
    start_b = start.astype(bf16)
    for p in range(pairs):
        two = pl.ds(p * 128, 128)
        ra = mm(phiq_ref[:, pl.ds(p * 256, 128)], sin_ref[2 * p])
        rb = mm(phiq_ref[:, pl.ds(p * 256 + 128, 128)], sin_ref[2 * p + 1])
        num = num_ref[:, two] + start * jnp.where(low, ra, rb)
        den = den_ref[:, two] + start * pltpu.roll(jnp.where(low, rb, ra), 64, 1)
        inv = 1.0 / den
        rden[:, two] = inv
        o_ref[:, two] = (num * inv).astype(bf16)
    x = x_ref[...].astype(f32)
    attn = mm(o_ref[...], w_out[...])
    mid = x + attn
    out, hat, rstd = normed(mid, gb[1:2], gb[3:4])
    h2 = out.astype(bf16)
    h_ref[...] = h2
    dy_b = dy_ref[...]
    branch = jnp.zeros((size, width), f32)
    dh2 = jnp.zeros((size, width), f32)
    for c in range(w_fc.shape[1] // chunk):
        cols = pl.ds(c * chunk, chunk)
        fc = mm(h2, w_fc[:, cols])
        square = fc * fc
        tan = jnp.tanh(fc * (GC + GC * GA * square))
        half = 0.5 + 0.5 * tan
        act = (fc * half).astype(bf16)
        a_ref[:, cols] = act
        branch = branch + mm(act, w_proj[cols, :])
        slope = half + fc * (1.0 - half) * half * (2.0 * GC + 6.0 * GC * GA * square)
        dfc = (mm_t(dy_b, w_proj[cols, :]) * slope).astype(bf16)
        df_ref[:, cols] = dfc
        dh2 = dh2 + mm_t(dfc, w_fc[:, cols])
    y = mid + branch
    y_ref[...] = y.astype(bf16)
    sum_ref[0:1] += jnp.sum(attn * attn, axis=0, keepdims=True)
    sum_ref[1:2] += jnp.sum(branch * branch, axis=0, keepdims=True)
    sum_ref[2:3] += jnp.sum(y * y, axis=0, keepdims=True)
    sum_ref[3:4] += jnp.sum(dh2 * hat, axis=0, keepdims=True)
    sum_ref[4:5] += jnp.sum(dh2, axis=0, keepdims=True)
    dr = dy_b.astype(f32) + normed_back(dh2, hat, rstd, gb[1:2])
    dr_ref[...] = dr
    dat = dr.astype(bf16)
    dat_ref[...] = dat
    d_o = mm_t(dat, w_out[...])
    ones = block_ones(256, 64)
    lane = lanes((size, 128))
    for q in range(pairs // 2):
        four = pl.ds(q * 256, 256)
        inv = rden[:, four]
        d_q = d_o[:, q * 256 : (q + 1) * 256]
        prod = d_q * o_ref[:, four].astype(f32)
        hi = prod.astype(bf16)
        lo = (prod - hi.astype(f32)).astype(bf16)
        dden = -(mm(hi, ones) + mm(lo, ones)) * inv
        dnum = (d_q * inv).astype(bf16)
        for i in range(2):
            p = 2 * q + i
            sub = slice(i * 128, (i + 1) * 128)
            dd = pltpu.roll(dden[:, sub], 64, 1)
            dhi = dd.astype(bf16)
            dlo = (dd - dhi.astype(f32)).astype(bf16)
            near = lane & 63
            aux = jnp.where(near == 0, dhi.astype(f32), jnp.where(near == 1, dlo.astype(f32), 0.0)).astype(bf16)
            dn = dnum[:, sub]
            for j, both in enumerate((jnp.where(low, dn, aux), jnp.where(low, aux, dn))):
                h = 2 * p + j
                dd_ref[:, pl.ds(h * 128, 128)] = both
                state[h] += mm_f(phiq_ref[:, pl.ds(h * 128, 128)], both * start_b)

    @pl.when(step == pl.num_programs(0) - 1)
    def _():
        pack_states(lambda h: state[h], gst_ref, pairs, True)


def back_body(
    base, pairs, all_pairs, me_ref, keep_ref, cend_ref, q_ref, k_ref, v_ref, phiq_ref, phik_ref, dd_ref, srel_ref, sin_ref,
    cnt_ref, row_ref, feat_ref, *refs
):
    sts = refs[:2]
    (dqkv_ref, gfeat_ref, mapq, mapk, state, gq, gk, stv, sems) = refs[2:]
    step = pl.program_id(0)
    nblk = pl.num_programs(0)
    here = nblk - 1 - step

    @pl.when(step == 0)
    def _():
        copies = []
        for c in range(2):
            copies.append(pltpu.make_async_copy(sts[c], stv.at[c], sems.at[c]))
            copies[c].start()
        pair_maps(feat_ref, mapq, pairs, 0)
        pair_maps(feat_ref, mapk, pairs, 1)
        gq[...] = jnp.zeros_like(gq)
        gk[...] = jnp.zeros_like(gk)
        for c in copies:
            c.wait()

        def put(h, value):
            state[h] = value

        unpack_states(me_ref[0], keep_ref, stv, put, base, pairs, all_pairs, True)

    size = q_ref.shape[0]
    width = q_ref.shape[1]
    cnt = cnt_ref[...]
    first, last = cend_ref[here], cend_ref[here + 1]
    row_id = lax.broadcasted_iota(jnp.int32, (size, size), 0)
    col_id = lanes((size, size))
    same = cnt == row_ref[...]
    mask = (row_id >= col_id) & same
    mask_t = (col_id >= row_id) & same
    before = jnp.where(cnt == first, 1.0, 0.0).astype(bf16)
    after = jnp.where(cnt == last, 1.0, 0.0).astype(bf16)
    keep = jnp.where(first == last, 1.0, 0.0)
    opened = jnp.where(first == 0.0, 1.0, 0.0)
    ones = block_ones(256, 64)
    low = lanes((size, 128)) < 64
    for p in range(pairs):
        two = pl.ds(p * 128, 128)
        dphi_q, dphi_k, dvs = [], [], []
        for j, val in enumerate(augmented(v_ref[:, two])):
            h = 2 * p + j
            own = pl.ds(h * 128, 128)
            pq, pk, dd = phiq_ref[:, own], phik_ref[:, own], dd_ref[:, own]
            scores_t = jnp.where(mask_t, mm_t(pk, pq), 0.0).astype(bf16)
            dsc = jnp.where(mask, mm_t(dd, val), 0.0).astype(bf16)
            dsc_t = jnp.where(mask_t, mm_t(val, dd), 0.0).astype(bf16)
            st = (srel_ref[0, h].astype(f32) + opened * sin_ref[h].astype(f32)).astype(bf16)
            dst = state[h]
            dst_b = dst.astype(bf16)
            ddw = dd * before
            dphi_q.append(mm(dsc, pk) + mm_t(ddw, st))
            dphi_k.append(mm(dsc_t, pq) + mm_t(val * after, dst_b))
            dvs.append(mm(scores_t, dd) + mm(pk * after, dst_b))
            state[h] = keep * dst + mm_f(pq, ddw)
        dqkv_ref[:, pl.ds(2 * width + p * 128, 128)] = jnp.where(low, dvs[0], dvs[1]).astype(bf16)
        for phi_ref, dphi, rows_ref, maps, acc, base in (
            (phiq_ref, dphi_q, q_ref, mapq, gq, 0),
            (phik_ref, dphi_k, k_ref, mapk, gk, width),
        ):
            phi = phi_ref[:, pl.ds(p * 256, 256)].astype(f32)
            dphi = jnp.concatenate(dphi, axis=1)
            total = mm((phi * dphi).astype(bf16), ones)
            dlog = (phi * (dphi - total)).astype(bf16)
            dqkv_ref[:, pl.ds(base + p * 128, 128)] = mm_t(dlog, maps[p]).astype(bf16)
            acc[p] += mm_f(rows_ref[:, two], dlog)

    @pl.when(step == nblk - 1)
    def _():
        lane = lanes((128, 128))
        row = lax.broadcasted_iota(jnp.int32, (128, 128), 0)
        for p in range(pairs):
            outs = []
            for acc in (gq, gk):
                one = jnp.where(row < 64, acc[p, :, :128], acc[p, :, 128:])
                outs.append(one - pltpu.roll(one, 64, 1))
            gfeat_ref[pl.ds(p * 128, 128), :] = jnp.where(lane < 64, outs[0], -outs[1]).astype(bf16)


def enter_body(groups, me_ref, x_ref, dr_ref, gb_ref, *refs):
    width = x_ref.shape[1]
    grads = refs[:groups]
    wl = refs[groups : groups + 2]
    (dx_ref, sum_ref, w1, sems) = refs[groups + 2 :]

    @pl.when(pl.program_id(0) == 0)
    def _():
        me = me_ref[0]
        copies = fetch_start(wl, w1, me, sems.at[0], 0, 3 * width)
        sum_ref[...] = jnp.zeros_like(sum_ref)
        for c in copies:
            c.wait()

    gb = gb_ref[...]
    _, hat, rstd = normed(x_ref[...].astype(f32), gb[0:1], gb[2:3])
    part = width // groups
    dh = jnp.zeros(x_ref.shape, f32)
    for g in range(groups):
        for i in range(3):
            dh = dh + mm_t(grads[g][:, pl.ds(i * part, part)], w1[:, pl.ds(i * width + g * part, part)])
    dx_ref[...] = dr_ref[...] + normed_back(dh, hat, rstd, gb[0:1])
    sum_ref[0:1] += jnp.sum(dh * hat, axis=0, keepdims=True)
    sum_ref[1:2] += jnp.sum(dh, axis=0, keepdims=True)


def whole(*_):
    return pl.BlockSpec(memory_space=pl.ANY)


def smem():
    return pl.BlockSpec(memory_space=pltpu.SMEM)


def rows_spec(size, cols, back=None):
    if back is None:
        return pl.BlockSpec((size, cols), lambda i: (i, 0))
    return pl.BlockSpec((size, cols), lambda i: (back - 1 - i, 0))


def full_spec(shape):
    zeros = (0,) * len(shape)
    return pl.BlockSpec(shape, lambda i: zeros)


def sds(shape, kind):
    return jax.ShapeDtypeStruct(shape, kind)


def cparams():
    return pltpu.CompilerParams(
        dimension_semantics=("arbitrary",), vmem_limit_bytes=58 * 1024 * 1024
    )


def cost(micros):
    return pl.CostEstimate(
        flops=int(micros * 5e8), transcendentals=0, bytes_accessed=int(micros * 1e6)
    )


def dma(*shape):
    return pltpu.SemaphoreType.DMA(shape)


def shards(n_seq, depth, inputs, resets, norm_gains, norm_biases, w_qkv, w_feat, w_out, w_fc, w_proj, cotangent):
    tokens, width = inputs.shape[1], inputs.shape[2]
    hidden = w_fc.shape[1]
    head_dim = w_feat.shape[1] // 2
    heads = width // head_dim
    pairs = heads // 2
    rows = w_qkv.shape[0]
    nblk = tokens // BT
    x, dy = inputs[0], cotangent[0]
    me = lax.axis_index("seq")
    me_arr = me.reshape(1).astype(jnp.int32)

    marks = resets[0].reshape(nblk, BT).astype(bf16)
    flag = jnp.where(jnp.max(resets) == 0, 1.0, 0.0).astype(bf16)
    upper = jnp.triu(jnp.ones((BT, BT), bf16))
    inner = jnp.dot(marks, upper, preferred_element_type=f32)
    ends = jnp.cumsum(inner[:, -1])
    cend = jnp.concatenate([jnp.zeros((1,), f32), ends])
    counts = inner + cend[:-1, None]
    cnt_col = counts.reshape(tokens, 1)
    cnt_row = counts.reshape(1, tokens)

    norms = jnp.concatenate(
        [norm_gains, norm_biases, jnp.broadcast_to(flag, (rows, 1)), jnp.zeros((rows, 123), bf16)],
        axis=1,
    )
    first = stream_rows(stream_send(jnp.concatenate([w_qkv, w_feat, norms], axis=1), depth), depth)
    first = Spread(first, n_seq, False).near()
    up = jnp.concatenate([w_fc, w_out], axis=1)
    first.far_halves()
    up = stream_send(after(up, *first.cuts), depth)
    first_blocks = first.cores()
    up = stream_rows([after(a, first_blocks[0]) for a in up], depth)
    up = Spread(up, n_seq, True).near(first_blocks[0])
    proj_pieces = stream_send(after(w_proj, first_blocks[1], up.block), depth)
    me_first = after(me_arr, up.block)

    packed = (pairs + 1, 128, 128)
    full = (heads, 128, 128)
    h_one, keys, vals, phi_k, state, gb, feat_all = pl.pallas_call(
        functools.partial(keys_body, n_seq, pairs),
        name="keys",
        cost_estimate=cost(22),
        grid=(tokens // TM,),
        in_specs=[smem(), smem(), rows_spec(TM, width), rows_spec(TM, 1)] + [whole()] * 2,
        out_specs=[rows_spec(TM, width)] * 3
        + [rows_spec(TM, 2 * width), full_spec(packed), full_spec((8, width)), full_spec((width, 128))],
        out_shape=[sds((tokens, width), bf16)] * 3
        + [sds((tokens, 2 * width), bf16), sds(packed, bf16), sds((8, width), f32), sds((width, 128), bf16)],
        scratch_shapes=[
            pltpu.VMEM((width, 2 * width + 256), bf16),
            pltpu.VMEM((pairs, 128, 256), bf16),
            pltpu.VMEM(full, f32),
            dma(2, n_seq),
        ],
        compiler_params=cparams(),
    )(me_first, cend, x, cnt_col, *first_blocks)
    level = lax.axis_index("stream")
    flags = gb[4].reshape(n_seq, depth, rows)[:, :, 0]
    keeps = lax.dynamic_index_in_dim(flags, level, 1, False)
    spread = Spread(state, n_seq, False)
    spread.near()
    up.far(gb)
    proj = Spread(stream_rows([after(a, gb) for a in proj_pieces], depth), n_seq, False).near()
    part_blk = nblk // 2
    local = []
    for part in range(2):
        base = part * part_blk

        def here(size, cols):
            return pl.BlockSpec((size, cols), lambda i: (base + i, 0))

        blocks_out = [
            sds((tokens, width), bf16), sds((tokens, 2 * width), bf16), sds((tokens, width), f32),
            sds((tokens, width), f32), sds((nblk,) + full, bf16),
        ]
        if part:
            me_two = after(me_arr, up_blocks[0], *[proj.found[b] for b in proj.bits], *spread.found.values())
        else:
            me_two = after(me_arr, proj.block, state, after(up.found[up.bits[0]], gb))
        local = pl.pallas_call(
            functools.partial(local_body, base, pairs),
            name="local",
            cost_estimate=cost(19),
            grid=(part_blk,),
            in_specs=[
                smem(), smem(), here(BT, width), here(BT, 2 * width), here(BT, width), here(BT, 1),
                pl.BlockSpec((1, BT), lambda i: (0, base + i)), full_spec((width, 128)),
            ]
            + [whole()] * 2
            + ([full_spec(full)] + [whole()] * 5 if part else []),
            out_specs=[
                here(BT, width), here(BT, 2 * width), here(BT, width), here(BT, width),
                pl.BlockSpec((1,) + full, lambda i: (base + i, 0, 0, 0)), full_spec(full),
            ],
            out_shape=blocks_out + [sds(full, f32)],
            scratch_shapes=[
                pltpu.VMEM((width, width), bf16),
                pltpu.VMEM((pairs, 128, 256), bf16),
                dma(n_seq),
            ],
            input_output_aliases={11 + i: i for i in range(5)} if part else {},
            compiler_params=cparams(),
        )(
            me_two, cend, h_one, phi_k, vals, cnt_col, cnt_row, feat_all, *first_blocks,
            *([local[5]] + list(local[:5]) if part else []),
        )
        if part == 0:
            event = local[5]
            proj.far(event)
            spread.far(event)
            up_blocks = up.cores(event)
    queries, phi_q, num, den, srel, event = local
    proj_blocks = proj.cores(event)
    states = spread.cores(event)

    y, att, h_two, act, d_fc, d_att, d_mid, dd, s_in, g_state, sums = pl.pallas_call(
        functools.partial(middle_body, n_seq, pairs),
        name="middle",
        cost_estimate=cost(43),
        grid=(tokens // TM,),
        in_specs=[
            smem(), smem(), rows_spec(TM, width), rows_spec(TM, width), rows_spec(TM, width),
            rows_spec(TM, width), rows_spec(TM, 2 * width), rows_spec(TM, 1), full_spec((8, width)),
        ]
        + [whole()] * 6,
        out_specs=[
            rows_spec(TM, width), rows_spec(TM, width), rows_spec(TM, width), rows_spec(TM, hidden),
            rows_spec(TM, hidden), rows_spec(TM, width), rows_spec(TM, width), rows_spec(TM, 2 * width),
            full_spec(full), full_spec(packed), full_spec((8, width)),
        ],
        out_shape=[
            sds((tokens, width), bf16), sds((tokens, width), bf16), sds((tokens, width), bf16),
            sds((tokens, hidden), bf16), sds((tokens, hidden), bf16), sds((tokens, width), bf16),
            sds((tokens, width), f32), sds((tokens, 2 * width), bf16), sds(full, bf16), sds(packed, bf16),
            sds((8, width), f32),
        ],
        scratch_shapes=[
            pltpu.VMEM((width, width), bf16),
            pltpu.VMEM((width, hidden), bf16),
            pltpu.VMEM((hidden, width), bf16),
            pltpu.VMEM((TM, width), f32),
            pltpu.VMEM(full, f32),
            pltpu.VMEM((2, n_seq // 2) + packed, bf16),
            dma(4, n_seq),
        ],
        compiler_params=cparams(),
    )(
        me_arr, keeps, x, dy, num, den, phi_q, cnt_col, gb,
        *up_blocks, *proj_blocks, *states,
    )

    spread = Spread(g_state, n_seq, True).near()
    squares = jnp.sum(sums[:3], axis=1)
    norm_two = jnp.stack([sums[3], sums[4]], axis=1).astype(bf16)
    norm_two = jnp.concatenate([norm_two, jnp.zeros((width, 126), bf16)], axis=1)

    g_proj = mm_f(act, dy).astype(bf16)
    spread.far(g_proj)
    red_proj = Reduce([g_proj], n_seq, depth).send()
    h_late = after(h_two, red_proj.out, *[spread.found[b] for b in spread.bits])
    g_fc = mm_f(h_late, d_fc).astype(bf16)
    g_states = spread.cores()
    red_fc = Reduce([g_fc], n_seq, depth).send()
    g_out = mm_f(after(att, red_fc.out, g_states[0]), d_att).astype(bf16)
    red_proj.add(red_fc.out).send()
    me_back = after(me_arr, red_proj.out, g_out)

    groups = 2
    some = pairs // groups
    part = some * 128
    d_qkv, g_feat = [], []
    for g in range(groups):

        def spec(cols):
            return pl.BlockSpec((BT, cols), lambda i: (nblk - 1 - i, g))

        def one_group(shape):
            return pl.BlockSpec(shape, lambda i: (g,) + (0,) * (len(shape) - 1))

        one = (2 * some, 128, 128)
        d_one, g_one = pl.pallas_call(
            functools.partial(back_body, g * some, some, pairs),
            name="back",
            cost_estimate=cost(22),
            grid=(nblk,),
            in_specs=[
                smem(), smem(), smem(), spec(part), spec(part), spec(part), spec(2 * part), spec(2 * part),
                spec(2 * part), pl.BlockSpec((1,) + one, lambda i: (nblk - 1 - i, g, 0, 0)), one_group(one),
                rows_spec(BT, 1, nblk), pl.BlockSpec((1, BT), lambda i: (0, nblk - 1 - i)),
                one_group((part, 128)),
            ]
            + [whole()] * 2,
            out_specs=[rows_spec(BT, 3 * part, nblk), full_spec((part, 128))],
            out_shape=[sds((tokens, 3 * part), bf16), sds((part, 128), bf16)],
            scratch_shapes=[
                pltpu.VMEM((some, 128, 256), bf16),
                pltpu.VMEM((some, 128, 256), bf16),
                pltpu.VMEM(one, f32),
                pltpu.VMEM((some, 128, 256), f32),
                pltpu.VMEM((some, 128, 256), f32),
                pltpu.VMEM((2, n_seq // 2) + packed, bf16),
                dma(n_seq),
            ],
            compiler_params=cparams(),
        )(
            me_back, keeps, cend, queries, keys, vals, phi_q, phi_k, dd, srel, s_in, cnt_col, cnt_row,
            feat_all, *g_states,
        )
        d_qkv.append(d_one)
        g_feat.append(g_one)
        if g == 0:
            red_fc.add(d_one).send()
            g_one = mm_f(after(h_one, red_fc.out), d_one).astype(bf16)
            red_one = Reduce([g_one, g_out, norm_two], n_seq, depth).send()
            red_proj.add(red_one.out).send()
            me_back = after(me_arr, red_proj.out, red_one.out)
        squares = squares + xor_send(squares, n_seq, 1 << g)
        squares = after(squares, d_one)

    last = d_qkv[-1]
    g_two = mm_f(h_one, last).astype(bf16)
    red_two = Reduce([g_two, jnp.concatenate(g_feat, axis=0)], n_seq, depth).send()
    red_fc.add(red_two.out).send()
    red_one.add(red_fc.out).send()
    red_proj.add(red_one.out).send_stream()
    me_late = after(me_arr, red_proj.out, red_one.out, red_fc.out)
    dx, sums_one = pl.pallas_call(
        functools.partial(enter_body, groups),
        name="enter",
        cost_estimate=cost(11),
        grid=(tokens // TM,),
        in_specs=[smem(), rows_spec(TM, width), rows_spec(TM, width), full_spec((8, width))]
        + [rows_spec(TM, 3 * part)] * groups
        + [whole()] * 2,
        out_specs=[rows_spec(TM, width), full_spec((8, width))],
        out_shape=[sds((tokens, width), f32), sds((8, width), f32)],
        scratch_shapes=[pltpu.VMEM((width, 3 * width), bf16), dma(2, n_seq)],
        compiler_params=cparams(),
    )(me_late, x, d_mid, gb, *d_qkv, *first_blocks)
    for bit in range(groups, n_seq.bit_length() - 1):
        squares = squares + xor_send(squares, n_seq, 1 << bit)
    branch_rms = jnp.sqrt(squares / (tokens * n_seq * width)).reshape(1, 3)
    norm_one = jnp.stack([sums_one[0], sums_one[1]], axis=1).astype(bf16)
    norm_one = jnp.concatenate([norm_one, jnp.zeros((width, 126), bf16)], axis=1)
    red_norm = Reduce([norm_one], n_seq, depth).send()
    red_a, red_b = red_two.add(dx).cut((3 * part + 128) // 2)
    red_a.send()
    red_norm.add(red_a.out)
    red_b.cur = red_b.cur + red_norm.cur
    red_b.send()
    grad_proj = red_proj.done(red_a.out, red_b.out)
    red_fc.add(red_a.out, red_b.out).send_stream()
    red_one.add(red_fc.out).send()
    red_a.add(red_one.out).send()
    red_b.add(red_one.out).send()
    for red in (red_one, red_a, red_b):
        while red.order:
            red.add().send()
    grad_fc = red_fc.done(red_a.out, red_b.out)
    for red in (red_one, red_a, red_b):
        red.add()
    tail = Reduce(red_one.cur + red_a.cur + red_b.cur, n_seq, depth, [], []).send_stream().done()
    first_cols = 3 * part + width + 128
    grads = [tail[:, : 3 * part], tail[:, first_cols : first_cols + 3 * part]]
    grad_out = tail[:, 3 * part : first_cols]
    grad_feat = tail[:, first_cols + 3 * part : first_cols + 3 * part + 128]
    norm_one = tail[:, first_cols + 3 * part + 128 :]
    grad_qkv = jnp.concatenate(
        [grads[g][:, i * part : (i + 1) * part] for i in range(3) for g in range(groups)], axis=1
    )
    return (
        y[None],
        dx[None],
        jnp.concatenate([norm_one[:, 0:1], grad_out[:, width : width + 1]], axis=1),
        jnp.concatenate([norm_one[:, 1:2], grad_out[:, width + 1 : width + 2]], axis=1),
        grad_qkv,
        grad_feat,
        grad_out[:, :width],
        grad_fc,
        grad_proj,
        branch_rms,
    )


def solution(mesh):
    both = P(("seq", "stream"), None)
    acts = P("stream", "seq", None)
    placed = (acts, P("stream", "seq"), both, both, both, both, both, both, both, acts)
    return jax.shard_map(
        functools.partial(shards, mesh.shape["seq"], mesh.shape["stream"]),
        mesh=mesh,
        in_specs=placed,
        out_specs=(acts, acts, both, both, both, both, both, both, both, P("stream", None)),
        check_vma=False,
    )
```

```python
import functools

import jax
import jax.numpy as jnp
from jax import lax
from jax.experimental import pallas as pl
from jax.experimental.pallas import tpu as pltpu
from jax.sharding import PartitionSpec as P

BT = 256
GF = 6
TK = 512
TM = 256
epsilon = 1e-05
f32 = jnp.float32
bf16 = jnp.bfloat16
GC = 0.7978845608028654
GA = 0.044715


def mm(a, b):
    return jnp.dot(a, b, preferred_element_type=f32)


def mm_t(a, b):
    return lax.dot_general(a, b, (((1,), (1,)), ((), ())), preferred_element_type=f32)


def mm_f(a, b):
    return lax.dot_general(a, b, (((0,), (0,)), ((), ())), preferred_element_type=f32)


def xor_send(arr, size, mask):
    return lax.ppermute(arr, "seq", [(i, i ^ mask) for i in range(size)])


def after(arr, *deps):
    return lax.optimization_barrier((arr,) + deps)[0]


def stream_send(shard, depth):
    return [shard] + [
        lax.ppermute(shard, "stream", [(i, (i + d) % depth) for i in range(depth)])
        for d in range(1, depth)
    ]


def stream_rows(pieces, depth):
    shard = pieces[0]
    ring = pieces[::-1]
    place = lax.axis_index("stream")
    rows = shard.shape[0]
    both = jnp.concatenate(ring + ring, axis=0)
    return lax.dynamic_slice_in_dim(both, (depth - 1 - place) * rows, depth * rows, 0)


class Spread:
    def __init__(self, block, size, flip):
        self.size = size
        bits = [1 << b for b in range(1, size.bit_length() - 1)]
        self.bits = bits[::-1] if flip else bits
        self.block = block
        self.found = {0: block}

    def near(self, *deps):
        block = after(self.block, *deps) if deps else self.block
        for bit in self.bits:
            self.found[bit] = xor_send(block, self.size, bit)
        return self

    def far(self, *deps):
        for bit in self.bits:
            for r in list(self.found):
                if r ^ bit not in self.found and r < 2 * max(self.bits):
                    src = self.found[r]
                    self.found[r ^ bit] = xor_send(after(src, *deps) if deps else src, self.size, bit)
        return self

    def far_halves(self):
        one, two = self.bits[:2]
        half = self.block.shape[1] // 2
        self.cuts = [self.found[one][:, :half], self.found[two][:, half:]]
        left = xor_send(self.cuts[0], self.size, two)
        right = xor_send(self.cuts[1], self.size, one)
        self.found[one ^ two] = jnp.concatenate([left, right], axis=1)
        return self.far()

    def cores(self, *deps):
        parts = [self.found[2 * r] for r in range(self.size // 2)]
        stack = jnp.stack(parts)
        if deps:
            stack = after(stack, *deps)
        return [stack, xor_send(stack, self.size, 1)]


def beside(parts):
    return parts[0] if len(parts) == 1 else jnp.concatenate(parts, axis=-1)


class Reduce:
    def __init__(self, grads, size, depth, order=None, rest=None):
        self.size, self.depth = size, depth
        nbits = size.bit_length() - 1
        self.rest = list(range(nbits))[::-1] if rest is None else list(rest)
        self.order = list(range(nbits)) if order is None else list(order)
        self.cur = [
            g.reshape([2] * len(self.rest) + [g.shape[0] // 2 ** len(self.rest), g.shape[1]])
            if g.ndim == 2
            else g
            for g in grads
        ]

    def send(self):
        place = lax.axis_index("seq")
        bit = self.order.pop(0)
        axis = self.rest.index(bit)
        own = (place >> bit) & 1
        self.out = beside([lax.dynamic_index_in_dim(c, 1 - own, axis, False) for c in self.cur])
        self.kept = [lax.dynamic_index_in_dim(c, own, axis, False) for c in self.cur]
        self.flight = xor_send(self.out, self.size, 1 << bit)
        self.rest.pop(axis)
        return self

    def add(self, *deps):
        got = after(self.flight, *deps) if deps else self.flight
        self.cur = [(beside(self.kept).astype(f32) + got.astype(f32)).astype(bf16)]
        return self

    def cut(self, at):
        (cur,) = self.cur
        parts = [
            Reduce([cur[..., :at]], self.size, self.depth, self.order, self.rest),
            Reduce([cur[..., at:]], self.size, self.depth, self.order[::-1], self.rest),
        ]
        return parts

    def send_stream(self):
        while self.order:
            self.send().add()
        depth = self.depth
        level = lax.axis_index("stream")
        cur = beside(self.cur)
        self.out = cur
        cur = cur.reshape(depth, cur.shape[0] // depth, cur.shape[1])
        self.total = lax.dynamic_index_in_dim(cur, level, 0, False).astype(f32)
        self.flights = []
        for d in range(1, depth):
            piece = lax.dynamic_index_in_dim(cur, (level + d) % depth, 0, False)
            self.flights.append(
                lax.ppermute(piece, "stream", [(i, (i + d) % depth) for i in range(depth)])
            )
        return self

    def done(self, *deps):
        total = self.total
        for f in self.flights:
            total = total + (after(f, *deps) if deps else f).astype(f32)
        return total


def lanes(shape):
    return lax.broadcasted_iota(jnp.int32, shape, len(shape) - 1)


def block_ones(width, part):
    r = lax.broadcasted_iota(jnp.int32, (width, width), 0) // part
    c = lax.broadcasted_iota(jnp.int32, (width, width), 1) // part
    return jnp.where(r == c, 1.0, 0.0).astype(bf16)


def fetch_start(stacks, dest, me, sems, col=0, width=None, at=0):
    half = stacks[0].shape[0]
    rows = dest.shape[0] // (2 * half)
    width = width or stacks[0].shape[2]
    copies = []
    for c, ref in enumerate(stacks):
        for r in range(half):
            off = pl.multiple_of((me ^ (2 * r + c)) * rows, 8)
            copy = pltpu.make_async_copy(
                ref.at[r, :, pl.ds(col, width)],
                dest.at[pl.ds(off, rows), pl.ds(at, width)],
                sems.at[2 * r + c],
            )
            copy.start()
            copies.append(copy)
    return copies


def pair_maps(feat_ref, dest, pairs, which):
    width = 128
    lane = lanes((width, width))
    row = lax.broadcasted_iota(jnp.int32, (width, width), 0)
    for p in range(pairs):
        both = feat_ref[pl.ds(p * width, width), :].astype(f32)
        half = width // 2
        other = pltpu.roll(both, half, 1)
        if which == 0:
            signed = jnp.where(lane < half, both, -other)
        else:
            signed = jnp.where(lane < half, other, -both)
        dest[p, :, pl.ds(0, width)] = jnp.where(row < half, signed, 0.0).astype(bf16)
        dest[p, :, pl.ds(width, width)] = jnp.where(row >= half, signed, 0.0).astype(bf16)


def features(logits_of, ones):
    halves = [one[:, j * 128 : (j + 1) * 128] for one in logits_of for j in range(2)]
    low = lanes(halves[0].shape) < 64
    tops = [
        (
            jnp.max(jnp.where(low, one, -jnp.inf), axis=1, keepdims=True),
            jnp.max(jnp.where(low, -jnp.inf, one), axis=1, keepdims=True),
        )
        for one in halves
    ]
    exps = [jnp.exp(one - jnp.where(low, *top)) for one, top in zip(halves, tops)]
    exps = [jnp.concatenate(exps[2 * i : 2 * i + 2], axis=1) for i in range(len(logits_of))]
    sums = [mm(e.astype(bf16), ones) for e in exps]
    return [(e / t).astype(bf16) for e, t in zip(exps, sums)]


def augmented(two):
    low = lanes(two.shape) < 64
    one = jnp.ones_like(two)
    return jnp.where(low, two, one), jnp.where(low, one, two)


def pack_states(get, dest, pairs, zsum):
    shape = (128, 128)
    lane = lanes(shape)
    low = lane < 64
    zt = jnp.zeros(shape, f32)
    for p in range(pairs):
        a, b = get(2 * p), get(2 * p + 1)
        dest[p] = jnp.where(low, a, b).astype(bf16)
        if zsum:
            za = jnp.sum(jnp.where(low, 0.0, a), axis=1, keepdims=True)
            zb = jnp.sum(jnp.where(low, b, 0.0), axis=1, keepdims=True)
        else:
            za, zb = a, b
        zt = jnp.where(lane == 64 + 2 * p, za, zt)
        zt = jnp.where(lane == 2 * p + 1, zb, zt)
    dest[pairs] = zt.astype(bf16)


def unpack_states(me, keep_ref, blocks, put, base, count, pairs, back):
    shape = (128, 128)
    lane = lanes(shape)
    low = lane < 64
    size = 2 * blocks.shape[1]
    coefs = [None]
    for r in range(1, size):
        j = me ^ r
        c = jnp.where(j > me if back else j < me, 1.0, 0.0)
        for i in range(size):
            between = ((i > me) & (i < j)) if back else ((i > j) & (i < me))
            c = c * jnp.where(between, keep_ref[i], 1.0)
        coefs.append(c)

    def total(i):
        acc = jnp.zeros(shape, f32)
        for r in range(1, size):
            acc = acc + coefs[r] * blocks[r % 2, r // 2, i].astype(f32)
        return acc

    zt = total(pairs)
    for q in range(count):
        p = base + q
        two = total(p)
        za = jnp.sum(jnp.where(lane == 64 + 2 * p, zt, 0.0), axis=1, keepdims=True)
        zb = jnp.sum(jnp.where(lane == 2 * p + 1, zt, 0.0), axis=1, keepdims=True)
        if back:
            put(2 * q, jnp.where(low, two, jnp.where(lane == 64, za, 0.0)))
            put(2 * q + 1, jnp.where(low, jnp.where(lane == 0, zb, 0.0), two))
        else:
            put(2 * q, jnp.where(low, two, za))
            put(2 * q + 1, jnp.where(low, zb, two))


def normed(values, gain, bias):
    mean = jnp.mean(values, axis=1, keepdims=True)
    cent = values - mean
    rstd = lax.rsqrt(jnp.mean(cent * cent, axis=1, keepdims=True) + epsilon)
    hat = cent * rstd
    return hat * gain + bias, hat, rstd


def normed_back(grad, hat, rstd, gain):
    dhat = grad * gain
    return rstd * (
        dhat
        - jnp.mean(dhat, axis=1, keepdims=True)
        - hat * jnp.mean(dhat * hat, axis=1, keepdims=True)
    )


def keys_body(n_seq, pairs, me_ref, cend_ref, x_ref, cnt_ref, *refs):
    width = x_ref.shape[1]
    wl = refs[:2]
    (h_ref, k_ref, v_ref, phi_ref, st_ref, gb_ref, feat_ref, w1, maps, state, sems) = refs[2:]
    step = pl.program_id(0)

    @pl.when(step == 0)
    def _():
        me = me_ref[0]
        copies = fetch_start(wl, w1, me, sems.at[0], width, 2 * width + 256)
        for c in copies:
            c.wait()
        gb_ref[...] = w1[:, pl.ds(2 * width + 128, 128)].astype(f32).T[:8]
        feat_ref[...] = w1[:, pl.ds(2 * width, 128)]
        pair_maps(feat_ref, maps, pairs, 1)
        state[...] = jnp.zeros_like(state)

    gb = gb_ref[...]
    out, _, _ = normed(x_ref[...].astype(f32), gb[0:1], gb[2:3])
    h1 = out.astype(bf16)
    h_ref[...] = h1
    keys = mm(h1, w1[:, pl.ds(0, width)]).astype(bf16)
    vals = mm(h1, w1[:, pl.ds(width, width)]).astype(bf16)
    k_ref[...] = keys
    v_ref[...] = vals
    ones = block_ones(256, 64)
    last = cend_ref[cend_ref.shape[0] - 1]
    used = jnp.where(cnt_ref[...] == last, 1.0, 0.0).astype(bf16)
    for g in range(0, pairs, GF):
        group = range(g, min(g + GF, pairs))
        phis = features([mm(keys[:, p * 128 : (p + 1) * 128], maps[p]) for p in group], ones)
        for p, phi in zip(group, phis):
            phi_ref[:, pl.ds(p * 256, 256)] = phi
            va, vb = augmented(vals[:, p * 128 : (p + 1) * 128])
            state[2 * p] += mm_f(phi[:, :128], va * used)
            state[2 * p + 1] += mm_f(phi[:, 128:], vb * used)

    @pl.when(step == pl.num_programs(0) - 1)
    def _():
        pack_states(lambda h: state[h], st_ref, pairs, False)


def local_body(base, pairs, me_ref, cend_ref, h_ref, phik_ref, v_ref, cnt_ref, row_ref, feat_ref, *refs):
    wq = refs[:2]
    (q_ref, phiq_ref, num_ref, den_ref, srel_ref, state, w1, maps, sems) = refs[-9:]
    step = pl.program_id(0)
    width = h_ref.shape[1]

    @pl.when(step == 0)
    def _():
        copies = fetch_start(wq, w1, me_ref[0], sems, 0, width)
        pair_maps(feat_ref, maps, pairs, 0)
        if base:
            state[...] = refs[2][...]
        else:
            state[...] = jnp.zeros_like(state)
        for c in copies:
            c.wait()

    queries = mm(h_ref[...], w1[...]).astype(bf16)
    q_ref[...] = queries
    ones = block_ones(256, 64)
    size = h_ref.shape[0]
    cnt = cnt_ref[...]
    first, last = cend_ref[base + step], cend_ref[base + step + 1]
    row_id = lax.broadcasted_iota(jnp.int32, (size, size), 0)
    mask = (row_id >= lanes((size, size))) & (cnt == row_ref[...])
    before = jnp.where(cnt == first, 1.0, 0.0)
    after = jnp.where(cnt == last, 1.0, 0.0).astype(bf16)
    keep = jnp.where(first == last, 1.0, 0.0)
    low = lanes((size, 128)) < 64
    for g in range(0, pairs, GF):
        group = range(g, min(g + GF, pairs))
        phis = features([mm(queries[:, p * 128 : (p + 1) * 128], maps[p]) for p in group], ones)
        for p, phi in zip(group, phis):
            phiq_ref[:, pl.ds(p * 256, 256)] = phi
        pqs = [phi[:, j * 128 : (j + 1) * 128] for phi in phis for j in range(2)]
        heads = [2 * p + j for p in group for j in range(2)]
        pks = [phik_ref[:, pl.ds(h * 128, 128)] for h in heads]
        scores = [jnp.where(mask, mm_t(pq, pk), 0.0).astype(bf16) for pq, pk in zip(pqs, pks)]
        val_of = [v for p in group for v in augmented(v_ref[:, p * 128 : (p + 1) * 128])]
        res = []
        for h, pq, pk, sc, val in zip(heads, pqs, pks, scores, val_of):
            st = state[h]
            st_b = st.astype(bf16)
            srel_ref[0, h] = st_b
            res.append(mm(sc, val) + before * mm(pq, st_b))
            state[h] = keep * st + mm_f(pk, val * after)
        for i, p in enumerate(group):
            two = pl.ds(p * 128, 128)
            num_ref[:, two] = jnp.where(low, res[2 * i], res[2 * i + 1])
            den_ref[:, two] = pltpu.roll(jnp.where(low, res[2 * i + 1], res[2 * i]), 64, 1)


def middle_body(
    n_seq, pairs, me_ref, keep_ref, x_ref, dy_ref, num_ref, den_ref, phiq_ref, cnt_ref, gb_ref, *refs
):
    width = x_ref.shape[1]
    wf, wp, sts = (refs[2 * i : 2 * i + 2] for i in range(3))
    (
        y_ref, o_ref, h_ref, a_ref, df_ref, dat_ref, dr_ref, dd_ref, sin_ref, gst_ref, sum_ref,
        w_out, w_fc, w_proj, rden, state, stv, sems,
    ) = refs[6:]
    step = pl.program_id(0)
    chunk = 768
    hidden = w_fc.shape[1]
    size = x_ref.shape[0]

    @pl.when(step == 0)
    def _():
        me = me_ref[0]
        st_copies = []
        for c in range(2):
            st_copies.append(pltpu.make_async_copy(sts[c], stv.at[c], sems.at[3, c]))
            st_copies[c].start()
        copies = fetch_start(wf, w_out, me, sems.at[0], hidden, width)
        copies += fetch_start(wf, w_fc, me, sems.at[1], 0, hidden)
        copies += fetch_start(wp, w_proj, me, sems.at[2])
        for c in st_copies:
            c.wait()

        def put(h, value):
            sin_ref[h] = value.astype(bf16)

        unpack_states(me, keep_ref, stv, put, 0, pairs, pairs, False)
        state[...] = jnp.zeros_like(state)
        sum_ref[...] = jnp.zeros_like(sum_ref)
        for c in copies:
            c.wait()

    gb = gb_ref[...]
    low = lanes((size, 128)) < 64
    start = jnp.where(cnt_ref[...] == 0.0, 1.0, 0.0)
    start_b = start.astype(bf16)
    res = [mm(phiq_ref[:, pl.ds(h * 128, 128)], sin_ref[h]) for h in range(2 * pairs)]
    for p in range(pairs):
        two = pl.ds(p * 128, 128)
        ra, rb = res[2 * p], res[2 * p + 1]
        num = num_ref[:, two] + start * jnp.where(low, ra, rb)
        den = den_ref[:, two] + start * pltpu.roll(jnp.where(low, rb, ra), 64, 1)
        inv = 1.0 / den
        rden[:, two] = inv
        o_ref[:, two] = (num * inv).astype(bf16)
    x = x_ref[...].astype(f32)
    attn = mm(o_ref[...], w_out[...])
    mid = x + attn
    out, hat, rstd = normed(mid, gb[1:2], gb[3:4])
    h2 = out.astype(bf16)
    h_ref[...] = h2
    dy_b = dy_ref[...]
    branch = jnp.zeros((size, width), f32)
    dh2 = jnp.zeros((size, width), f32)
    for c in range(w_fc.shape[1] // chunk):
        cols = pl.ds(c * chunk, chunk)
        fc = mm(h2, w_fc[:, cols])
        square = fc * fc
        tan = jnp.tanh(fc * (GC + GC * GA * square))
        half = 0.5 + 0.5 * tan
        act = (fc * half).astype(bf16)
        a_ref[:, cols] = act
        branch = branch + mm(act, w_proj[cols, :])
        slope = half + fc * (1.0 - half) * half * (2.0 * GC + 6.0 * GC * GA * square)
        dfc = (mm_t(dy_b, w_proj[cols, :]) * slope).astype(bf16)
        df_ref[:, cols] = dfc
        dh2 = dh2 + mm_t(dfc, w_fc[:, cols])
    y = mid + branch
    y_ref[...] = y.astype(bf16)
    sum_ref[0:1] += jnp.sum(attn * attn, axis=0, keepdims=True)
    sum_ref[1:2] += jnp.sum(branch * branch, axis=0, keepdims=True)
    sum_ref[2:3] += jnp.sum(y * y, axis=0, keepdims=True)
    sum_ref[3:4] += jnp.sum(dh2 * hat, axis=0, keepdims=True)
    sum_ref[4:5] += jnp.sum(dh2, axis=0, keepdims=True)
    dr = dy_b.astype(f32) + normed_back(dh2, hat, rstd, gb[1:2])
    dr_ref[...] = dr
    dat = dr.astype(bf16)
    dat_ref[...] = dat
    d_o = mm_t(dat, w_out[...])
    ones = block_ones(256, 64)
    lane = lanes((size, 128))
    quads = range(pairs // 2)
    fours = [pl.ds(q * 256, 256) for q in quads]
    d_os = [d_o[:, q * 256 : (q + 1) * 256] for q in quads]
    prods = [d * o_ref[:, c].astype(f32) for d, c in zip(d_os, fours)]
    his = [a.astype(bf16) for a in prods]
    los = [(a - hi.astype(f32)).astype(bf16) for a, hi in zip(prods, his)]
    ddens = [-(mm(hi, ones) + mm(lo, ones)) * rden[:, c] for hi, lo, c in zip(his, los, fours)]
    dnums = [(d * rden[:, c]).astype(bf16) for d, c in zip(d_os, fours)]
    near = lane & 63
    for p in range(pairs):
        sub = slice((p % 2) * 128, (p % 2 + 1) * 128)
        dd = pltpu.roll(ddens[p // 2][:, sub], 64, 1)
        dhi = dd.astype(bf16)
        dlo = (dd - dhi.astype(f32)).astype(bf16)
        aux = jnp.where(near == 0, dhi.astype(f32), jnp.where(near == 1, dlo.astype(f32), 0.0)).astype(bf16)
        dn = dnums[p // 2][:, sub]
        dd_ref[:, pl.ds(p * 256, 128)] = jnp.where(low, dn, aux)
        dd_ref[:, pl.ds(p * 256 + 128, 128)] = jnp.where(low, aux, dn)
    for h in range(2 * pairs):
        own = pl.ds(h * 128, 128)
        state[h] += mm_f(phiq_ref[:, own], dd_ref[:, own] * start_b)

    @pl.when(step == pl.num_programs(0) - 1)
    def _():
        pack_states(lambda h: state[h], gst_ref, pairs, True)


def back_body(
    base, pairs, all_pairs, me_ref, keep_ref, cend_ref, q_ref, k_ref, v_ref, phiq_ref, phik_ref, dd_ref, srel_ref, sin_ref,
    cnt_ref, row_ref, feat_ref, *refs
):
    sts = refs[:2]
    (dqkv_ref, gfeat_ref, mapq, mapk, state, gq, gk, stv, sems) = refs[2:]
    step = pl.program_id(0)
    nblk = pl.num_programs(0)
    here = nblk - 1 - step

    @pl.when(step == 0)
    def _():
        copies = []
        for c in range(2):
            copies.append(pltpu.make_async_copy(sts[c], stv.at[c], sems.at[c]))
            copies[c].start()
        pair_maps(feat_ref, mapq, pairs, 0)
        pair_maps(feat_ref, mapk, pairs, 1)
        gq[...] = jnp.zeros_like(gq)
        gk[...] = jnp.zeros_like(gk)
        for c in copies:
            c.wait()

        def put(h, value):
            state[h] = value

        unpack_states(me_ref[0], keep_ref, stv, put, base, pairs, all_pairs, True)

    size = q_ref.shape[0]
    width = q_ref.shape[1]
    cnt = cnt_ref[...]
    first, last = cend_ref[here], cend_ref[here + 1]
    row_id = lax.broadcasted_iota(jnp.int32, (size, size), 0)
    col_id = lanes((size, size))
    same = cnt == row_ref[...]
    mask = (row_id >= col_id) & same
    mask_t = (col_id >= row_id) & same
    before = jnp.where(cnt == first, 1.0, 0.0).astype(bf16)
    after = jnp.where(cnt == last, 1.0, 0.0).astype(bf16)
    keep = jnp.where(first == last, 1.0, 0.0)
    opened = jnp.where(first == 0.0, 1.0, 0.0)
    ones = block_ones(256, 64)
    low = lanes((size, 128)) < 64
    heads = range(2 * pairs)
    cols = [pl.ds(h * 128, 128) for h in heads]
    vals = [v for p in range(pairs) for v in augmented(v_ref[:, pl.ds(p * 128, 128)])]
    scores_t = [
        jnp.where(mask_t, mm_t(phik_ref[:, c], phiq_ref[:, c]), 0.0).astype(bf16) for c in cols
    ]
    dsc = [jnp.where(mask, mm_t(dd_ref[:, c], v), 0.0).astype(bf16) for c, v in zip(cols, vals)]
    dsc_t = [jnp.where(mask_t, mm_t(v, dd_ref[:, c]), 0.0).astype(bf16) for c, v in zip(cols, vals)]
    sts = [
        (srel_ref[0, h].astype(f32) + opened * sin_ref[h].astype(f32)).astype(bf16) for h in heads
    ]
    dsts = [state[h].astype(bf16) for h in heads]
    ddws = [dd_ref[:, c] * before for c in cols]
    dphi_q = [mm(dsc[h], phik_ref[:, cols[h]]) + mm_t(ddws[h], sts[h]) for h in heads]
    dphi_k = [mm(dsc_t[h], phiq_ref[:, cols[h]]) + mm_t(vals[h] * after, dsts[h]) for h in heads]
    dvs = [mm(scores_t[h], dd_ref[:, cols[h]]) + mm(phik_ref[:, cols[h]] * after, dsts[h]) for h in heads]
    for h in heads:
        state[h] = keep * state[h] + mm_f(phiq_ref[:, cols[h]], ddws[h])
    for p in range(pairs):
        dqkv_ref[:, pl.ds(2 * width + p * 128, 128)] = jnp.where(low, dvs[2 * p], dvs[2 * p + 1]).astype(bf16)
    for phi_ref, dphi, rows_ref, maps, acc, base_col in (
        (phiq_ref, dphi_q, q_ref, mapq, gq, 0),
        (phik_ref, dphi_k, k_ref, mapk, gk, width),
    ):
        phis = [phi_ref[:, pl.ds(p * 256, 256)].astype(f32) for p in range(pairs)]
        dphis = [jnp.concatenate(dphi[2 * p : 2 * p + 2], axis=1) for p in range(pairs)]
        totals = [mm((phi * d).astype(bf16), ones) for phi, d in zip(phis, dphis)]
        dlogs = [(phi * (d - t)).astype(bf16) for phi, d, t in zip(phis, dphis, totals)]
        for p in range(pairs):
            two = pl.ds(p * 128, 128)
            dqkv_ref[:, pl.ds(base_col + p * 128, 128)] = mm_t(dlogs[p], maps[p]).astype(bf16)
            acc[p] += mm_f(rows_ref[:, two], dlogs[p])

    @pl.when(step == nblk - 1)
    def _():
        lane = lanes((128, 128))
        row = lax.broadcasted_iota(jnp.int32, (128, 128), 0)
        for p in range(pairs):
            outs = []
            for acc in (gq, gk):
                one = jnp.where(row < 64, acc[p, :, :128], acc[p, :, 128:])
                outs.append(one - pltpu.roll(one, 64, 1))
            gfeat_ref[pl.ds(p * 128, 128), :] = jnp.where(lane < 64, outs[0], -outs[1]).astype(bf16)


def enter_body(groups, me_ref, x_ref, dr_ref, gb_ref, *refs):
    width = x_ref.shape[1]
    grads = refs[:groups]
    wl = refs[groups : groups + 2]
    (dx_ref, sum_ref, w1, sems) = refs[groups + 2 :]

    @pl.when(pl.program_id(0) == 0)
    def _():
        me = me_ref[0]
        copies = fetch_start(wl, w1, me, sems.at[0], 0, 3 * width)
        sum_ref[...] = jnp.zeros_like(sum_ref)
        for c in copies:
            c.wait()

    gb = gb_ref[...]
    _, hat, rstd = normed(x_ref[...].astype(f32), gb[0:1], gb[2:3])
    part = width // groups
    dh = jnp.zeros(x_ref.shape, f32)
    for g in range(groups):
        for i in range(3):
            dh = dh + mm_t(grads[g][:, pl.ds(i * part, part)], w1[:, pl.ds(i * width + g * part, part)])
    dx_ref[...] = dr_ref[...] + normed_back(dh, hat, rstd, gb[0:1])
    sum_ref[0:1] += jnp.sum(dh * hat, axis=0, keepdims=True)
    sum_ref[1:2] += jnp.sum(dh, axis=0, keepdims=True)


def whole(*_):
    return pl.BlockSpec(memory_space=pl.ANY)


def smem():
    return pl.BlockSpec(memory_space=pltpu.SMEM)


def rows_spec(size, cols, back=None):
    if back is None:
        return pl.BlockSpec((size, cols), lambda i: (i, 0))
    return pl.BlockSpec((size, cols), lambda i: (back - 1 - i, 0))


def full_spec(shape):
    zeros = (0,) * len(shape)
    return pl.BlockSpec(shape, lambda i: zeros)


def sds(shape, kind):
    return jax.ShapeDtypeStruct(shape, kind)


def cparams():
    return pltpu.CompilerParams(
        dimension_semantics=("arbitrary",), vmem_limit_bytes=58 * 1024 * 1024
    )


def cost(micros):
    return pl.CostEstimate(
        flops=int(micros * 5e8), transcendentals=0, bytes_accessed=int(micros * 1e6)
    )


def dma(*shape):
    return pltpu.SemaphoreType.DMA(shape)


def shards(n_seq, depth, inputs, resets, norm_gains, norm_biases, w_qkv, w_feat, w_out, w_fc, w_proj, cotangent):
    tokens, width = inputs.shape[1], inputs.shape[2]
    hidden = w_fc.shape[1]
    head_dim = w_feat.shape[1] // 2
    heads = width // head_dim
    pairs = heads // 2
    rows = w_qkv.shape[0]
    nblk = tokens // BT
    x, dy = inputs[0], cotangent[0]
    me = lax.axis_index("seq")
    me_arr = me.reshape(1).astype(jnp.int32)

    marks = resets[0].reshape(nblk, BT).astype(bf16)
    flag = jnp.where(jnp.max(resets) == 0, 1.0, 0.0).astype(bf16)
    upper = jnp.triu(jnp.ones((BT, BT), bf16))
    inner = jnp.dot(marks, upper, preferred_element_type=f32)
    ends = jnp.cumsum(inner[:, -1])
    cend = jnp.concatenate([jnp.zeros((1,), f32), ends])
    counts = inner + cend[:-1, None]
    cnt_col = counts.reshape(tokens, 1)
    cnt_row = counts.reshape(1, tokens)

    norms = jnp.concatenate(
        [norm_gains, norm_biases, jnp.broadcast_to(flag, (rows, 1)), jnp.zeros((rows, 123), bf16)],
        axis=1,
    )
    first = stream_rows(stream_send(jnp.concatenate([w_qkv, w_feat, norms], axis=1), depth), depth)
    first = Spread(first, n_seq, False).near()
    up = jnp.concatenate([w_fc, w_out], axis=1)
    first.far_halves()
    up = stream_send(after(up, *first.cuts), depth)
    first_blocks = first.cores()
    up = stream_rows([after(a, first_blocks[0]) for a in up], depth)
    up = Spread(up, n_seq, True).near(first_blocks[0])
    proj_pieces = stream_send(after(w_proj, first_blocks[1], up.block), depth)
    me_first = after(me_arr, up.block)

    packed = (pairs + 1, 128, 128)
    full = (heads, 128, 128)
    h_one, keys, vals, phi_k, state, gb, feat_all = pl.pallas_call(
        functools.partial(keys_body, n_seq, pairs),
        name="keys",
        cost_estimate=cost(22),
        grid=(tokens // TK,),
        in_specs=[smem(), smem(), rows_spec(TK, width), rows_spec(TK, 1)] + [whole()] * 2,
        out_specs=[rows_spec(TK, width)] * 3
        + [rows_spec(TK, 2 * width), full_spec(packed), full_spec((8, width)), full_spec((width, 128))],
        out_shape=[sds((tokens, width), bf16)] * 3
        + [sds((tokens, 2 * width), bf16), sds(packed, bf16), sds((8, width), f32), sds((width, 128), bf16)],
        scratch_shapes=[
            pltpu.VMEM((width, 2 * width + 256), bf16),
            pltpu.VMEM((pairs, 128, 256), bf16),
            pltpu.VMEM(full, f32),
            dma(2, n_seq),
        ],
        compiler_params=cparams(),
    )(me_first, cend, x, cnt_col, *first_blocks)
    level = lax.axis_index("stream")
    flags = gb[4].reshape(n_seq, depth, rows)[:, :, 0]
    keeps = lax.dynamic_index_in_dim(flags, level, 1, False)
    spread = Spread(state, n_seq, False)
    spread.near()
    up.far(gb)
    proj = Spread(stream_rows([after(a, gb) for a in proj_pieces], depth), n_seq, False).near()
    part_blk = nblk // 2
    local = []
    for part in range(2):
        base = part * part_blk

        def here(size, cols):
            return pl.BlockSpec((size, cols), lambda i: (base + i, 0))

        blocks_out = [
            sds((tokens, width), bf16), sds((tokens, 2 * width), bf16), sds((tokens, width), f32),
            sds((tokens, width), f32), sds((nblk,) + full, bf16),
        ]
        if part:
            me_two = after(me_arr, up_blocks[0], *[proj.found[b] for b in proj.bits], *spread.found.values())
        else:
            me_two = after(me_arr, proj.block, state, after(up.found[up.bits[0]], gb))
        local = pl.pallas_call(
            functools.partial(local_body, base, pairs),
            name="local",
            cost_estimate=cost(15),
            grid=(part_blk,),
            in_specs=[
                smem(), smem(), here(BT, width), here(BT, 2 * width), here(BT, width), here(BT, 1),
                pl.BlockSpec((1, BT), lambda i: (0, base + i)), full_spec((width, 128)),
            ]
            + [whole()] * 2
            + ([full_spec(full)] + [whole()] * 5 if part else []),
            out_specs=[
                here(BT, width), here(BT, 2 * width), here(BT, width), here(BT, width),
                pl.BlockSpec((1,) + full, lambda i: (base + i, 0, 0, 0)), full_spec(full),
            ],
            out_shape=blocks_out + [sds(full, f32)],
            scratch_shapes=[
                pltpu.VMEM((width, width), bf16),
                pltpu.VMEM((pairs, 128, 256), bf16),
                dma(n_seq),
            ],
            input_output_aliases={11 + i: i for i in range(5)} if part else {},
            compiler_params=cparams(),
        )(
            me_two, cend, h_one, phi_k, vals, cnt_col, cnt_row, feat_all, *first_blocks,
            *([local[5]] + list(local[:5]) if part else []),
        )
        if part == 0:
            event = local[5]
            proj.far(event)
            spread.far(event)
            up_blocks = up.cores(event)
    queries, phi_q, num, den, srel, event = local
    proj_blocks = proj.cores(event)
    states = spread.cores(event)

    y, att, h_two, act, d_fc, d_att, d_mid, dd, s_in, g_state, sums = pl.pallas_call(
        functools.partial(middle_body, n_seq, pairs),
        name="middle",
        cost_estimate=cost(43),
        grid=(tokens // TM,),
        in_specs=[
            smem(), smem(), rows_spec(TM, width), rows_spec(TM, width), rows_spec(TM, width),
            rows_spec(TM, width), rows_spec(TM, 2 * width), rows_spec(TM, 1), full_spec((8, width)),
        ]
        + [whole()] * 6,
        out_specs=[
            rows_spec(TM, width), rows_spec(TM, width), rows_spec(TM, width), rows_spec(TM, hidden),
            rows_spec(TM, hidden), rows_spec(TM, width), rows_spec(TM, width), rows_spec(TM, 2 * width),
            full_spec(full), full_spec(packed), full_spec((8, width)),
        ],
        out_shape=[
            sds((tokens, width), bf16), sds((tokens, width), bf16), sds((tokens, width), bf16),
            sds((tokens, hidden), bf16), sds((tokens, hidden), bf16), sds((tokens, width), bf16),
            sds((tokens, width), f32), sds((tokens, 2 * width), bf16), sds(full, bf16), sds(packed, bf16),
            sds((8, width), f32),
        ],
        scratch_shapes=[
            pltpu.VMEM((width, width), bf16),
            pltpu.VMEM((width, hidden), bf16),
            pltpu.VMEM((hidden, width), bf16),
            pltpu.VMEM((TM, width), f32),
            pltpu.VMEM(full, f32),
            pltpu.VMEM((2, n_seq // 2) + packed, bf16),
            dma(4, n_seq),
        ],
        compiler_params=cparams(),
    )(
        me_arr, keeps, x, dy, num, den, phi_q, cnt_col, gb,
        *up_blocks, *proj_blocks, *states,
    )

    spread = Spread(g_state, n_seq, True).near()
    squares = jnp.sum(sums[:3], axis=1)
    norm_two = jnp.stack([sums[3], sums[4]], axis=1).astype(bf16)
    norm_two = jnp.concatenate([norm_two, jnp.zeros((width, 126), bf16)], axis=1)

    g_proj = mm_f(act, dy).astype(bf16)
    spread.far(g_proj)
    red_proj = Reduce([g_proj], n_seq, depth).send()
    h_late = after(h_two, red_proj.out, *[spread.found[b] for b in spread.bits])
    g_fc = mm_f(h_late, d_fc).astype(bf16)
    g_states = spread.cores()
    red_fc = Reduce([g_fc], n_seq, depth).send()
    g_out = mm_f(after(att, red_fc.out, g_states[0]), d_att).astype(bf16)
    red_proj.add(red_fc.out).send()
    me_back = after(me_arr, red_proj.out, g_out)

    groups = 2
    some = pairs // groups
    part = some * 128
    d_qkv, g_feat = [], []
    for g in range(groups):

        def spec(cols):
            return pl.BlockSpec((BT, cols), lambda i: (nblk - 1 - i, g))

        def one_group(shape):
            return pl.BlockSpec(shape, lambda i: (g,) + (0,) * (len(shape) - 1))

        one = (2 * some, 128, 128)
        d_one, g_one = pl.pallas_call(
            functools.partial(back_body, g * some, some, pairs),
            name="back",
            cost_estimate=cost(19),
            grid=(nblk,),
            in_specs=[
                smem(), smem(), smem(), spec(part), spec(part), spec(part), spec(2 * part), spec(2 * part),
                spec(2 * part), pl.BlockSpec((1,) + one, lambda i: (nblk - 1 - i, g, 0, 0)), one_group(one),
                rows_spec(BT, 1, nblk), pl.BlockSpec((1, BT), lambda i: (0, nblk - 1 - i)),
                one_group((part, 128)),
            ]
            + [whole()] * 2,
            out_specs=[rows_spec(BT, 3 * part, nblk), full_spec((part, 128))],
            out_shape=[sds((tokens, 3 * part), bf16), sds((part, 128), bf16)],
            scratch_shapes=[
                pltpu.VMEM((some, 128, 256), bf16),
                pltpu.VMEM((some, 128, 256), bf16),
                pltpu.VMEM(one, f32),
                pltpu.VMEM((some, 128, 256), f32),
                pltpu.VMEM((some, 128, 256), f32),
                pltpu.VMEM((2, n_seq // 2) + packed, bf16),
                dma(n_seq),
            ],
            compiler_params=cparams(),
        )(
            me_back, keeps, cend, queries, keys, vals, phi_q, phi_k, dd, srel, s_in, cnt_col, cnt_row,
            feat_all, *g_states,
        )
        d_qkv.append(d_one)
        g_feat.append(g_one)
        if g == 0:
            red_fc.add(d_one).send()
            g_one = mm_f(after(h_one, red_fc.out), d_one).astype(bf16)
            red_one = Reduce([g_one, g_out, norm_two], n_seq, depth).send()
            red_proj.add(red_one.out).send()
            me_back = after(me_arr, red_proj.out, red_one.out)
        squares = squares + xor_send(squares, n_seq, 1 << g)
        squares = after(squares, d_one)

    last = d_qkv[-1]
    g_two = mm_f(h_one, last).astype(bf16)
    red_two = Reduce([g_two, jnp.concatenate(g_feat, axis=0)], n_seq, depth).send()
    red_fc.add(red_two.out).send()
    red_one.add(red_fc.out).send()
    red_proj.add(red_one.out).send_stream()
    me_late = after(me_arr, red_proj.out, red_one.out, red_fc.out)
    dx, sums_one = pl.pallas_call(
        functools.partial(enter_body, groups),
        name="enter",
        cost_estimate=cost(11),
        grid=(tokens // TK,),
        in_specs=[smem(), rows_spec(TK, width), rows_spec(TK, width), full_spec((8, width))]
        + [rows_spec(TK, 3 * part)] * groups
        + [whole()] * 2,
        out_specs=[rows_spec(TK, width), full_spec((8, width))],
        out_shape=[sds((tokens, width), f32), sds((8, width), f32)],
        scratch_shapes=[pltpu.VMEM((width, 3 * width), bf16), dma(2, n_seq)],
        compiler_params=cparams(),
    )(me_late, x, d_mid, gb, *d_qkv, *first_blocks)
    for bit in range(groups, n_seq.bit_length() - 1):
        squares = squares + xor_send(squares, n_seq, 1 << bit)
    branch_rms = jnp.sqrt(squares / (tokens * n_seq * width)).reshape(1, 3)
    norm_one = jnp.stack([sums_one[0], sums_one[1]], axis=1).astype(bf16)
    norm_one = jnp.concatenate([norm_one, jnp.zeros((width, 126), bf16)], axis=1)
    red_norm = Reduce([norm_one], n_seq, depth).send()
    red_a, red_b = red_two.add(dx).cut((3 * part + 128) // 2)
    red_a.send()
    red_norm.add(red_a.out)
    red_b.cur = red_b.cur + red_norm.cur
    red_b.send()
    grad_proj = red_proj.done(red_a.out, red_b.out)
    red_fc.add(red_a.out, red_b.out).send_stream()
    red_one.add(red_fc.out).send()
    red_a.add(red_one.out).send()
    red_b.add(red_one.out).send()
    for red in (red_one, red_a, red_b):
        while red.order:
            red.add().send()
    grad_fc = red_fc.done(red_a.out, red_b.out)
    for red in (red_one, red_a, red_b):
        red.add()
    tail = Reduce(red_one.cur + red_a.cur + red_b.cur, n_seq, depth, [], []).send_stream().done()
    first_cols = 3 * part + width + 128
    grads = [tail[:, : 3 * part], tail[:, first_cols : first_cols + 3 * part]]
    grad_out = tail[:, 3 * part : first_cols]
    grad_feat = tail[:, first_cols + 3 * part : first_cols + 3 * part + 128]
    norm_one = tail[:, first_cols + 3 * part + 128 :]
    grad_qkv = jnp.concatenate(
        [grads[g][:, i * part : (i + 1) * part] for i in range(3) for g in range(groups)], axis=1
    )
    return (
        y[None],
        dx[None],
        jnp.concatenate([norm_one[:, 0:1], grad_out[:, width : width + 1]], axis=1),
        jnp.concatenate([norm_one[:, 1:2], grad_out[:, width + 1 : width + 2]], axis=1),
        grad_qkv,
        grad_feat,
        grad_out[:, :width],
        grad_fc,
        grad_proj,
        branch_rms,
    )


def solution(mesh):
    both = P(("seq", "stream"), None)
    acts = P("stream", "seq", None)
    placed = (acts, P("stream", "seq"), both, both, both, both, both, both, both, acts)
    return jax.shard_map(
        functools.partial(shards, mesh.shape["seq"], mesh.shape["stream"]),
        mesh=mesh,
        in_specs=placed,
        out_specs=(acts, acts, both, both, both, both, both, both, both, P("stream", None)),
        check_vma=False,
    )
```

```python
import functools

import jax
import jax.numpy as jnp
from jax import lax
from jax.experimental import pallas as pl
from jax.experimental.pallas import tpu as pltpu
from jax.sharding import PartitionSpec as P

BT = 256
GF = 6
TK = 512
TM = 256
epsilon = 1e-05
f32 = jnp.float32
bf16 = jnp.bfloat16
GC = 0.7978845608028654
GA = 0.044715


def mm(a, b):
    return jnp.dot(a, b, preferred_element_type=f32)


def mm_t(a, b):
    return lax.dot_general(a, b, (((1,), (1,)), ((), ())), preferred_element_type=f32)


def mm_f(a, b):
    return lax.dot_general(a, b, (((0,), (0,)), ((), ())), preferred_element_type=f32)


def xor_send(arr, size, mask):
    return lax.ppermute(arr, "seq", [(i, i ^ mask) for i in range(size)])


def after(arr, *deps):
    return lax.optimization_barrier((arr,) + deps)[0]


def stream_send(shard, depth):
    return [shard] + [
        lax.ppermute(shard, "stream", [(i, (i + d) % depth) for i in range(depth)])
        for d in range(1, depth)
    ]


def stream_rows(pieces, depth):
    shard = pieces[0]
    ring = pieces[::-1]
    place = lax.axis_index("stream")
    rows = shard.shape[0]
    both = jnp.concatenate(ring + ring, axis=0)
    return lax.dynamic_slice_in_dim(both, (depth - 1 - place) * rows, depth * rows, 0)


class Spread:
    def __init__(self, block, size, flip):
        self.size = size
        bits = [1 << b for b in range(1, size.bit_length() - 1)]
        self.bits = bits[::-1] if flip else bits
        self.block = block
        self.found = {0: block}

    def near(self, *deps):
        block = after(self.block, *deps) if deps else self.block
        for bit in self.bits:
            self.found[bit] = xor_send(block, self.size, bit)
        return self

    def near_all(self):
        for r in range(2, self.size, 2):
            self.found[r] = xor_send(self.block, self.size, r)
        return self

    def far(self, *deps):
        for bit in self.bits:
            for r in list(self.found):
                if r ^ bit not in self.found and r < 2 * max(self.bits):
                    src = self.found[r]
                    self.found[r ^ bit] = xor_send(after(src, *deps) if deps else src, self.size, bit)
        return self

    def far_halves(self):
        one, two = self.bits[:2]
        half = self.block.shape[1] // 2
        self.cuts = [self.found[one][:, :half], self.found[two][:, half:]]
        left = xor_send(self.cuts[0], self.size, two)
        right = xor_send(self.cuts[1], self.size, one)
        self.found[one ^ two] = jnp.concatenate([left, right], axis=1)
        return self.far()

    def cores(self, *deps):
        parts = [self.found[2 * r] for r in range(self.size // 2)]
        if deps:
            parts = lax.optimization_barrier(tuple(parts) + deps)[: len(parts)]
        stack = jnp.stack(parts)
        return [stack, xor_send(stack, self.size, 1)]


def beside(parts):
    return parts[0] if len(parts) == 1 else jnp.concatenate(parts, axis=-1)


class Reduce:
    def __init__(self, grads, size, depth, order=None, rest=None):
        self.size, self.depth = size, depth
        nbits = size.bit_length() - 1
        self.rest = list(range(nbits))[::-1] if rest is None else list(rest)
        self.order = list(range(nbits)) if order is None else list(order)
        self.cur = [
            g.reshape([2] * len(self.rest) + [g.shape[0] // 2 ** len(self.rest), g.shape[1]])
            if g.ndim == 2
            else g
            for g in grads
        ]

    def send(self):
        place = lax.axis_index("seq")
        bit = self.order.pop(0)
        axis = self.rest.index(bit)
        own = (place >> bit) & 1
        self.out = beside([lax.dynamic_index_in_dim(c, 1 - own, axis, False) for c in self.cur])
        self.kept = [lax.dynamic_index_in_dim(c, own, axis, False) for c in self.cur]
        self.flight = xor_send(self.out, self.size, 1 << bit)
        self.rest.pop(axis)
        return self

    def add(self, *deps):
        got = after(self.flight, *deps) if deps else self.flight
        self.cur = [(beside(self.kept).astype(f32) + got.astype(f32)).astype(bf16)]
        return self

    def cut(self, at):
        (cur,) = self.cur
        parts = [
            Reduce([cur[..., :at]], self.size, self.depth, self.order, self.rest),
            Reduce([cur[..., at:]], self.size, self.depth, self.order[::-1], self.rest),
        ]
        return parts

    def send_stream(self):
        while self.order:
            self.send().add()
        depth = self.depth
        level = lax.axis_index("stream")
        cur = beside(self.cur)
        self.out = cur
        cur = cur.reshape(depth, cur.shape[0] // depth, cur.shape[1])
        self.total = lax.dynamic_index_in_dim(cur, level, 0, False).astype(f32)
        self.flights = []
        for d in range(1, depth):
            piece = lax.dynamic_index_in_dim(cur, (level + d) % depth, 0, False)
            self.flights.append(
                lax.ppermute(piece, "stream", [(i, (i + d) % depth) for i in range(depth)])
            )
        return self

    def done(self, *deps):
        total = self.total
        for f in self.flights:
            total = total + (after(f, *deps) if deps else f).astype(f32)
        return total


def lanes(shape):
    return lax.broadcasted_iota(jnp.int32, shape, len(shape) - 1)


def block_ones(width, part):
    r = lax.broadcasted_iota(jnp.int32, (width, width), 0) // part
    c = lax.broadcasted_iota(jnp.int32, (width, width), 1) // part
    return jnp.where(r == c, 1.0, 0.0).astype(bf16)


def fetch_start(stacks, dest, me, sems, col=0, width=None, at=0):
    half = stacks[0].shape[0]
    rows = dest.shape[0] // (2 * half)
    width = width or stacks[0].shape[2]
    copies = []
    for c, ref in enumerate(stacks):
        for r in range(half):
            off = pl.multiple_of((me ^ (2 * r + c)) * rows, 8)
            copy = pltpu.make_async_copy(
                ref.at[r, :, pl.ds(col, width)],
                dest.at[pl.ds(off, rows), pl.ds(at, width)],
                sems.at[2 * r + c],
            )
            copy.start()
            copies.append(copy)
    return copies


def pair_maps(feat_ref, dest, pairs, which):
    width = 128
    lane = lanes((width, width))
    row = lax.broadcasted_iota(jnp.int32, (width, width), 0)
    for p in range(pairs):
        both = feat_ref[pl.ds(p * width, width), :].astype(f32)
        half = width // 2
        other = pltpu.roll(both, half, 1)
        if which == 0:
            signed = jnp.where(lane < half, both, -other)
        else:
            signed = jnp.where(lane < half, other, -both)
        dest[p, :, pl.ds(0, width)] = jnp.where(row < half, signed, 0.0).astype(bf16)
        dest[p, :, pl.ds(width, width)] = jnp.where(row >= half, signed, 0.0).astype(bf16)


def features(logits_of, ones):
    halves = [one[:, j * 128 : (j + 1) * 128] for one in logits_of for j in range(2)]
    low = lanes(halves[0].shape) < 64
    tops = [
        (
            jnp.max(jnp.where(low, one, -jnp.inf), axis=1, keepdims=True),
            jnp.max(jnp.where(low, -jnp.inf, one), axis=1, keepdims=True),
        )
        for one in halves
    ]
    exps = [jnp.exp(one - jnp.where(low, *top)) for one, top in zip(halves, tops)]
    exps = [jnp.concatenate(exps[2 * i : 2 * i + 2], axis=1) for i in range(len(logits_of))]
    sums = [mm(e.astype(bf16), ones) for e in exps]
    return [(e / t).astype(bf16) for e, t in zip(exps, sums)]


def augmented(two):
    low = lanes(two.shape) < 64
    one = jnp.ones_like(two)
    return jnp.where(low, two, one), jnp.where(low, one, two)


def pack_states(get, dest, pairs, zsum):
    shape = (128, 128)
    lane = lanes(shape)
    low = lane < 64
    zt = jnp.zeros(shape, f32)
    for p in range(pairs):
        a, b = get(2 * p), get(2 * p + 1)
        dest[p] = jnp.where(low, a, b).astype(bf16)
        if zsum:
            za = jnp.sum(jnp.where(low, 0.0, a), axis=1, keepdims=True)
            zb = jnp.sum(jnp.where(low, b, 0.0), axis=1, keepdims=True)
        else:
            za, zb = a, b
        zt = jnp.where(lane == 64 + 2 * p, za, zt)
        zt = jnp.where(lane == 2 * p + 1, zb, zt)
    dest[pairs] = zt.astype(bf16)


def unpack_states(me, keep_ref, blocks, put, base, count, pairs, back):
    shape = (128, 128)
    lane = lanes(shape)
    low = lane < 64
    size = 2 * blocks.shape[1]
    coefs = [None]
    for r in range(1, size):
        j = me ^ r
        c = jnp.where(j > me if back else j < me, 1.0, 0.0)
        for i in range(size):
            between = ((i > me) & (i < j)) if back else ((i > j) & (i < me))
            c = c * jnp.where(between, keep_ref[i], 1.0)
        coefs.append(c)

    def total(i):
        acc = jnp.zeros(shape, f32)
        for r in range(1, size):
            acc = acc + coefs[r] * blocks[r % 2, r // 2, i].astype(f32)
        return acc

    zt = total(pairs)
    for q in range(count):
        p = base + q
        two = total(p)
        za = jnp.sum(jnp.where(lane == 64 + 2 * p, zt, 0.0), axis=1, keepdims=True)
        zb = jnp.sum(jnp.where(lane == 2 * p + 1, zt, 0.0), axis=1, keepdims=True)
        if back:
            put(2 * q, jnp.where(low, two, jnp.where(lane == 64, za, 0.0)))
            put(2 * q + 1, jnp.where(low, jnp.where(lane == 0, zb, 0.0), two))
        else:
            put(2 * q, jnp.where(low, two, za))
            put(2 * q + 1, jnp.where(low, zb, two))


def normed(values, gain, bias):
    mean = jnp.mean(values, axis=1, keepdims=True)
    cent = values - mean
    rstd = lax.rsqrt(jnp.mean(cent * cent, axis=1, keepdims=True) + epsilon)
    hat = cent * rstd
    return hat * gain + bias, hat, rstd


def normed_back(grad, hat, rstd, gain):
    dhat = grad * gain
    return rstd * (
        dhat
        - jnp.mean(dhat, axis=1, keepdims=True)
        - hat * jnp.mean(dhat * hat, axis=1, keepdims=True)
    )


def keys_body(n_seq, pairs, me_ref, cend_ref, x_ref, cnt_ref, *refs):
    width = x_ref.shape[1]
    wl = refs[:2]
    (h_ref, k_ref, v_ref, phi_ref, st_ref, gb_ref, feat_ref, w1, maps, state, sems) = refs[2:]
    step = pl.program_id(0)

    @pl.when(step == 0)
    def _():
        me = me_ref[0]
        copies = fetch_start(wl, w1, me, sems.at[0], width, 2 * width + 256)
        for c in copies:
            c.wait()
        gb_ref[...] = w1[:, pl.ds(2 * width + 128, 128)].astype(f32).T[:8]
        feat_ref[...] = w1[:, pl.ds(2 * width, 128)]
        pair_maps(feat_ref, maps, pairs, 1)
        state[...] = jnp.zeros_like(state)

    gb = gb_ref[...]
    out, _, _ = normed(x_ref[...].astype(f32), gb[0:1], gb[2:3])
    h1 = out.astype(bf16)
    h_ref[...] = h1
    keys = mm(h1, w1[:, pl.ds(0, width)]).astype(bf16)
    vals = mm(h1, w1[:, pl.ds(width, width)]).astype(bf16)
    k_ref[...] = keys
    v_ref[...] = vals
    ones = block_ones(256, 64)
    last = cend_ref[cend_ref.shape[0] - 1]
    used = jnp.where(cnt_ref[...] == last, 1.0, 0.0).astype(bf16)
    for g in range(0, pairs, GF):
        group = range(g, min(g + GF, pairs))
        phis = features([mm(keys[:, p * 128 : (p + 1) * 128], maps[p]) for p in group], ones)
        for p, phi in zip(group, phis):
            phi_ref[:, pl.ds(p * 256, 256)] = phi
            va, vb = augmented(vals[:, p * 128 : (p + 1) * 128])
            state[2 * p] += mm_f(phi[:, :128], va * used)
            state[2 * p + 1] += mm_f(phi[:, 128:], vb * used)

    @pl.when(step == pl.num_programs(0) - 1)
    def _():
        pack_states(lambda h: state[h], st_ref, pairs, False)


def local_body(base, pairs, me_ref, cend_ref, h_ref, phik_ref, v_ref, cnt_ref, row_ref, feat_ref, *refs):
    wq = refs[:2]
    (q_ref, phiq_ref, num_ref, den_ref, srel_ref, state, w1, maps, sems) = refs[-9:]
    step = pl.program_id(0)
    width = h_ref.shape[1]

    @pl.when(step == 0)
    def _():
        copies = fetch_start(wq, w1, me_ref[0], sems, 0, width)
        pair_maps(feat_ref, maps, pairs, 0)
        if base:
            state[...] = refs[2][...]
        else:
            state[...] = jnp.zeros_like(state)
        for c in copies:
            c.wait()

    queries = mm(h_ref[...], w1[...]).astype(bf16)
    q_ref[...] = queries
    ones = block_ones(256, 64)
    size = h_ref.shape[0]
    cnt = cnt_ref[...]
    first, last = cend_ref[base + step], cend_ref[base + step + 1]
    row_id = lax.broadcasted_iota(jnp.int32, (size, size), 0)
    mask = (row_id >= lanes((size, size))) & (cnt == row_ref[...])
    before = jnp.where(cnt == first, 1.0, 0.0)
    after = jnp.where(cnt == last, 1.0, 0.0).astype(bf16)
    keep = jnp.where(first == last, 1.0, 0.0)
    low = lanes((size, 128)) < 64
    for g in range(0, pairs, GF):
        group = range(g, min(g + GF, pairs))
        phis = features([mm(queries[:, p * 128 : (p + 1) * 128], maps[p]) for p in group], ones)
        for p, phi in zip(group, phis):
            phiq_ref[:, pl.ds(p * 256, 256)] = phi
        pqs = [phi[:, j * 128 : (j + 1) * 128] for phi in phis for j in range(2)]
        heads = [2 * p + j for p in group for j in range(2)]
        pks = [phik_ref[:, pl.ds(h * 128, 128)] for h in heads]
        scores = [jnp.where(mask, mm_t(pq, pk), 0.0).astype(bf16) for pq, pk in zip(pqs, pks)]
        val_of = [v for p in group for v in augmented(v_ref[:, p * 128 : (p + 1) * 128])]
        res = []
        for h, pq, pk, sc, val in zip(heads, pqs, pks, scores, val_of):
            st = state[h]
            st_b = st.astype(bf16)
            srel_ref[0, h] = st_b
            res.append(mm(sc, val) + before * mm(pq, st_b))
            state[h] = keep * st + mm_f(pk, val * after)
        for i, p in enumerate(group):
            two = pl.ds(p * 128, 128)
            num_ref[:, two] = jnp.where(low, res[2 * i], res[2 * i + 1])
            den_ref[:, two] = pltpu.roll(jnp.where(low, res[2 * i + 1], res[2 * i]), 64, 1)


def middle_body(
    n_seq, pairs, me_ref, keep_ref, x_ref, dy_ref, num_ref, den_ref, phiq_ref, cnt_ref, gb_ref, *refs
):
    width = x_ref.shape[1]
    wf, wp, sts = (refs[2 * i : 2 * i + 2] for i in range(3))
    (
        y_ref, o_ref, h_ref, a_ref, df_ref, dat_ref, dr_ref, dd_ref, sin_ref, gst_ref, sum_ref,
        w_out, w_fc, w_proj, rden, state, stv, sems,
    ) = refs[6:]
    step = pl.program_id(0)
    chunk = 768
    hidden = w_fc.shape[1]
    size = x_ref.shape[0]

    @pl.when(step == 0)
    def _():
        me = me_ref[0]
        st_copies = []
        for c in range(2):
            st_copies.append(pltpu.make_async_copy(sts[c], stv.at[c], sems.at[3, c]))
            st_copies[c].start()
        copies = fetch_start(wf, w_out, me, sems.at[0], hidden, width)
        copies += fetch_start(wf, w_fc, me, sems.at[1], 0, hidden)
        copies += fetch_start(wp, w_proj, me, sems.at[2])
        for c in st_copies:
            c.wait()

        def put(h, value):
            sin_ref[h] = value.astype(bf16)

        unpack_states(me, keep_ref, stv, put, 0, pairs, pairs, False)
        state[...] = jnp.zeros_like(state)
        sum_ref[...] = jnp.zeros_like(sum_ref)
        for c in copies:
            c.wait()

    gb = gb_ref[...]
    low = lanes((size, 128)) < 64
    start = jnp.where(cnt_ref[...] == 0.0, 1.0, 0.0)
    start_b = start.astype(bf16)
    res = [mm(phiq_ref[:, pl.ds(h * 128, 128)], sin_ref[h]) for h in range(2 * pairs)]
    for p in range(pairs):
        two = pl.ds(p * 128, 128)
        ra, rb = res[2 * p], res[2 * p + 1]
        num = num_ref[:, two] + start * jnp.where(low, ra, rb)
        den = den_ref[:, two] + start * pltpu.roll(jnp.where(low, rb, ra), 64, 1)
        inv = 1.0 / den
        rden[:, two] = inv
        o_ref[:, two] = (num * inv).astype(bf16)
    x = x_ref[...].astype(f32)
    attn = mm(o_ref[...], w_out[...])
    mid = x + attn
    out, hat, rstd = normed(mid, gb[1:2], gb[3:4])
    h2 = out.astype(bf16)
    h_ref[...] = h2
    dy_b = dy_ref[...]
    branch = jnp.zeros((size, width), f32)
    dh2 = jnp.zeros((size, width), f32)
    for c in range(w_fc.shape[1] // chunk):
        cols = pl.ds(c * chunk, chunk)
        fc = mm(h2, w_fc[:, cols])
        square = fc * fc
        tan = jnp.tanh(fc * (GC + GC * GA * square))
        half = 0.5 + 0.5 * tan
        act = (fc * half).astype(bf16)
        a_ref[:, cols] = act
        branch = branch + mm(act, w_proj[cols, :])
        slope = half + fc * (1.0 - half) * half * (2.0 * GC + 6.0 * GC * GA * square)
        dfc = (mm_t(dy_b, w_proj[cols, :]) * slope).astype(bf16)
        df_ref[:, cols] = dfc
        dh2 = dh2 + mm_t(dfc, w_fc[:, cols])
    y = mid + branch
    y_ref[...] = y.astype(bf16)
    sum_ref[0:1] += jnp.sum(attn * attn, axis=0, keepdims=True)
    sum_ref[1:2] += jnp.sum(branch * branch, axis=0, keepdims=True)
    sum_ref[2:3] += jnp.sum(y * y, axis=0, keepdims=True)
    sum_ref[3:4] += jnp.sum(dh2 * hat, axis=0, keepdims=True)
    sum_ref[4:5] += jnp.sum(dh2, axis=0, keepdims=True)
    dr = dy_b.astype(f32) + normed_back(dh2, hat, rstd, gb[1:2])
    dr_ref[...] = dr
    dat = dr.astype(bf16)
    dat_ref[...] = dat
    d_o = mm_t(dat, w_out[...])
    ones = block_ones(256, 64)
    lane = lanes((size, 128))
    quads = range(pairs // 2)
    fours = [pl.ds(q * 256, 256) for q in quads]
    d_os = [d_o[:, q * 256 : (q + 1) * 256] for q in quads]
    prods = [d * o_ref[:, c].astype(f32) for d, c in zip(d_os, fours)]
    his = [a.astype(bf16) for a in prods]
    los = [(a - hi.astype(f32)).astype(bf16) for a, hi in zip(prods, his)]
    ddens = [-(mm(hi, ones) + mm(lo, ones)) * rden[:, c] for hi, lo, c in zip(his, los, fours)]
    dnums = [(d * rden[:, c]).astype(bf16) for d, c in zip(d_os, fours)]
    near = lane & 63
    for p in range(pairs):
        sub = slice((p % 2) * 128, (p % 2 + 1) * 128)
        dd = pltpu.roll(ddens[p // 2][:, sub], 64, 1)
        dhi = dd.astype(bf16)
        dlo = (dd - dhi.astype(f32)).astype(bf16)
        aux = jnp.where(near == 0, dhi.astype(f32), jnp.where(near == 1, dlo.astype(f32), 0.0)).astype(bf16)
        dn = dnums[p // 2][:, sub]
        dd_ref[:, pl.ds(p * 256, 128)] = jnp.where(low, dn, aux)
        dd_ref[:, pl.ds(p * 256 + 128, 128)] = jnp.where(low, aux, dn)
    for h in range(2 * pairs):
        own = pl.ds(h * 128, 128)
        state[h] += mm_f(phiq_ref[:, own], dd_ref[:, own] * start_b)

    @pl.when(step == pl.num_programs(0) - 1)
    def _():
        pack_states(lambda h: state[h], gst_ref, pairs, True)
        total = jnp.sum(sum_ref[...], axis=1, keepdims=True)
        high = total.astype(bf16).astype(f32)
        place = lanes((8, 128))
        tile = jnp.where(place == 126, high, jnp.where(place == 127, total - high, 0.0))
        tile = jnp.concatenate([tile, jnp.zeros_like(tile)], axis=0)
        top = gst_ref[pairs, pl.ds(0, 16), :].astype(f32)
        gst_ref[pairs, pl.ds(0, 16), :] = (top + tile).astype(bf16)


def back_body(
    base, pairs, all_pairs, me_ref, keep_ref, cend_ref, q_ref, k_ref, v_ref, phiq_ref, phik_ref, dd_ref, srel_ref, sin_ref,
    cnt_ref, row_ref, feat_ref, *refs
):
    sts = refs[:2]
    (dqkv_ref, gfeat_ref, mapq, mapk, state, gq, gk, stv, sems) = refs[2:]
    step = pl.program_id(0)
    nblk = pl.num_programs(0)
    here = nblk - 1 - step

    @pl.when(step == 0)
    def _():
        copies = []
        for c in range(2):
            copies.append(pltpu.make_async_copy(sts[c], stv.at[c], sems.at[c]))
            copies[c].start()
        pair_maps(feat_ref, mapq, pairs, 0)
        pair_maps(feat_ref, mapk, pairs, 1)
        gq[...] = jnp.zeros_like(gq)
        gk[...] = jnp.zeros_like(gk)
        for c in copies:
            c.wait()

        def put(h, value):
            state[h] = value

        unpack_states(me_ref[0], keep_ref, stv, put, base, pairs, all_pairs, True)

    size = q_ref.shape[0]
    width = q_ref.shape[1]
    cnt = cnt_ref[...]
    first, last = cend_ref[here], cend_ref[here + 1]
    row_id = lax.broadcasted_iota(jnp.int32, (size, size), 0)
    col_id = lanes((size, size))
    same = cnt == row_ref[...]
    mask = (row_id >= col_id) & same
    mask_t = (col_id >= row_id) & same
    before = jnp.where(cnt == first, 1.0, 0.0).astype(bf16)
    after = jnp.where(cnt == last, 1.0, 0.0).astype(bf16)
    keep = jnp.where(first == last, 1.0, 0.0)
    opened = jnp.where(first == 0.0, 1.0, 0.0)
    ones = block_ones(256, 64)
    low = lanes((size, 128)) < 64
    heads = range(2 * pairs)
    cols = [pl.ds(h * 128, 128) for h in heads]
    vals = [v for p in range(pairs) for v in augmented(v_ref[:, pl.ds(p * 128, 128)])]
    scores_t = [
        jnp.where(mask_t, mm_t(phik_ref[:, c], phiq_ref[:, c]), 0.0).astype(bf16) for c in cols
    ]
    dsc = [jnp.where(mask, mm_t(dd_ref[:, c], v), 0.0).astype(bf16) for c, v in zip(cols, vals)]
    dsc_t = [jnp.where(mask_t, mm_t(v, dd_ref[:, c]), 0.0).astype(bf16) for c, v in zip(cols, vals)]
    sts = [
        (srel_ref[0, h].astype(f32) + opened * sin_ref[h].astype(f32)).astype(bf16) for h in heads
    ]
    dsts = [state[h].astype(bf16) for h in heads]
    ddws = [dd_ref[:, c] * before for c in cols]
    dphi_q = [mm(dsc[h], phik_ref[:, cols[h]]) + mm_t(ddws[h], sts[h]) for h in heads]
    dphi_k = [mm(dsc_t[h], phiq_ref[:, cols[h]]) + mm_t(vals[h] * after, dsts[h]) for h in heads]
    dvs = [mm(scores_t[h], dd_ref[:, cols[h]]) + mm(phik_ref[:, cols[h]] * after, dsts[h]) for h in heads]
    for h in heads:
        state[h] = keep * state[h] + mm_f(phiq_ref[:, cols[h]], ddws[h])
    for p in range(pairs):
        dqkv_ref[:, pl.ds(2 * width + p * 128, 128)] = jnp.where(low, dvs[2 * p], dvs[2 * p + 1]).astype(bf16)
    for phi_ref, dphi, rows_ref, maps, acc, base_col in (
        (phiq_ref, dphi_q, q_ref, mapq, gq, 0),
        (phik_ref, dphi_k, k_ref, mapk, gk, width),
    ):
        phis = [phi_ref[:, pl.ds(p * 256, 256)].astype(f32) for p in range(pairs)]
        dphis = [jnp.concatenate(dphi[2 * p : 2 * p + 2], axis=1) for p in range(pairs)]
        totals = [mm((phi * d).astype(bf16), ones) for phi, d in zip(phis, dphis)]
        dlogs = [(phi * (d - t)).astype(bf16) for phi, d, t in zip(phis, dphis, totals)]
        for p in range(pairs):
            two = pl.ds(p * 128, 128)
            dqkv_ref[:, pl.ds(base_col + p * 128, 128)] = mm_t(dlogs[p], maps[p]).astype(bf16)
            acc[p] += mm_f(rows_ref[:, two], dlogs[p])

    @pl.when(step == nblk - 1)
    def _():
        lane = lanes((128, 128))
        row = lax.broadcasted_iota(jnp.int32, (128, 128), 0)
        for p in range(pairs):
            outs = []
            for acc in (gq, gk):
                one = jnp.where(row < 64, acc[p, :, :128], acc[p, :, 128:])
                outs.append(one - pltpu.roll(one, 64, 1))
            gfeat_ref[pl.ds(p * 128, 128), :] = jnp.where(lane < 64, outs[0], -outs[1]).astype(bf16)


def enter_body(groups, me_ref, x_ref, dr_ref, gb_ref, *refs):
    width = x_ref.shape[1]
    grads = refs[:groups]
    wl = refs[groups : groups + 2]
    (dx_ref, sum_ref, w1, sems) = refs[groups + 2 :]

    @pl.when(pl.program_id(0) == 0)
    def _():
        me = me_ref[0]
        copies = fetch_start(wl, w1, me, sems.at[0], 0, 3 * width)
        sum_ref[...] = jnp.zeros_like(sum_ref)
        for c in copies:
            c.wait()

    gb = gb_ref[...]
    _, hat, rstd = normed(x_ref[...].astype(f32), gb[0:1], gb[2:3])
    part = width // groups
    dh = jnp.zeros(x_ref.shape, f32)
    for g in range(groups):
        for i in range(3):
            dh = dh + mm_t(grads[g][:, pl.ds(i * part, part)], w1[:, pl.ds(i * width + g * part, part)])
    dx_ref[...] = dr_ref[...] + normed_back(dh, hat, rstd, gb[0:1])
    sum_ref[0:1] += jnp.sum(dh * hat, axis=0, keepdims=True)
    sum_ref[1:2] += jnp.sum(dh, axis=0, keepdims=True)


def whole(*_):
    return pl.BlockSpec(memory_space=pl.ANY)


def smem():
    return pl.BlockSpec(memory_space=pltpu.SMEM)


def rows_spec(size, cols, back=None):
    if back is None:
        return pl.BlockSpec((size, cols), lambda i: (i, 0))
    return pl.BlockSpec((size, cols), lambda i: (back - 1 - i, 0))


def full_spec(shape):
    zeros = (0,) * len(shape)
    return pl.BlockSpec(shape, lambda i: zeros)


def sds(shape, kind):
    return jax.ShapeDtypeStruct(shape, kind)


def cparams():
    return pltpu.CompilerParams(
        dimension_semantics=("arbitrary",), vmem_limit_bytes=58 * 1024 * 1024
    )


def cost(micros):
    return pl.CostEstimate(
        flops=int(micros * 5e8), transcendentals=0, bytes_accessed=int(micros * 1e6)
    )


def dma(*shape):
    return pltpu.SemaphoreType.DMA(shape)


def shards(n_seq, depth, inputs, resets, norm_gains, norm_biases, w_qkv, w_feat, w_out, w_fc, w_proj, cotangent):
    tokens, width = inputs.shape[1], inputs.shape[2]
    hidden = w_fc.shape[1]
    head_dim = w_feat.shape[1] // 2
    heads = width // head_dim
    pairs = heads // 2
    rows = w_qkv.shape[0]
    nblk = tokens // BT
    x, dy = inputs[0], cotangent[0]
    me = lax.axis_index("seq")
    me_arr = me.reshape(1).astype(jnp.int32)

    marks = resets[0].reshape(nblk, BT).astype(bf16)
    flag = jnp.where(jnp.max(resets) == 0, 1.0, 0.0).astype(bf16)
    upper = jnp.triu(jnp.ones((BT, BT), bf16))
    inner = jnp.dot(marks, upper, preferred_element_type=f32)
    ends = jnp.cumsum(inner[:, -1])
    cend = jnp.concatenate([jnp.zeros((1,), f32), ends])
    counts = inner + cend[:-1, None]
    cnt_col = counts.reshape(tokens, 1)
    cnt_row = counts.reshape(1, tokens)

    norms = jnp.concatenate(
        [norm_gains, norm_biases, jnp.broadcast_to(flag, (rows, 1)), jnp.zeros((rows, 123), bf16)],
        axis=1,
    )
    first = stream_rows(stream_send(jnp.concatenate([w_qkv, w_feat, norms], axis=1), depth), depth)
    first = Spread(first, n_seq, False).near()
    up = jnp.concatenate([w_fc, w_out], axis=1)
    first.far_halves()
    up = stream_send(after(up, first.block), depth)
    first_blocks = first.cores()
    up = stream_rows([after(a, first_blocks[0]) for a in up], depth)
    up = Spread(up, n_seq, True).near(first_blocks[0])
    proj_pieces = stream_send(after(w_proj, first_blocks[1], up.block), depth)
    me_first = after(me_arr, up.block)

    packed = (pairs + 1, 128, 128)
    full = (heads, 128, 128)
    h_one, keys, vals, phi_k, state, gb, feat_all = pl.pallas_call(
        functools.partial(keys_body, n_seq, pairs),
        name="keys",
        cost_estimate=cost(22),
        grid=(tokens // TK,),
        in_specs=[smem(), smem(), rows_spec(TK, width), rows_spec(TK, 1)] + [whole()] * 2,
        out_specs=[rows_spec(TK, width)] * 3
        + [rows_spec(TK, 2 * width), full_spec(packed), full_spec((8, width)), full_spec((width, 128))],
        out_shape=[sds((tokens, width), bf16)] * 3
        + [sds((tokens, 2 * width), bf16), sds(packed, bf16), sds((8, width), f32), sds((width, 128), bf16)],
        scratch_shapes=[
            pltpu.VMEM((width, 2 * width + 256), bf16),
            pltpu.VMEM((pairs, 128, 256), bf16),
            pltpu.VMEM(full, f32),
            dma(2, n_seq),
        ],
        compiler_params=cparams(),
    )(me_first, cend, x, cnt_col, *first_blocks)
    level = lax.axis_index("stream")
    flags = gb[4].reshape(n_seq, depth, rows)[:, :, 0]
    keeps = lax.dynamic_index_in_dim(flags, level, 1, False)
    spread = Spread(state, n_seq, False).near_all()
    up.far(gb)
    proj = Spread(stream_rows([after(a, gb) for a in proj_pieces], depth), n_seq, False).near()
    part_blk = nblk // 2
    local = []
    for part in range(2):
        base = part * part_blk

        def here(size, cols):
            return pl.BlockSpec((size, cols), lambda i: (base + i, 0))

        blocks_out = [
            sds((tokens, width), bf16), sds((tokens, 2 * width), bf16), sds((tokens, width), f32),
            sds((tokens, width), f32), sds((nblk,) + full, bf16),
        ]
        if part:
            me_two = after(me_arr, up_blocks[0], *[proj.found[b] for b in proj.bits], states[0])
        else:
            me_two = after(me_arr, proj.block, state, after(up.found[up.bits[0]], gb))
        local = pl.pallas_call(
            functools.partial(local_body, base, pairs),
            name="local",
            cost_estimate=cost(15),
            grid=(part_blk,),
            in_specs=[
                smem(), smem(), here(BT, width), here(BT, 2 * width), here(BT, width), here(BT, 1),
                pl.BlockSpec((1, BT), lambda i: (0, base + i)), full_spec((width, 128)),
            ]
            + [whole()] * 2
            + ([full_spec(full)] + [whole()] * 5 if part else []),
            out_specs=[
                here(BT, width), here(BT, 2 * width), here(BT, width), here(BT, width),
                pl.BlockSpec((1,) + full, lambda i: (base + i, 0, 0, 0)), full_spec(full),
            ],
            out_shape=blocks_out + [sds(full, f32)],
            scratch_shapes=[
                pltpu.VMEM((width, width), bf16),
                pltpu.VMEM((pairs, 128, 256), bf16),
                dma(n_seq),
            ],
            input_output_aliases={11 + i: i for i in range(5)} if part else {},
            compiler_params=cparams(),
        )(
            me_two, cend, h_one, phi_k, vals, cnt_col, cnt_row, feat_all, *first_blocks,
            *([local[5]] + list(local[:5]) if part else []),
        )
        if part == 0:
            event = local[5]
            proj.far(event)
            states = spread.cores(event)
            up_blocks = up.cores(event)
    queries, phi_q, num, den, srel, event = local
    proj_blocks = proj.cores(event)

    y, att, h_two, act, d_fc, d_att, d_mid, dd, s_in, g_state, sums = pl.pallas_call(
        functools.partial(middle_body, n_seq, pairs),
        name="middle",
        cost_estimate=cost(43),
        grid=(tokens // TM,),
        in_specs=[
            smem(), smem(), rows_spec(TM, width), rows_spec(TM, width), rows_spec(TM, width),
            rows_spec(TM, width), rows_spec(TM, 2 * width), rows_spec(TM, 1), full_spec((8, width)),
        ]
        + [whole()] * 6,
        out_specs=[
            rows_spec(TM, width), rows_spec(TM, width), rows_spec(TM, width), rows_spec(TM, hidden),
            rows_spec(TM, hidden), rows_spec(TM, width), rows_spec(TM, width), rows_spec(TM, 2 * width),
            full_spec(full), full_spec(packed), full_spec((8, width)),
        ],
        out_shape=[
            sds((tokens, width), bf16), sds((tokens, width), bf16), sds((tokens, width), bf16),
            sds((tokens, hidden), bf16), sds((tokens, hidden), bf16), sds((tokens, width), bf16),
            sds((tokens, width), f32), sds((tokens, 2 * width), bf16), sds(full, bf16), sds(packed, bf16),
            sds((8, width), f32),
        ],
        scratch_shapes=[
            pltpu.VMEM((width, width), bf16),
            pltpu.VMEM((width, hidden), bf16),
            pltpu.VMEM((hidden, width), bf16),
            pltpu.VMEM((TM, width), f32),
            pltpu.VMEM(full, f32),
            pltpu.VMEM((2, n_seq // 2) + packed, bf16),
            dma(4, n_seq),
        ],
        compiler_params=cparams(),
    )(
        me_arr, keeps, x, dy, num, den, phi_q, cnt_col, gb,
        *up_blocks, *proj_blocks, *states,
    )

    spread = Spread(g_state, n_seq, True).near_all()
    norm_two = jnp.stack([sums[3], sums[4]], axis=1).astype(bf16)
    norm_two = jnp.concatenate([norm_two, jnp.zeros((width, 126), bf16)], axis=1)
    nbits = n_seq.bit_length() - 1
    g_fc = mm_f(h_two, d_fc).astype(bf16)
    g_out = mm_f(att, d_att).astype(bf16)
    red_fc = Reduce([g_fc, g_out, norm_two], n_seq, depth, [0] + list(range(1, nbits))[::-1]).send()
    g_states = spread.cores(red_fc.out)
    g_proj = mm_f(after(act, red_fc.out, g_states[0]), dy).astype(bf16)
    red_proj = Reduce([g_proj], n_seq, depth).send()
    red_fc.add(red_proj.out).send()
    red_proj.add(red_fc.out).send()
    me_back = after(me_arr, red_proj.out, red_fc.out)
    squares = sum(
        jnp.sum(stack[:, pairs, :3, 126:].astype(f32), axis=(0, 2)) for stack in g_states
    )
    branch_rms = jnp.sqrt(squares / (tokens * n_seq * width)).reshape(1, 3)

    groups = 2
    some = pairs // groups
    part = some * 128
    d_qkv, g_feat = [], []
    for g in range(groups):

        def spec(cols):
            return pl.BlockSpec((BT, cols), lambda i: (nblk - 1 - i, g))

        def one_group(shape):
            return pl.BlockSpec(shape, lambda i: (g,) + (0,) * (len(shape) - 1))

        one = (2 * some, 128, 128)
        d_one, g_one = pl.pallas_call(
            functools.partial(back_body, g * some, some, pairs),
            name="back",
            cost_estimate=cost(19),
            grid=(nblk,),
            in_specs=[
                smem(), smem(), smem(), spec(part), spec(part), spec(part), spec(2 * part), spec(2 * part),
                spec(2 * part), pl.BlockSpec((1,) + one, lambda i: (nblk - 1 - i, g, 0, 0)), one_group(one),
                rows_spec(BT, 1, nblk), pl.BlockSpec((1, BT), lambda i: (0, nblk - 1 - i)),
                one_group((part, 128)),
            ]
            + [whole()] * 2,
            out_specs=[rows_spec(BT, 3 * part, nblk), full_spec((part, 128))],
            out_shape=[sds((tokens, 3 * part), bf16), sds((part, 128), bf16)],
            scratch_shapes=[
                pltpu.VMEM((some, 128, 256), bf16),
                pltpu.VMEM((some, 128, 256), bf16),
                pltpu.VMEM(one, f32),
                pltpu.VMEM((some, 128, 256), f32),
                pltpu.VMEM((some, 128, 256), f32),
                pltpu.VMEM((2, n_seq // 2) + packed, bf16),
                dma(n_seq),
            ],
            compiler_params=cparams(),
        )(
            me_back, keeps, cend, queries, keys, vals, phi_q, phi_k, dd, srel, s_in, cnt_col, cnt_row,
            feat_all, *g_states,
        )
        d_qkv.append(d_one)
        g_feat.append(g_one)
        if g == 0:
            red_proj.add(d_one).send()
            me_back = after(me_arr, red_proj.out)

    last = d_qkv[-1]
    g_qkv = [mm_f(h_one, d).astype(bf16) for d in d_qkv]
    red_two = Reduce(g_qkv + [jnp.concatenate(g_feat, axis=0)], n_seq, depth).send()
    red_fc.add(red_two.out).send()
    red_proj.add(red_fc.out).send_stream()
    me_late = after(me_arr, red_proj.out, red_fc.out)
    dx, sums_one = pl.pallas_call(
        functools.partial(enter_body, groups),
        name="enter",
        cost_estimate=cost(11),
        grid=(tokens // TM,),
        in_specs=[smem(), rows_spec(TM, width), rows_spec(TM, width), full_spec((8, width))]
        + [rows_spec(TM, 3 * part)] * groups
        + [whole()] * 2,
        out_specs=[rows_spec(TM, width), full_spec((8, width))],
        out_shape=[sds((tokens, width), f32), sds((8, width), f32)],
        scratch_shapes=[pltpu.VMEM((width, 3 * width), bf16), dma(2, n_seq)],
        compiler_params=cparams(),
    )(me_late, x, d_mid, gb, *d_qkv, *first_blocks)
    norm_one = jnp.stack([sums_one[0], sums_one[1]], axis=1).astype(bf16)
    norm_one = jnp.concatenate([norm_one, jnp.zeros((width, 126), bf16)], axis=1)
    red_norm = Reduce([norm_one], n_seq, depth).send()
    red_a, red_b = red_two.add(dx).cut((groups * 3 * part + 256) // 2)
    red_a.send()
    red_norm.add(red_a.out)
    red_b.cur = [beside(red_b.cur + red_norm.cur)]
    red_b.send()
    red_fc.add(red_a.out, red_b.out).send_stream()
    grad_proj = red_proj.done(red_fc.out)
    while red_a.order:
        red_a.add().send()
        red_b.add().send()
    tail = Reduce(red_a.add().cur + red_b.add().cur, n_seq, depth, [], []).send_stream()
    grad_up = red_fc.done(tail.out)
    tail = tail.done()
    grads = [tail[:, g * 3 * part : (g + 1) * 3 * part] for g in range(groups)]
    grad_feat = tail[:, groups * 3 * part : groups * 3 * part + 128]
    norm_one = tail[:, groups * 3 * part + 128 :]
    grad_fc = grad_up[:, :hidden]
    grad_out = grad_up[:, hidden:]
    grad_qkv = jnp.concatenate(
        [grads[g][:, i * part : (i + 1) * part] for i in range(3) for g in range(groups)], axis=1
    )
    return (
        y[None],
        dx[None],
        jnp.concatenate([norm_one[:, 0:1], grad_out[:, width : width + 1]], axis=1),
        jnp.concatenate([norm_one[:, 1:2], grad_out[:, width + 1 : width + 2]], axis=1),
        grad_qkv,
        grad_feat,
        grad_out[:, :width],
        grad_fc,
        grad_proj,
        branch_rms,
    )


def solution(mesh):
    both = P(("seq", "stream"), None)
    acts = P("stream", "seq", None)
    placed = (acts, P("stream", "seq"), both, both, both, both, both, both, both, acts)
    return jax.shard_map(
        functools.partial(shards, mesh.shape["seq"], mesh.shape["stream"]),
        mesh=mesh,
        in_specs=placed,
        out_specs=(acts, acts, both, both, both, both, both, both, both, P("stream", None)),
        check_vma=False,
    )
```

```python
import functools

import jax
import jax.numpy as jnp
from jax import lax
from jax.experimental import pallas as pl
from jax.experimental.pallas import tpu as pltpu
from jax.sharding import PartitionSpec as P

BT = 256
GF = 6
TK = 512
TM = 256
epsilon = 1e-05
f32 = jnp.float32
bf16 = jnp.bfloat16
GC = 0.7978845608028654
GA = 0.044715


def mm(a, b):
    return jnp.dot(a, b, preferred_element_type=f32)


def mm_t(a, b):
    return lax.dot_general(a, b, (((1,), (1,)), ((), ())), preferred_element_type=f32)


def mm_f(a, b):
    return lax.dot_general(a, b, (((0,), (0,)), ((), ())), preferred_element_type=f32)


def xor_send(arr, size, mask):
    return lax.ppermute(arr, "seq", [(i, i ^ mask) for i in range(size)])


def after(arr, *deps):
    return lax.optimization_barrier((arr,) + deps)[0]


def stream_send(shard, depth):
    return [shard] + [
        lax.ppermute(shard, "stream", [(i, (i + d) % depth) for i in range(depth)])
        for d in range(1, depth)
    ]


def stream_rows(pieces, depth):
    shard = pieces[0]
    ring = pieces[::-1]
    place = lax.axis_index("stream")
    rows = shard.shape[0]
    both = jnp.concatenate(ring + ring, axis=0)
    return lax.dynamic_slice_in_dim(both, (depth - 1 - place) * rows, depth * rows, 0)


class Spread:
    def __init__(self, block, size, flip):
        self.size = size
        bits = [1 << b for b in range(1, size.bit_length() - 1)]
        self.bits = bits[::-1] if flip else bits
        self.block = block
        self.found = {0: block}

    def near(self, *deps):
        block = after(self.block, *deps) if deps else self.block
        for bit in self.bits:
            self.found[bit] = xor_send(block, self.size, bit)
        return self

    def near_all(self):
        for r in range(2, self.size, 2):
            self.found[r] = xor_send(self.block, self.size, r)
        return self

    def far(self, *deps):
        for bit in self.bits:
            for r in list(self.found):
                if r ^ bit not in self.found and r < 2 * max(self.bits):
                    src = self.found[r]
                    self.found[r ^ bit] = xor_send(after(src, *deps) if deps else src, self.size, bit)
        return self

    def far_halves(self):
        one, two = self.bits[:2]
        half = self.block.shape[1] // 2
        self.cuts = [self.found[one][:, :half], self.found[two][:, half:]]
        left = xor_send(self.cuts[0], self.size, two)
        right = xor_send(self.cuts[1], self.size, one)
        self.found[one ^ two] = jnp.concatenate([left, right], axis=1)
        return self.far()

    def cores(self, *deps):
        parts = [self.found[2 * r] for r in range(self.size // 2)]
        if deps:
            parts = lax.optimization_barrier(tuple(parts) + deps)[: len(parts)]
        stack = jnp.stack(parts)
        return [stack, xor_send(stack, self.size, 1)]


def beside(parts):
    return parts[0] if len(parts) == 1 else jnp.concatenate(parts, axis=-1)


class Reduce:
    def __init__(self, grads, size, depth, order=None, rest=None):
        self.size, self.depth = size, depth
        nbits = size.bit_length() - 1
        self.rest = list(range(nbits))[::-1] if rest is None else list(rest)
        self.order = list(range(nbits)) if order is None else list(order)
        self.cur = [
            g.reshape([2] * len(self.rest) + [g.shape[0] // 2 ** len(self.rest), g.shape[1]])
            if g.ndim == 2
            else g
            for g in grads
        ]

    def send(self):
        place = lax.axis_index("seq")
        bit = self.order.pop(0)
        axis = self.rest.index(bit)
        own = (place >> bit) & 1
        self.out = beside([lax.dynamic_index_in_dim(c, 1 - own, axis, False) for c in self.cur])
        self.kept = [lax.dynamic_index_in_dim(c, own, axis, False) for c in self.cur]
        self.flight = xor_send(self.out, self.size, 1 << bit)
        self.rest.pop(axis)
        return self

    def add(self, *deps):
        got = after(self.flight, *deps) if deps else self.flight
        self.cur = [(beside(self.kept).astype(f32) + got.astype(f32)).astype(bf16)]
        return self

    def cut(self, at):
        (cur,) = self.cur
        parts = [
            Reduce([cur[..., :at]], self.size, self.depth, self.order, self.rest),
            Reduce([cur[..., at:]], self.size, self.depth, self.order[::-1], self.rest),
        ]
        return parts

    def send_stream(self):
        while self.order:
            self.send().add()
        depth = self.depth
        level = lax.axis_index("stream")
        cur = beside(self.cur)
        self.out = cur
        cur = cur.reshape(depth, cur.shape[0] // depth, cur.shape[1])
        self.total = lax.dynamic_index_in_dim(cur, level, 0, False).astype(f32)
        self.flights = []
        for d in range(1, depth):
            piece = lax.dynamic_index_in_dim(cur, (level + d) % depth, 0, False)
            self.flights.append(
                lax.ppermute(piece, "stream", [(i, (i + d) % depth) for i in range(depth)])
            )
        return self

    def done(self, *deps):
        total = self.total
        for f in self.flights:
            total = total + (after(f, *deps) if deps else f).astype(f32)
        return total


def lanes(shape):
    return lax.broadcasted_iota(jnp.int32, shape, len(shape) - 1)


def block_ones(width, part):
    r = lax.broadcasted_iota(jnp.int32, (width, width), 0) // part
    c = lax.broadcasted_iota(jnp.int32, (width, width), 1) // part
    return jnp.where(r == c, 1.0, 0.0).astype(bf16)


def fetch_start(stacks, dest, me, sems, col=0, width=None, at=0):
    half = stacks[0].shape[0]
    rows = dest.shape[0] // (2 * half)
    width = width or stacks[0].shape[2]
    copies = []
    for c, ref in enumerate(stacks):
        for r in range(half):
            off = pl.multiple_of((me ^ (2 * r + c)) * rows, 8)
            copy = pltpu.make_async_copy(
                ref.at[r, :, pl.ds(col, width)],
                dest.at[pl.ds(off, rows), pl.ds(at, width)],
                sems.at[2 * r + c],
            )
            copy.start()
            copies.append(copy)
    return copies


def pair_maps(feat_ref, dest, pairs, which):
    width = 128
    lane = lanes((width, width))
    row = lax.broadcasted_iota(jnp.int32, (width, width), 0)
    for p in range(pairs):
        both = feat_ref[pl.ds(p * width, width), :].astype(f32)
        half = width // 2
        other = pltpu.roll(both, half, 1)
        if which == 0:
            signed = jnp.where(lane < half, both, -other)
        else:
            signed = jnp.where(lane < half, other, -both)
        dest[p, :, pl.ds(0, width)] = jnp.where(row < half, signed, 0.0).astype(bf16)
        dest[p, :, pl.ds(width, width)] = jnp.where(row >= half, signed, 0.0).astype(bf16)


def features(logits_of, ones):
    halves = [one[:, j * 128 : (j + 1) * 128] for one in logits_of for j in range(2)]
    low = lanes(halves[0].shape) < 64
    tops = [
        (
            jnp.max(jnp.where(low, one, -jnp.inf), axis=1, keepdims=True),
            jnp.max(jnp.where(low, -jnp.inf, one), axis=1, keepdims=True),
        )
        for one in halves
    ]
    exps = [jnp.exp(one - jnp.where(low, *top)) for one, top in zip(halves, tops)]
    exps = [jnp.concatenate(exps[2 * i : 2 * i + 2], axis=1) for i in range(len(logits_of))]
    sums = [mm(e.astype(bf16), ones) for e in exps]
    return [(e / t).astype(bf16) for e, t in zip(exps, sums)]


def augmented(two):
    low = lanes(two.shape) < 64
    one = jnp.ones_like(two)
    return jnp.where(low, two, one), jnp.where(low, one, two)


def pack_states(get, dest, pairs, zsum):
    shape = (128, 128)
    lane = lanes(shape)
    low = lane < 64
    zt = jnp.zeros(shape, f32)
    for p in range(pairs):
        a, b = get(2 * p), get(2 * p + 1)
        dest[p] = jnp.where(low, a, b).astype(bf16)
        if zsum:
            za = jnp.sum(jnp.where(low, 0.0, a), axis=1, keepdims=True)
            zb = jnp.sum(jnp.where(low, b, 0.0), axis=1, keepdims=True)
        else:
            za, zb = a, b
        zt = jnp.where(lane == 64 + 2 * p, za, zt)
        zt = jnp.where(lane == 2 * p + 1, zb, zt)
    dest[pairs] = zt.astype(bf16)


def unpack_states(me, keep_ref, blocks, put, base, count, pairs, back):
    shape = (128, 128)
    lane = lanes(shape)
    low = lane < 64
    size = 2 * blocks.shape[1]
    coefs = [None]
    for r in range(1, size):
        j = me ^ r
        c = jnp.where(j > me if back else j < me, 1.0, 0.0)
        for i in range(size):
            between = ((i > me) & (i < j)) if back else ((i > j) & (i < me))
            c = c * jnp.where(between, keep_ref[i], 1.0)
        coefs.append(c)

    def total(i):
        acc = jnp.zeros(shape, f32)
        for r in range(1, size):
            acc = acc + coefs[r] * blocks[r % 2, r // 2, i].astype(f32)
        return acc

    zt = total(pairs)
    for q in range(count):
        p = base + q
        two = total(p)
        za = jnp.sum(jnp.where(lane == 64 + 2 * p, zt, 0.0), axis=1, keepdims=True)
        zb = jnp.sum(jnp.where(lane == 2 * p + 1, zt, 0.0), axis=1, keepdims=True)
        if back:
            put(2 * q, jnp.where(low, two, jnp.where(lane == 64, za, 0.0)))
            put(2 * q + 1, jnp.where(low, jnp.where(lane == 0, zb, 0.0), two))
        else:
            put(2 * q, jnp.where(low, two, za))
            put(2 * q + 1, jnp.where(low, zb, two))


def normed(values, gain, bias):
    mean = jnp.mean(values, axis=1, keepdims=True)
    cent = values - mean
    rstd = lax.rsqrt(jnp.mean(cent * cent, axis=1, keepdims=True) + epsilon)
    hat = cent * rstd
    return hat * gain + bias, hat, rstd


def normed_back(grad, hat, rstd, gain):
    dhat = grad * gain
    return rstd * (
        dhat
        - jnp.mean(dhat, axis=1, keepdims=True)
        - hat * jnp.mean(dhat * hat, axis=1, keepdims=True)
    )


def keys_body(n_seq, pairs, me_ref, cend_ref, x_ref, cnt_ref, *refs):
    width = x_ref.shape[1]
    wl = refs[:2]
    (h_ref, k_ref, v_ref, phi_ref, st_ref, gb_ref, feat_ref, w1, maps, state, sems) = refs[2:]
    step = pl.program_id(0)

    @pl.when(step == 0)
    def _():
        me = me_ref[0]
        copies = fetch_start(wl, w1, me, sems.at[0], width, 2 * width + 256)
        for c in copies:
            c.wait()
        gb_ref[...] = w1[:, pl.ds(2 * width + 128, 128)].astype(f32).T[:8]
        feat_ref[...] = w1[:, pl.ds(2 * width, 128)]
        pair_maps(feat_ref, maps, pairs, 1)
        state[...] = jnp.zeros_like(state)

    gb = gb_ref[...]
    out, _, _ = normed(x_ref[...].astype(f32), gb[0:1], gb[2:3])
    h1 = out.astype(bf16)
    h_ref[...] = h1
    keys = mm(h1, w1[:, pl.ds(0, width)]).astype(bf16)
    vals = mm(h1, w1[:, pl.ds(width, width)]).astype(bf16)
    k_ref[...] = keys
    v_ref[...] = vals
    ones = block_ones(256, 64)
    last = cend_ref[cend_ref.shape[0] - 1]
    used = jnp.where(cnt_ref[...] == last, 1.0, 0.0).astype(bf16)
    for g in range(0, pairs, GF):
        group = range(g, min(g + GF, pairs))
        phis = features([mm(keys[:, p * 128 : (p + 1) * 128], maps[p]) for p in group], ones)
        for p, phi in zip(group, phis):
            phi_ref[:, pl.ds(p * 256, 256)] = phi
            va, vb = augmented(vals[:, p * 128 : (p + 1) * 128])
            state[2 * p] += mm_f(phi[:, :128], va * used)
            state[2 * p + 1] += mm_f(phi[:, 128:], vb * used)

    @pl.when(step == pl.num_programs(0) - 1)
    def _():
        pack_states(lambda h: state[h], st_ref, pairs, False)


def local_body(base, pairs, me_ref, cend_ref, h_ref, phik_ref, v_ref, cnt_ref, row_ref, feat_ref, *refs):
    wq = refs[:2]
    (q_ref, phiq_ref, num_ref, den_ref, srel_ref, state, w1, maps, sems) = refs[-9:]
    step = pl.program_id(0)
    width = h_ref.shape[1]

    @pl.when(step == 0)
    def _():
        copies = fetch_start(wq, w1, me_ref[0], sems, 0, width)
        pair_maps(feat_ref, maps, pairs, 0)
        if base:
            state[...] = refs[2][...]
        else:
            state[...] = jnp.zeros_like(state)
        for c in copies:
            c.wait()

    queries = mm(h_ref[...], w1[...]).astype(bf16)
    q_ref[...] = queries
    ones = block_ones(256, 64)
    size = h_ref.shape[0]
    cnt = cnt_ref[...]
    first, last = cend_ref[base + step], cend_ref[base + step + 1]
    row_id = lax.broadcasted_iota(jnp.int32, (size, size), 0)
    mask = (row_id >= lanes((size, size))) & (cnt == row_ref[...])
    before = jnp.where(cnt == first, 1.0, 0.0)
    after = jnp.where(cnt == last, 1.0, 0.0).astype(bf16)
    keep = jnp.where(first == last, 1.0, 0.0)
    low = lanes((size, 128)) < 64
    for g in range(0, pairs, GF):
        group = range(g, min(g + GF, pairs))
        phis = features([mm(queries[:, p * 128 : (p + 1) * 128], maps[p]) for p in group], ones)
        for p, phi in zip(group, phis):
            phiq_ref[:, pl.ds(p * 256, 256)] = phi
        pqs = [phi[:, j * 128 : (j + 1) * 128] for phi in phis for j in range(2)]
        heads = [2 * p + j for p in group for j in range(2)]
        pks = [phik_ref[:, pl.ds(h * 128, 128)] for h in heads]
        scores = [jnp.where(mask, mm_t(pq, pk), 0.0).astype(bf16) for pq, pk in zip(pqs, pks)]
        val_of = [v for p in group for v in augmented(v_ref[:, p * 128 : (p + 1) * 128])]
        res = []
        for h, pq, pk, sc, val in zip(heads, pqs, pks, scores, val_of):
            st = state[h]
            st_b = st.astype(bf16)
            srel_ref[0, h] = st_b
            res.append(mm(sc, val) + before * mm(pq, st_b))
            state[h] = keep * st + mm_f(pk, val * after)
        for i, p in enumerate(group):
            two = pl.ds(p * 128, 128)
            num_ref[:, two] = jnp.where(low, res[2 * i], res[2 * i + 1])
            den_ref[:, two] = pltpu.roll(jnp.where(low, res[2 * i + 1], res[2 * i]), 64, 1)


def middle_body(
    n_seq, pairs, me_ref, keep_ref, x_ref, dy_ref, num_ref, den_ref, phiq_ref, cnt_ref, gb_ref, *refs
):
    width = x_ref.shape[1]
    wf, wp, sts = (refs[2 * i : 2 * i + 2] for i in range(3))
    (
        y_ref, o_ref, h_ref, a_ref, df_ref, dat_ref, dr_ref, dd_ref, sin_ref, gst_ref, sum_ref,
        w_out, w_fc, w_proj, rden, state, stv, sems,
    ) = refs[6:]
    step = pl.program_id(0)
    chunk = 768
    hidden = w_fc.shape[1]
    size = x_ref.shape[0]

    @pl.when(step == 0)
    def _():
        me = me_ref[0]
        st_copies = []
        for c in range(2):
            st_copies.append(pltpu.make_async_copy(sts[c], stv.at[c], sems.at[3, c]))
            st_copies[c].start()
        copies = fetch_start(wf, w_out, me, sems.at[0], hidden, width)
        copies += fetch_start(wf, w_fc, me, sems.at[1], 0, hidden)
        copies += fetch_start(wp, w_proj, me, sems.at[2])
        for c in st_copies:
            c.wait()

        def put(h, value):
            sin_ref[h] = value.astype(bf16)

        unpack_states(me, keep_ref, stv, put, 0, pairs, pairs, False)
        state[...] = jnp.zeros_like(state)
        sum_ref[...] = jnp.zeros_like(sum_ref)
        for c in copies:
            c.wait()

    gb = gb_ref[...]
    low = lanes((size, 128)) < 64
    start = jnp.where(cnt_ref[...] == 0.0, 1.0, 0.0)
    start_b = start.astype(bf16)
    res = [mm(phiq_ref[:, pl.ds(h * 128, 128)], sin_ref[h]) for h in range(2 * pairs)]
    for p in range(pairs):
        two = pl.ds(p * 128, 128)
        ra, rb = res[2 * p], res[2 * p + 1]
        num = num_ref[:, two] + start * jnp.where(low, ra, rb)
        den = den_ref[:, two] + start * pltpu.roll(jnp.where(low, rb, ra), 64, 1)
        inv = 1.0 / den
        rden[:, two] = inv
        o_ref[:, two] = (num * inv).astype(bf16)
    x = x_ref[...].astype(f32)
    attn = mm(o_ref[...], w_out[...])
    mid = x + attn
    out, hat, rstd = normed(mid, gb[1:2], gb[3:4])
    h2 = out.astype(bf16)
    h_ref[...] = h2
    dy_b = dy_ref[...]
    branch = jnp.zeros((size, width), f32)
    dh2 = jnp.zeros((size, width), f32)
    for c in range(w_fc.shape[1] // chunk):
        cols = pl.ds(c * chunk, chunk)
        fc = mm(h2, w_fc[:, cols])
        square = fc * fc
        tan = jnp.tanh(fc * (GC + GC * GA * square))
        half = 0.5 + 0.5 * tan
        act = (fc * half).astype(bf16)
        a_ref[:, cols] = act
        branch = branch + mm(act, w_proj[cols, :])
        slope = half + fc * (1.0 - half) * half * (2.0 * GC + 6.0 * GC * GA * square)
        dfc = (mm_t(dy_b, w_proj[cols, :]) * slope).astype(bf16)
        df_ref[:, cols] = dfc
        dh2 = dh2 + mm_t(dfc, w_fc[:, cols])
    y = mid + branch
    y_ref[...] = y.astype(bf16)
    sum_ref[0:1] += jnp.sum(attn * attn, axis=0, keepdims=True)
    sum_ref[1:2] += jnp.sum(branch * branch, axis=0, keepdims=True)
    sum_ref[2:3] += jnp.sum(y * y, axis=0, keepdims=True)
    sum_ref[3:4] += jnp.sum(dh2 * hat, axis=0, keepdims=True)
    sum_ref[4:5] += jnp.sum(dh2, axis=0, keepdims=True)
    dr = dy_b.astype(f32) + normed_back(dh2, hat, rstd, gb[1:2])
    dr_ref[...] = dr
    dat = dr.astype(bf16)
    dat_ref[...] = dat
    d_o = mm_t(dat, w_out[...])
    ones = block_ones(256, 64)
    lane = lanes((size, 128))
    quads = range(pairs // 2)
    fours = [pl.ds(q * 256, 256) for q in quads]
    d_os = [d_o[:, q * 256 : (q + 1) * 256] for q in quads]
    prods = [d * o_ref[:, c].astype(f32) for d, c in zip(d_os, fours)]
    his = [a.astype(bf16) for a in prods]
    los = [(a - hi.astype(f32)).astype(bf16) for a, hi in zip(prods, his)]
    ddens = [-(mm(hi, ones) + mm(lo, ones)) * rden[:, c] for hi, lo, c in zip(his, los, fours)]
    dnums = [(d * rden[:, c]).astype(bf16) for d, c in zip(d_os, fours)]
    near = lane & 63
    for p in range(pairs):
        sub = slice((p % 2) * 128, (p % 2 + 1) * 128)
        dd = pltpu.roll(ddens[p // 2][:, sub], 64, 1)
        dhi = dd.astype(bf16)
        dlo = (dd - dhi.astype(f32)).astype(bf16)
        aux = jnp.where(near == 0, dhi.astype(f32), jnp.where(near == 1, dlo.astype(f32), 0.0)).astype(bf16)
        dn = dnums[p // 2][:, sub]
        dd_ref[:, pl.ds(p * 256, 128)] = jnp.where(low, dn, aux)
        dd_ref[:, pl.ds(p * 256 + 128, 128)] = jnp.where(low, aux, dn)
    for h in range(2 * pairs):
        own = pl.ds(h * 128, 128)
        state[h] += mm_f(phiq_ref[:, own], dd_ref[:, own] * start_b)

    @pl.when(step == pl.num_programs(0) - 1)
    def _():
        pack_states(lambda h: state[h], gst_ref, pairs, True)
        total = jnp.sum(sum_ref[...], axis=1, keepdims=True)
        high = total.astype(bf16).astype(f32)
        place = lanes((8, 128))
        tile = jnp.where(place == 126, high, jnp.where(place == 127, total - high, 0.0))
        tile = jnp.concatenate([tile, jnp.zeros_like(tile)], axis=0)
        top = gst_ref[pairs, pl.ds(0, 16), :].astype(f32)
        gst_ref[pairs, pl.ds(0, 16), :] = (top + tile).astype(bf16)


def back_body(
    base, pairs, all_pairs, me_ref, keep_ref, cend_ref, q_ref, k_ref, v_ref, phiq_ref, phik_ref, dd_ref, srel_ref, sin_ref,
    cnt_ref, row_ref, feat_ref, *refs
):
    sts = refs[:2]
    (dqkv_ref, gfeat_ref, mapq, mapk, state, gq, gk, stv, sems) = refs[2:]
    step = pl.program_id(0)
    nblk = pl.num_programs(0)
    here = nblk - 1 - step

    @pl.when(step == 0)
    def _():
        copies = []
        for c in range(2):
            copies.append(pltpu.make_async_copy(sts[c], stv.at[c], sems.at[c]))
            copies[c].start()
        pair_maps(feat_ref, mapq, pairs, 0)
        pair_maps(feat_ref, mapk, pairs, 1)
        gq[...] = jnp.zeros_like(gq)
        gk[...] = jnp.zeros_like(gk)
        for c in copies:
            c.wait()

        def put(h, value):
            state[h] = value

        unpack_states(me_ref[0], keep_ref, stv, put, base, pairs, all_pairs, True)

    size = q_ref.shape[0]
    width = q_ref.shape[1]
    cnt = cnt_ref[...]
    first, last = cend_ref[here], cend_ref[here + 1]
    row_id = lax.broadcasted_iota(jnp.int32, (size, size), 0)
    col_id = lanes((size, size))
    same = cnt == row_ref[...]
    mask = (row_id >= col_id) & same
    mask_t = (col_id >= row_id) & same
    before = jnp.where(cnt == first, 1.0, 0.0).astype(bf16)
    after = jnp.where(cnt == last, 1.0, 0.0).astype(bf16)
    keep = jnp.where(first == last, 1.0, 0.0)
    opened = jnp.where(first == 0.0, 1.0, 0.0)
    ones = block_ones(256, 64)
    low = lanes((size, 128)) < 64
    heads = range(2 * pairs)
    cols = [pl.ds(h * 128, 128) for h in heads]
    vals = [v for p in range(pairs) for v in augmented(v_ref[:, pl.ds(p * 128, 128)])]
    scores_t = [
        jnp.where(mask_t, mm_t(phik_ref[:, c], phiq_ref[:, c]), 0.0).astype(bf16) for c in cols
    ]
    dsc = [jnp.where(mask, mm_t(dd_ref[:, c], v), 0.0).astype(bf16) for c, v in zip(cols, vals)]
    dsc_t = [jnp.where(mask_t, mm_t(v, dd_ref[:, c]), 0.0).astype(bf16) for c, v in zip(cols, vals)]
    sts = [
        (srel_ref[0, h].astype(f32) + opened * sin_ref[h].astype(f32)).astype(bf16) for h in heads
    ]
    dsts = [state[h].astype(bf16) for h in heads]
    ddws = [dd_ref[:, c] * before for c in cols]
    dphi_q = [mm(dsc[h], phik_ref[:, cols[h]]) + mm_t(ddws[h], sts[h]) for h in heads]
    dphi_k = [mm(dsc_t[h], phiq_ref[:, cols[h]]) + mm_t(vals[h] * after, dsts[h]) for h in heads]
    dvs = [mm(scores_t[h], dd_ref[:, cols[h]]) + mm(phik_ref[:, cols[h]] * after, dsts[h]) for h in heads]
    for h in heads:
        state[h] = keep * state[h] + mm_f(phiq_ref[:, cols[h]], ddws[h])
    for p in range(pairs):
        dqkv_ref[:, pl.ds(2 * width + p * 128, 128)] = jnp.where(low, dvs[2 * p], dvs[2 * p + 1]).astype(bf16)
    for phi_ref, dphi, rows_ref, maps, acc, base_col in (
        (phiq_ref, dphi_q, q_ref, mapq, gq, 0),
        (phik_ref, dphi_k, k_ref, mapk, gk, width),
    ):
        phis = [phi_ref[:, pl.ds(p * 256, 256)].astype(f32) for p in range(pairs)]
        dphis = [jnp.concatenate(dphi[2 * p : 2 * p + 2], axis=1) for p in range(pairs)]
        totals = [mm((phi * d).astype(bf16), ones) for phi, d in zip(phis, dphis)]
        dlogs = [(phi * (d - t)).astype(bf16) for phi, d, t in zip(phis, dphis, totals)]
        for p in range(pairs):
            two = pl.ds(p * 128, 128)
            dqkv_ref[:, pl.ds(base_col + p * 128, 128)] = mm_t(dlogs[p], maps[p]).astype(bf16)
            acc[p] += mm_f(rows_ref[:, two], dlogs[p])

    @pl.when(step == nblk - 1)
    def _():
        lane = lanes((128, 128))
        row = lax.broadcasted_iota(jnp.int32, (128, 128), 0)
        for p in range(pairs):
            outs = []
            for acc in (gq, gk):
                one = jnp.where(row < 64, acc[p, :, :128], acc[p, :, 128:])
                outs.append(one - pltpu.roll(one, 64, 1))
            gfeat_ref[pl.ds(p * 128, 128), :] = jnp.where(lane < 64, outs[0], -outs[1]).astype(bf16)


def enter_body(groups, me_ref, x_ref, dr_ref, gb_ref, *refs):
    width = x_ref.shape[1]
    grads = refs[:groups]
    wl = refs[groups : groups + 2]
    (dx_ref, sum_ref, w1, sems) = refs[groups + 2 :]

    @pl.when(pl.program_id(0) == 0)
    def _():
        me = me_ref[0]
        copies = fetch_start(wl, w1, me, sems.at[0], 0, 3 * width)
        sum_ref[...] = jnp.zeros_like(sum_ref)
        for c in copies:
            c.wait()

    gb = gb_ref[...]
    _, hat, rstd = normed(x_ref[...].astype(f32), gb[0:1], gb[2:3])
    part = width // groups
    dh = jnp.zeros(x_ref.shape, f32)
    for g in range(groups):
        for i in range(3):
            dh = dh + mm_t(grads[g][:, pl.ds(i * part, part)], w1[:, pl.ds(i * width + g * part, part)])
    dx_ref[...] = dr_ref[...] + normed_back(dh, hat, rstd, gb[0:1])
    sum_ref[0:1] += jnp.sum(dh * hat, axis=0, keepdims=True)
    sum_ref[1:2] += jnp.sum(dh, axis=0, keepdims=True)


def whole(*_):
    return pl.BlockSpec(memory_space=pl.ANY)


def smem():
    return pl.BlockSpec(memory_space=pltpu.SMEM)


def rows_spec(size, cols, back=None):
    if back is None:
        return pl.BlockSpec((size, cols), lambda i: (i, 0))
    return pl.BlockSpec((size, cols), lambda i: (back - 1 - i, 0))


def full_spec(shape):
    zeros = (0,) * len(shape)
    return pl.BlockSpec(shape, lambda i: zeros)


def sds(shape, kind):
    return jax.ShapeDtypeStruct(shape, kind)


def cparams():
    return pltpu.CompilerParams(
        dimension_semantics=("arbitrary",), vmem_limit_bytes=58 * 1024 * 1024
    )


def cost(micros):
    return pl.CostEstimate(
        flops=int(micros * 5e8), transcendentals=0, bytes_accessed=int(micros * 1e6)
    )


def dma(*shape):
    return pltpu.SemaphoreType.DMA(shape)


def shards(n_seq, depth, inputs, resets, norm_gains, norm_biases, w_qkv, w_feat, w_out, w_fc, w_proj, cotangent):
    tokens, width = inputs.shape[1], inputs.shape[2]
    hidden = w_fc.shape[1]
    head_dim = w_feat.shape[1] // 2
    heads = width // head_dim
    pairs = heads // 2
    rows = w_qkv.shape[0]
    nblk = tokens // BT
    x, dy = inputs[0], cotangent[0]
    me = lax.axis_index("seq")
    me_arr = me.reshape(1).astype(jnp.int32)

    marks = resets[0].reshape(nblk, BT).astype(bf16)
    flag = jnp.where(jnp.max(resets) == 0, 1.0, 0.0).astype(bf16)
    upper = jnp.triu(jnp.ones((BT, BT), bf16))
    inner = jnp.dot(marks, upper, preferred_element_type=f32)
    ends = jnp.cumsum(inner[:, -1])
    cend = jnp.concatenate([jnp.zeros((1,), f32), ends])
    counts = inner + cend[:-1, None]
    cnt_col = counts.reshape(tokens, 1)
    cnt_row = counts.reshape(1, tokens)

    norms = jnp.concatenate(
        [norm_gains, norm_biases, jnp.broadcast_to(flag, (rows, 1)), jnp.zeros((rows, 123), bf16)],
        axis=1,
    )
    first = stream_rows(stream_send(jnp.concatenate([w_qkv, w_feat, norms], axis=1), depth), depth)
    first = Spread(first, n_seq, False).near()
    up = jnp.concatenate([w_fc, w_out], axis=1)
    first.far_halves()
    up = stream_send(after(up, first.block), depth)
    first_blocks = first.cores()
    up = stream_rows([after(a, first_blocks[0]) for a in up], depth)
    up = Spread(up, n_seq, True).near(first_blocks[0])
    proj_pieces = stream_send(after(w_proj, first_blocks[1], up.block), depth)
    me_first = after(me_arr, up.block)

    packed = (pairs + 1, 128, 128)
    full = (heads, 128, 128)
    h_one, keys, vals, phi_k, state, gb, feat_all = pl.pallas_call(
        functools.partial(keys_body, n_seq, pairs),
        name="keys",
        cost_estimate=cost(22),
        grid=(tokens // TK,),
        in_specs=[smem(), smem(), rows_spec(TK, width), rows_spec(TK, 1)] + [whole()] * 2,
        out_specs=[rows_spec(TK, width)] * 3
        + [rows_spec(TK, 2 * width), full_spec(packed), full_spec((8, width)), full_spec((width, 128))],
        out_shape=[sds((tokens, width), bf16)] * 3
        + [sds((tokens, 2 * width), bf16), sds(packed, bf16), sds((8, width), f32), sds((width, 128), bf16)],
        scratch_shapes=[
            pltpu.VMEM((width, 2 * width + 256), bf16),
            pltpu.VMEM((pairs, 128, 256), bf16),
            pltpu.VMEM(full, f32),
            dma(2, n_seq),
        ],
        compiler_params=cparams(),
    )(me_first, cend, x, cnt_col, *first_blocks)
    level = lax.axis_index("stream")
    flags = gb[4].reshape(n_seq, depth, rows)[:, :, 0]
    keeps = lax.dynamic_index_in_dim(flags, level, 1, False)
    spread = Spread(state, n_seq, False).near_all()
    up.far(gb)
    proj = Spread(stream_rows([after(a, gb) for a in proj_pieces], depth), n_seq, False).near()
    part_blk = nblk // 2
    local = []
    for part in range(2):
        base = part * part_blk

        def here(size, cols):
            return pl.BlockSpec((size, cols), lambda i: (base + i, 0))

        blocks_out = [
            sds((tokens, width), bf16), sds((tokens, 2 * width), bf16), sds((tokens, width), f32),
            sds((tokens, width), f32), sds((nblk,) + full, bf16),
        ]
        if part:
            me_two = after(me_arr, up_blocks[0], *[proj.found[b] for b in proj.bits], *spread.found.values())
        else:
            me_two = after(me_arr, proj.block, state, after(up.found[up.bits[0]], gb))
        local = pl.pallas_call(
            functools.partial(local_body, base, pairs),
            name="local",
            cost_estimate=cost(15),
            grid=(part_blk,),
            in_specs=[
                smem(), smem(), here(BT, width), here(BT, 2 * width), here(BT, width), here(BT, 1),
                pl.BlockSpec((1, BT), lambda i: (0, base + i)), full_spec((width, 128)),
            ]
            + [whole()] * 2
            + ([full_spec(full)] + [whole()] * 5 if part else []),
            out_specs=[
                here(BT, width), here(BT, 2 * width), here(BT, width), here(BT, width),
                pl.BlockSpec((1,) + full, lambda i: (base + i, 0, 0, 0)), full_spec(full),
            ],
            out_shape=blocks_out + [sds(full, f32)],
            scratch_shapes=[
                pltpu.VMEM((width, width), bf16),
                pltpu.VMEM((pairs, 128, 256), bf16),
                dma(n_seq),
            ],
            input_output_aliases={11 + i: i for i in range(5)} if part else {},
            compiler_params=cparams(),
        )(
            me_two, cend, h_one, phi_k, vals, cnt_col, cnt_row, feat_all, *first_blocks,
            *([local[5]] + list(local[:5]) if part else []),
        )
        if part == 0:
            event = local[5]
            proj.far(event)
            up_blocks = up.cores(event)
    queries, phi_q, num, den, srel, event = local
    states = spread.cores(event)
    proj_blocks = proj.cores(event)

    y, att, h_two, act, d_fc, d_att, d_mid, dd, s_in, g_state, sums = pl.pallas_call(
        functools.partial(middle_body, n_seq, pairs),
        name="middle",
        cost_estimate=cost(43),
        grid=(tokens // TM,),
        in_specs=[
            smem(), smem(), rows_spec(TM, width), rows_spec(TM, width), rows_spec(TM, width),
            rows_spec(TM, width), rows_spec(TM, 2 * width), rows_spec(TM, 1), full_spec((8, width)),
        ]
        + [whole()] * 6,
        out_specs=[
            rows_spec(TM, width), rows_spec(TM, width), rows_spec(TM, width), rows_spec(TM, hidden),
            rows_spec(TM, hidden), rows_spec(TM, width), rows_spec(TM, width), rows_spec(TM, 2 * width),
            full_spec(full), full_spec(packed), full_spec((8, width)),
        ],
        out_shape=[
            sds((tokens, width), bf16), sds((tokens, width), bf16), sds((tokens, width), bf16),
            sds((tokens, hidden), bf16), sds((tokens, hidden), bf16), sds((tokens, width), bf16),
            sds((tokens, width), f32), sds((tokens, 2 * width), bf16), sds(full, bf16), sds(packed, bf16),
            sds((8, width), f32),
        ],
        scratch_shapes=[
            pltpu.VMEM((width, width), bf16),
            pltpu.VMEM((width, hidden), bf16),
            pltpu.VMEM((hidden, width), bf16),
            pltpu.VMEM((TM, width), f32),
            pltpu.VMEM(full, f32),
            pltpu.VMEM((2, n_seq // 2) + packed, bf16),
            dma(4, n_seq),
        ],
        compiler_params=cparams(),
    )(
        me_arr, keeps, x, dy, num, den, phi_q, cnt_col, gb,
        *up_blocks, *proj_blocks, *states,
    )

    spread = Spread(g_state, n_seq, True).near_all()
    norm_two = jnp.stack([sums[3], sums[4]], axis=1).astype(bf16)
    norm_two = jnp.concatenate([norm_two, jnp.zeros((width, 126), bf16)], axis=1)
    nbits = n_seq.bit_length() - 1
    g_fc = mm_f(h_two, d_fc).astype(bf16)
    g_out = mm_f(att, d_att).astype(bf16)
    red_fc = Reduce([g_fc, g_out, norm_two], n_seq, depth, [0] + list(range(1, nbits))[::-1]).send()
    g_states = spread.cores(red_fc.out)
    g_proj = mm_f(after(act, red_fc.out, g_states[0]), dy).astype(bf16)
    red_proj = Reduce([g_proj], n_seq, depth).send()
    red_fc.add(red_proj.out).send()
    red_proj.add(red_fc.out).send()
    me_back = after(me_arr, red_proj.out, red_fc.out)
    squares = sum(
        jnp.sum(stack[:, pairs, :3, 126:].astype(f32), axis=(0, 2)) for stack in g_states
    )
    branch_rms = jnp.sqrt(squares / (tokens * n_seq * width)).reshape(1, 3)

    groups = 2
    some = pairs // groups
    part = some * 128
    d_qkv, g_feat = [], []
    for g in range(groups):

        def spec(cols):
            return pl.BlockSpec((BT, cols), lambda i: (nblk - 1 - i, g))

        def one_group(shape):
            return pl.BlockSpec(shape, lambda i: (g,) + (0,) * (len(shape) - 1))

        one = (2 * some, 128, 128)
        d_one, g_one = pl.pallas_call(
            functools.partial(back_body, g * some, some, pairs),
            name="back",
            cost_estimate=cost(19),
            grid=(nblk,),
            in_specs=[
                smem(), smem(), smem(), spec(part), spec(part), spec(part), spec(2 * part), spec(2 * part),
                spec(2 * part), pl.BlockSpec((1,) + one, lambda i: (nblk - 1 - i, g, 0, 0)), one_group(one),
                rows_spec(BT, 1, nblk), pl.BlockSpec((1, BT), lambda i: (0, nblk - 1 - i)),
                one_group((part, 128)),
            ]
            + [whole()] * 2,
            out_specs=[rows_spec(BT, 3 * part, nblk), full_spec((part, 128))],
            out_shape=[sds((tokens, 3 * part), bf16), sds((part, 128), bf16)],
            scratch_shapes=[
                pltpu.VMEM((some, 128, 256), bf16),
                pltpu.VMEM((some, 128, 256), bf16),
                pltpu.VMEM(one, f32),
                pltpu.VMEM((some, 128, 256), f32),
                pltpu.VMEM((some, 128, 256), f32),
                pltpu.VMEM((2, n_seq // 2) + packed, bf16),
                dma(n_seq),
            ],
            compiler_params=cparams(),
        )(
            me_back, keeps, cend, queries, keys, vals, phi_q, phi_k, dd, srel, s_in, cnt_col, cnt_row,
            feat_all, *g_states,
        )
        d_qkv.append(d_one)
        g_feat.append(g_one)
        if g == 0:
            red_proj.add(d_one).send()
            me_back = after(me_arr, red_proj.out)

    last = d_qkv[-1]
    g_qkv = [mm_f(h_one, d).astype(bf16) for d in d_qkv]
    red_two = Reduce(g_qkv + [jnp.concatenate(g_feat, axis=0)], n_seq, depth).send()
    red_fc.add(red_two.out).send()
    red_proj.add(red_fc.out).send_stream()
    me_late = after(me_arr, red_proj.out, red_fc.out)
    dx, sums_one = pl.pallas_call(
        functools.partial(enter_body, groups),
        name="enter",
        cost_estimate=cost(11),
        grid=(tokens // TM,),
        in_specs=[smem(), rows_spec(TM, width), rows_spec(TM, width), full_spec((8, width))]
        + [rows_spec(TM, 3 * part)] * groups
        + [whole()] * 2,
        out_specs=[rows_spec(TM, width), full_spec((8, width))],
        out_shape=[sds((tokens, width), f32), sds((8, width), f32)],
        scratch_shapes=[pltpu.VMEM((width, 3 * width), bf16), dma(2, n_seq)],
        compiler_params=cparams(),
    )(me_late, x, d_mid, gb, *d_qkv, *first_blocks)
    norm_one = jnp.stack([sums_one[0], sums_one[1]], axis=1).astype(bf16)
    norm_one = jnp.concatenate([norm_one, jnp.zeros((width, 126), bf16)], axis=1)
    red_norm = Reduce([norm_one], n_seq, depth).send()
    red_a, red_b = red_two.add(dx).cut((groups * 3 * part + 256) // 2)
    red_a.send()
    red_norm.add(red_a.out)
    red_b.cur = [beside(red_b.cur + red_norm.cur)]
    red_b.send()
    red_fc.add(red_a.out, red_b.out).send_stream()
    grad_proj = red_proj.done(red_fc.out)
    while red_a.order:
        red_a.add().send()
        red_b.add().send()
    tail = Reduce(red_a.add().cur + red_b.add().cur, n_seq, depth, [], []).send_stream()
    grad_up = red_fc.done(tail.out)
    tail = tail.done()
    grads = [tail[:, g * 3 * part : (g + 1) * 3 * part] for g in range(groups)]
    grad_feat = tail[:, groups * 3 * part : groups * 3 * part + 128]
    norm_one = tail[:, groups * 3 * part + 128 :]
    grad_fc = grad_up[:, :hidden]
    grad_out = grad_up[:, hidden:]
    grad_qkv = jnp.concatenate(
        [grads[g][:, i * part : (i + 1) * part] for i in range(3) for g in range(groups)], axis=1
    )
    return (
        y[None],
        dx[None],
        jnp.concatenate([norm_one[:, 0:1], grad_out[:, width : width + 1]], axis=1),
        jnp.concatenate([norm_one[:, 1:2], grad_out[:, width + 1 : width + 2]], axis=1),
        grad_qkv,
        grad_feat,
        grad_out[:, :width],
        grad_fc,
        grad_proj,
        branch_rms,
    )


def solution(mesh):
    both = P(("seq", "stream"), None)
    acts = P("stream", "seq", None)
    placed = (acts, P("stream", "seq"), both, both, both, both, both, both, both, acts)
    return jax.shard_map(
        functools.partial(shards, mesh.shape["seq"], mesh.shape["stream"]),
        mesh=mesh,
        in_specs=placed,
        out_specs=(acts, acts, both, both, both, both, both, both, both, P("stream", None)),
        check_vma=False,
    )
```

```python
import functools

import jax
import jax.numpy as jnp
from jax import lax
from jax.experimental import pallas as pl
from jax.experimental.pallas import tpu as pltpu
from jax.sharding import PartitionSpec as P

BT = 256
GF = 6
TK = 512
TM = 256
epsilon = 1e-05
f32 = jnp.float32
bf16 = jnp.bfloat16
GC = 0.7978845608028654
GA = 0.044715


def mm(a, b):
    return jnp.dot(a, b, preferred_element_type=f32)


def mm_t(a, b):
    return lax.dot_general(a, b, (((1,), (1,)), ((), ())), preferred_element_type=f32)


def mm_f(a, b):
    return lax.dot_general(a, b, (((0,), (0,)), ((), ())), preferred_element_type=f32)


def xor_send(arr, size, mask):
    return lax.ppermute(arr, "seq", [(i, i ^ mask) for i in range(size)])


def after(arr, *deps):
    return lax.optimization_barrier((arr,) + deps)[0]


def stream_send(shard, depth):
    return [shard] + [
        lax.ppermute(shard, "stream", [(i, (i + d) % depth) for i in range(depth)])
        for d in range(1, depth)
    ]


def stream_rows(pieces, depth):
    shard = pieces[0]
    ring = pieces[::-1]
    place = lax.axis_index("stream")
    rows = shard.shape[0]
    both = jnp.concatenate(ring + ring, axis=0)
    return lax.dynamic_slice_in_dim(both, (depth - 1 - place) * rows, depth * rows, 0)


class Spread:
    def __init__(self, block, size, flip):
        self.size = size
        bits = [1 << b for b in range(1, size.bit_length() - 1)]
        self.bits = bits[::-1] if flip else bits
        self.block = block
        self.found = {0: block}

    def near(self, *deps):
        block = after(self.block, *deps) if deps else self.block
        for bit in self.bits:
            self.found[bit] = xor_send(block, self.size, bit)
        return self

    def near_all(self):
        for r in range(2, self.size, 2):
            self.found[r] = xor_send(self.block, self.size, r)
        return self

    def far(self, *deps):
        for bit in self.bits:
            for r in list(self.found):
                if r ^ bit not in self.found and r < 2 * max(self.bits):
                    src = self.found[r]
                    self.found[r ^ bit] = xor_send(after(src, *deps) if deps else src, self.size, bit)
        return self

    def far_halves(self, *deps):
        one, two = self.bits[:2]
        half = self.block.shape[1] // 256 * 128
        srcs = (self.found[one], self.found[two])
        if deps:
            srcs = lax.optimization_barrier(srcs + deps)[:2]
        self.cuts = [srcs[0][:, :half], srcs[1][:, half:]]
        left = xor_send(self.cuts[0], self.size, two)
        right = xor_send(self.cuts[1], self.size, one)
        self.found[one ^ two] = jnp.concatenate([left, right], axis=1)
        return self.far(*deps)

    def cores(self, *deps):
        parts = [self.found[2 * r] for r in range(self.size // 2)]
        if deps:
            parts = lax.optimization_barrier(tuple(parts) + deps)[: len(parts)]
        stack = jnp.stack(parts)
        return [stack, xor_send(stack, self.size, 1)]


def beside(parts):
    return parts[0] if len(parts) == 1 else jnp.concatenate(parts, axis=-1)


class Reduce:
    def __init__(self, grads, size, depth, order=None, rest=None):
        self.size, self.depth = size, depth
        nbits = size.bit_length() - 1
        self.rest = list(range(nbits))[::-1] if rest is None else list(rest)
        self.order = list(range(nbits)) if order is None else list(order)
        self.cur = [
            g.reshape([2] * len(self.rest) + [g.shape[0] // 2 ** len(self.rest), g.shape[1]])
            if g.ndim == 2
            else g
            for g in grads
        ]

    def send(self):
        place = lax.axis_index("seq")
        bit = self.order.pop(0)
        axis = self.rest.index(bit)
        own = (place >> bit) & 1
        self.out = beside([lax.dynamic_index_in_dim(c, 1 - own, axis, False) for c in self.cur])
        self.kept = [lax.dynamic_index_in_dim(c, own, axis, False) for c in self.cur]
        self.flight = xor_send(self.out, self.size, 1 << bit)
        self.rest.pop(axis)
        return self

    def add(self, *deps):
        got = after(self.flight, *deps) if deps else self.flight
        self.cur = [(beside(self.kept).astype(f32) + got.astype(f32)).astype(bf16)]
        return self

    def cut(self, at):
        (cur,) = self.cur
        parts = [
            Reduce([cur[..., :at]], self.size, self.depth, self.order, self.rest),
            Reduce([cur[..., at:]], self.size, self.depth, self.order[::-1], self.rest),
        ]
        return parts

    def send_stream(self):
        while self.order:
            self.send().add()
        depth = self.depth
        level = lax.axis_index("stream")
        cur = beside(self.cur)
        self.out = cur
        cur = cur.reshape(depth, cur.shape[0] // depth, cur.shape[1])
        self.total = lax.dynamic_index_in_dim(cur, level, 0, False).astype(f32)
        self.flights = []
        for d in range(1, depth):
            piece = lax.dynamic_index_in_dim(cur, (level + d) % depth, 0, False)
            self.flights.append(
                lax.ppermute(piece, "stream", [(i, (i + d) % depth) for i in range(depth)])
            )
        return self

    def done(self, *deps):
        total = self.total
        for f in self.flights:
            total = total + (after(f, *deps) if deps else f).astype(f32)
        return total


def lanes(shape):
    return lax.broadcasted_iota(jnp.int32, shape, len(shape) - 1)


def block_ones(width, part):
    r = lax.broadcasted_iota(jnp.int32, (width, width), 0) // part
    c = lax.broadcasted_iota(jnp.int32, (width, width), 1) // part
    return jnp.where(r == c, 1.0, 0.0).astype(bf16)


def fetch_start(stacks, dest, me, sems, col=0, width=None, at=0):
    half = stacks[0].shape[0]
    rows = dest.shape[0] // (2 * half)
    width = width or stacks[0].shape[2]
    copies = []
    for c, ref in enumerate(stacks):
        for r in range(half):
            off = pl.multiple_of((me ^ (2 * r + c)) * rows, 8)
            copy = pltpu.make_async_copy(
                ref.at[r, :, pl.ds(col, width)],
                dest.at[pl.ds(off, rows), pl.ds(at, width)],
                sems.at[2 * r + c],
            )
            copy.start()
            copies.append(copy)
    return copies


def pair_maps(feat_ref, dest, pairs, which):
    width = 128
    lane = lanes((width, width))
    row = lax.broadcasted_iota(jnp.int32, (width, width), 0)
    for p in range(pairs):
        both = feat_ref[pl.ds(p * width, width), :].astype(f32)
        half = width // 2
        other = pltpu.roll(both, half, 1)
        if which == 0:
            signed = jnp.where(lane < half, both, -other)
        else:
            signed = jnp.where(lane < half, other, -both)
        dest[p, :, pl.ds(0, width)] = jnp.where(row < half, signed, 0.0).astype(bf16)
        dest[p, :, pl.ds(width, width)] = jnp.where(row >= half, signed, 0.0).astype(bf16)


def features(logits_of, ones):
    halves = [one[:, j * 128 : (j + 1) * 128] for one in logits_of for j in range(2)]
    low = lanes(halves[0].shape) < 64
    tops = [
        (
            jnp.max(jnp.where(low, one, -jnp.inf), axis=1, keepdims=True),
            jnp.max(jnp.where(low, -jnp.inf, one), axis=1, keepdims=True),
        )
        for one in halves
    ]
    exps = [jnp.exp(one - jnp.where(low, *top)) for one, top in zip(halves, tops)]
    exps = [jnp.concatenate(exps[2 * i : 2 * i + 2], axis=1) for i in range(len(logits_of))]
    sums = [mm(e.astype(bf16), ones) for e in exps]
    return [(e / t).astype(bf16) for e, t in zip(exps, sums)]


def augmented(two):
    low = lanes(two.shape) < 64
    one = jnp.ones_like(two)
    return jnp.where(low, two, one), jnp.where(low, one, two)


def pack_states(get, dest, pairs, zsum):
    shape = (128, 128)
    lane = lanes(shape)
    low = lane < 64
    zt = jnp.zeros(shape, f32)
    for p in range(pairs):
        a, b = get(2 * p), get(2 * p + 1)
        dest[p] = jnp.where(low, a, b).astype(bf16)
        if zsum:
            za = jnp.sum(jnp.where(low, 0.0, a), axis=1, keepdims=True)
            zb = jnp.sum(jnp.where(low, b, 0.0), axis=1, keepdims=True)
        else:
            za, zb = a, b
        zt = jnp.where(lane == 64 + 2 * p, za, zt)
        zt = jnp.where(lane == 2 * p + 1, zb, zt)
    dest[pairs] = zt.astype(bf16)


def unpack_states(me, keep_ref, blocks, put, base, count, pairs, back):
    shape = (128, 128)
    lane = lanes(shape)
    low = lane < 64
    size = 2 * blocks.shape[1]
    coefs = [None]
    for r in range(1, size):
        j = me ^ r
        c = jnp.where(j > me if back else j < me, 1.0, 0.0)
        for i in range(size):
            between = ((i > me) & (i < j)) if back else ((i > j) & (i < me))
            c = c * jnp.where(between, keep_ref[i], 1.0)
        coefs.append(c)

    def total(i):
        acc = jnp.zeros(shape, f32)
        for r in range(1, size):
            acc = acc + coefs[r] * blocks[r % 2, r // 2, i].astype(f32)
        return acc

    zt = total(pairs)
    for q in range(count):
        p = base + q
        two = total(p)
        za = jnp.sum(jnp.where(lane == 64 + 2 * p, zt, 0.0), axis=1, keepdims=True)
        zb = jnp.sum(jnp.where(lane == 2 * p + 1, zt, 0.0), axis=1, keepdims=True)
        if back:
            put(2 * q, jnp.where(low, two, jnp.where(lane == 64, za, 0.0)))
            put(2 * q + 1, jnp.where(low, jnp.where(lane == 0, zb, 0.0), two))
        else:
            put(2 * q, jnp.where(low, two, za))
            put(2 * q + 1, jnp.where(low, zb, two))


def normed(values, gain, bias):
    mean = jnp.mean(values, axis=1, keepdims=True)
    cent = values - mean
    rstd = lax.rsqrt(jnp.mean(cent * cent, axis=1, keepdims=True) + epsilon)
    hat = cent * rstd
    return hat * gain + bias, hat, rstd


def normed_back(grad, hat, rstd, gain):
    dhat = grad * gain
    return rstd * (
        dhat
        - jnp.mean(dhat, axis=1, keepdims=True)
        - hat * jnp.mean(dhat * hat, axis=1, keepdims=True)
    )


def keys_body(n_seq, pairs, me_ref, cend_ref, x_ref, cnt_ref, *refs):
    width = x_ref.shape[1]
    wl = refs[:2]
    (h_ref, k_ref, v_ref, phi_ref, st_ref, gb_ref, feat_ref, w1, maps, state, sems) = refs[2:]
    step = pl.program_id(0)

    @pl.when(step == 0)
    def _():
        me = me_ref[0]
        copies = fetch_start(wl, w1, me, sems.at[0], width, 2 * width + 256)
        for c in copies:
            c.wait()
        gb_ref[...] = w1[:, pl.ds(2 * width + 128, 128)].astype(f32).T[:8]
        feat_ref[...] = w1[:, pl.ds(2 * width, 128)]
        pair_maps(feat_ref, maps, pairs, 1)
        state[...] = jnp.zeros_like(state)

    gb = gb_ref[...]
    out, _, _ = normed(x_ref[...].astype(f32), gb[0:1], gb[2:3])
    h1 = out.astype(bf16)
    h_ref[...] = h1
    keys = mm(h1, w1[:, pl.ds(0, width)]).astype(bf16)
    vals = mm(h1, w1[:, pl.ds(width, width)]).astype(bf16)
    k_ref[...] = keys
    v_ref[...] = vals
    ones = block_ones(256, 64)
    last = cend_ref[cend_ref.shape[0] - 1]
    used = jnp.where(cnt_ref[...] == last, 1.0, 0.0).astype(bf16)
    for g in range(0, pairs, GF):
        group = range(g, min(g + GF, pairs))
        phis = features([mm(keys[:, p * 128 : (p + 1) * 128], maps[p]) for p in group], ones)
        for p, phi in zip(group, phis):
            phi_ref[:, pl.ds(p * 256, 256)] = phi
            va, vb = augmented(vals[:, p * 128 : (p + 1) * 128])
            state[2 * p] += mm_f(phi[:, :128], va * used)
            state[2 * p + 1] += mm_f(phi[:, 128:], vb * used)

    @pl.when(step == pl.num_programs(0) - 1)
    def _():
        pack_states(lambda h: state[h], st_ref, pairs, False)


def local_body(base, pairs, me_ref, cend_ref, h_ref, phik_ref, v_ref, cnt_ref, row_ref, feat_ref, *refs):
    wq = refs[:2]
    (q_ref, phiq_ref, num_ref, den_ref, srel_ref, state, w1, maps, sems) = refs[-9:]
    step = pl.program_id(0)
    width = h_ref.shape[1]

    @pl.when(step == 0)
    def _():
        copies = fetch_start(wq, w1, me_ref[0], sems, 0, width)
        pair_maps(feat_ref, maps, pairs, 0)
        if base:
            state[...] = refs[2][...]
        else:
            state[...] = jnp.zeros_like(state)
        for c in copies:
            c.wait()

    queries = mm(h_ref[...], w1[...]).astype(bf16)
    q_ref[...] = queries
    ones = block_ones(256, 64)
    size = h_ref.shape[0]
    cnt = cnt_ref[...]
    first, last = cend_ref[base + step], cend_ref[base + step + 1]
    row_id = lax.broadcasted_iota(jnp.int32, (size, size), 0)
    mask = (row_id >= lanes((size, size))) & (cnt == row_ref[...])
    before = jnp.where(cnt == first, 1.0, 0.0)
    after = jnp.where(cnt == last, 1.0, 0.0).astype(bf16)
    keep = jnp.where(first == last, 1.0, 0.0)
    low = lanes((size, 128)) < 64
    for g in range(0, pairs, GF):
        group = range(g, min(g + GF, pairs))
        phis = features([mm(queries[:, p * 128 : (p + 1) * 128], maps[p]) for p in group], ones)
        for p, phi in zip(group, phis):
            phiq_ref[:, pl.ds(p * 256, 256)] = phi
        pqs = [phi[:, j * 128 : (j + 1) * 128] for phi in phis for j in range(2)]
        heads = [2 * p + j for p in group for j in range(2)]
        pks = [phik_ref[:, pl.ds(h * 128, 128)] for h in heads]
        scores = [jnp.where(mask, mm_t(pq, pk), 0.0).astype(bf16) for pq, pk in zip(pqs, pks)]
        val_of = [v for p in group for v in augmented(v_ref[:, p * 128 : (p + 1) * 128])]
        res = []
        for h, pq, pk, sc, val in zip(heads, pqs, pks, scores, val_of):
            st = state[h]
            st_b = st.astype(bf16)
            srel_ref[0, h] = st_b
            res.append(mm(sc, val) + before * mm(pq, st_b))
            state[h] = keep * st + mm_f(pk, val * after)
        for i, p in enumerate(group):
            two = pl.ds(p * 128, 128)
            num_ref[:, two] = jnp.where(low, res[2 * i], res[2 * i + 1])
            den_ref[:, two] = pltpu.roll(jnp.where(low, res[2 * i + 1], res[2 * i]), 64, 1)


def middle_body(
    n_seq, pairs, me_ref, keep_ref, x_ref, dy_ref, num_ref, den_ref, phiq_ref, cnt_ref, gb_ref, *refs
):
    width = x_ref.shape[1]
    wf, wp, sts = (refs[2 * i : 2 * i + 2] for i in range(3))
    (
        y_ref, o_ref, h_ref, a_ref, df_ref, dat_ref, dr_ref, dd_ref, sin_ref, gst_ref, sum_ref,
        w_out, w_fc, w_proj, rden, state, stv, sems,
    ) = refs[6:]
    step = pl.program_id(0)
    chunk = 768
    hidden = w_fc.shape[1]
    size = x_ref.shape[0]

    @pl.when(step == 0)
    def _():
        me = me_ref[0]
        st_copies = []
        for c in range(2):
            st_copies.append(pltpu.make_async_copy(sts[c], stv.at[c], sems.at[3, c]))
            st_copies[c].start()
        copies = fetch_start(wf, w_out, me, sems.at[0], hidden, width)
        copies += fetch_start(wf, w_fc, me, sems.at[1], 0, hidden)
        copies += fetch_start(wp, w_proj, me, sems.at[2])
        for c in st_copies:
            c.wait()

        def put(h, value):
            sin_ref[h] = value.astype(bf16)

        unpack_states(me, keep_ref, stv, put, 0, pairs, pairs, False)
        state[...] = jnp.zeros_like(state)
        sum_ref[...] = jnp.zeros_like(sum_ref)
        for c in copies:
            c.wait()

    gb = gb_ref[...]
    low = lanes((size, 128)) < 64
    start = jnp.where(cnt_ref[...] == 0.0, 1.0, 0.0)
    start_b = start.astype(bf16)
    res = [mm(phiq_ref[:, pl.ds(h * 128, 128)], sin_ref[h]) for h in range(2 * pairs)]
    for p in range(pairs):
        two = pl.ds(p * 128, 128)
        ra, rb = res[2 * p], res[2 * p + 1]
        num = num_ref[:, two] + start * jnp.where(low, ra, rb)
        den = den_ref[:, two] + start * pltpu.roll(jnp.where(low, rb, ra), 64, 1)
        inv = 1.0 / den
        rden[:, two] = inv
        o_ref[:, two] = (num * inv).astype(bf16)
    x = x_ref[...].astype(f32)
    attn = mm(o_ref[...], w_out[...])
    mid = x + attn
    out, hat, rstd = normed(mid, gb[1:2], gb[3:4])
    h2 = out.astype(bf16)
    h_ref[...] = h2
    dy_b = dy_ref[...]
    branch = jnp.zeros((size, width), f32)
    dh2 = jnp.zeros((size, width), f32)
    for c in range(w_fc.shape[1] // chunk):
        cols = pl.ds(c * chunk, chunk)
        fc = mm(h2, w_fc[:, cols])
        square = fc * fc
        tan = jnp.tanh(fc * (GC + GC * GA * square))
        half = 0.5 + 0.5 * tan
        act = (fc * half).astype(bf16)
        a_ref[:, cols] = act
        branch = branch + mm(act, w_proj[cols, :])
        slope = half + fc * (1.0 - half) * half * (2.0 * GC + 6.0 * GC * GA * square)
        dfc = (mm_t(dy_b, w_proj[cols, :]) * slope).astype(bf16)
        df_ref[:, cols] = dfc
        dh2 = dh2 + mm_t(dfc, w_fc[:, cols])
    y = mid + branch
    y_ref[...] = y.astype(bf16)
    sum_ref[0:1] += jnp.sum(attn * attn, axis=0, keepdims=True)
    sum_ref[1:2] += jnp.sum(branch * branch, axis=0, keepdims=True)
    sum_ref[2:3] += jnp.sum(y * y, axis=0, keepdims=True)
    sum_ref[3:4] += jnp.sum(dh2 * hat, axis=0, keepdims=True)
    sum_ref[4:5] += jnp.sum(dh2, axis=0, keepdims=True)
    dr = dy_b.astype(f32) + normed_back(dh2, hat, rstd, gb[1:2])
    dr_ref[...] = dr
    dat = dr.astype(bf16)
    dat_ref[...] = dat
    d_o = mm_t(dat, w_out[...])
    ones = block_ones(256, 64)
    lane = lanes((size, 128))
    quads = range(pairs // 2)
    fours = [pl.ds(q * 256, 256) for q in quads]
    d_os = [d_o[:, q * 256 : (q + 1) * 256] for q in quads]
    prods = [d * o_ref[:, c].astype(f32) for d, c in zip(d_os, fours)]
    his = [a.astype(bf16) for a in prods]
    los = [(a - hi.astype(f32)).astype(bf16) for a, hi in zip(prods, his)]
    ddens = [-(mm(hi, ones) + mm(lo, ones)) * rden[:, c] for hi, lo, c in zip(his, los, fours)]
    dnums = [(d * rden[:, c]).astype(bf16) for d, c in zip(d_os, fours)]
    near = lane & 63
    for p in range(pairs):
        sub = slice((p % 2) * 128, (p % 2 + 1) * 128)
        dd = pltpu.roll(ddens[p // 2][:, sub], 64, 1)
        dhi = dd.astype(bf16)
        dlo = (dd - dhi.astype(f32)).astype(bf16)
        aux = jnp.where(near == 0, dhi.astype(f32), jnp.where(near == 1, dlo.astype(f32), 0.0)).astype(bf16)
        dn = dnums[p // 2][:, sub]
        dd_ref[:, pl.ds(p * 256, 128)] = jnp.where(low, dn, aux)
        dd_ref[:, pl.ds(p * 256 + 128, 128)] = jnp.where(low, aux, dn)
    for h in range(2 * pairs):
        own = pl.ds(h * 128, 128)
        state[h] += mm_f(phiq_ref[:, own], dd_ref[:, own] * start_b)

    @pl.when(step == pl.num_programs(0) - 1)
    def _():
        pack_states(lambda h: state[h], gst_ref, pairs, True)
        total = jnp.sum(sum_ref[...], axis=1, keepdims=True)
        high = total.astype(bf16).astype(f32)
        place = lanes((8, 128))
        tile = jnp.where(place == 126, high, jnp.where(place == 127, total - high, 0.0))
        tile = jnp.concatenate([tile, jnp.zeros_like(tile)], axis=0)
        top = gst_ref[pairs, pl.ds(0, 16), :].astype(f32)
        gst_ref[pairs, pl.ds(0, 16), :] = (top + tile).astype(bf16)


def back_body(
    base, pairs, all_pairs, me_ref, keep_ref, cend_ref, q_ref, k_ref, v_ref, phiq_ref, phik_ref, dd_ref, srel_ref, sin_ref,
    cnt_ref, row_ref, feat_ref, *refs
):
    sts = refs[:2]
    (dqkv_ref, gfeat_ref, mapq, mapk, state, gq, gk, stv, sems) = refs[2:]
    step = pl.program_id(0)
    nblk = pl.num_programs(0)
    here = nblk - 1 - step

    @pl.when(step == 0)
    def _():
        copies = []
        for c in range(2):
            copies.append(pltpu.make_async_copy(sts[c], stv.at[c], sems.at[c]))
            copies[c].start()
        pair_maps(feat_ref, mapq, pairs, 0)
        pair_maps(feat_ref, mapk, pairs, 1)
        gq[...] = jnp.zeros_like(gq)
        gk[...] = jnp.zeros_like(gk)
        for c in copies:
            c.wait()

        def put(h, value):
            state[h] = value

        unpack_states(me_ref[0], keep_ref, stv, put, base, pairs, all_pairs, True)

    size = q_ref.shape[0]
    width = q_ref.shape[1]
    cnt = cnt_ref[...]
    first, last = cend_ref[here], cend_ref[here + 1]
    row_id = lax.broadcasted_iota(jnp.int32, (size, size), 0)
    col_id = lanes((size, size))
    same = cnt == row_ref[...]
    mask = (row_id >= col_id) & same
    mask_t = (col_id >= row_id) & same
    before = jnp.where(cnt == first, 1.0, 0.0).astype(bf16)
    after = jnp.where(cnt == last, 1.0, 0.0).astype(bf16)
    keep = jnp.where(first == last, 1.0, 0.0)
    opened = jnp.where(first == 0.0, 1.0, 0.0)
    ones = block_ones(256, 64)
    low = lanes((size, 128)) < 64
    heads = range(2 * pairs)
    cols = [pl.ds(h * 128, 128) for h in heads]
    vals = [v for p in range(pairs) for v in augmented(v_ref[:, pl.ds(p * 128, 128)])]
    scores_t = [
        jnp.where(mask_t, mm_t(phik_ref[:, c], phiq_ref[:, c]), 0.0).astype(bf16) for c in cols
    ]
    dsc = [jnp.where(mask, mm_t(dd_ref[:, c], v), 0.0).astype(bf16) for c, v in zip(cols, vals)]
    dsc_t = [jnp.where(mask_t, mm_t(v, dd_ref[:, c]), 0.0).astype(bf16) for c, v in zip(cols, vals)]
    sts = [
        (srel_ref[0, h].astype(f32) + opened * sin_ref[h].astype(f32)).astype(bf16) for h in heads
    ]
    dsts = [state[h].astype(bf16) for h in heads]
    ddws = [dd_ref[:, c] * before for c in cols]
    dphi_q = [mm(dsc[h], phik_ref[:, cols[h]]) + mm_t(ddws[h], sts[h]) for h in heads]
    dphi_k = [mm(dsc_t[h], phiq_ref[:, cols[h]]) + mm_t(vals[h] * after, dsts[h]) for h in heads]
    dvs = [mm(scores_t[h], dd_ref[:, cols[h]]) + mm(phik_ref[:, cols[h]] * after, dsts[h]) for h in heads]
    for h in heads:
        state[h] = keep * state[h] + mm_f(phiq_ref[:, cols[h]], ddws[h])
    for p in range(pairs):
        dqkv_ref[:, pl.ds(2 * width + p * 128, 128)] = jnp.where(low, dvs[2 * p], dvs[2 * p + 1]).astype(bf16)
    for phi_ref, dphi, rows_ref, maps, acc, base_col in (
        (phiq_ref, dphi_q, q_ref, mapq, gq, 0),
        (phik_ref, dphi_k, k_ref, mapk, gk, width),
    ):
        phis = [phi_ref[:, pl.ds(p * 256, 256)].astype(f32) for p in range(pairs)]
        dphis = [jnp.concatenate(dphi[2 * p : 2 * p + 2], axis=1) for p in range(pairs)]
        totals = [mm((phi * d).astype(bf16), ones) for phi, d in zip(phis, dphis)]
        dlogs = [(phi * (d - t)).astype(bf16) for phi, d, t in zip(phis, dphis, totals)]
        for p in range(pairs):
            two = pl.ds(p * 128, 128)
            dqkv_ref[:, pl.ds(base_col + p * 128, 128)] = mm_t(dlogs[p], maps[p]).astype(bf16)
            acc[p] += mm_f(rows_ref[:, two], dlogs[p])

    @pl.when(step == nblk - 1)
    def _():
        lane = lanes((128, 128))
        row = lax.broadcasted_iota(jnp.int32, (128, 128), 0)
        for p in range(pairs):
            outs = []
            for acc in (gq, gk):
                one = jnp.where(row < 64, acc[p, :, :128], acc[p, :, 128:])
                outs.append(one - pltpu.roll(one, 64, 1))
            gfeat_ref[pl.ds(p * 128, 128), :] = jnp.where(lane < 64, outs[0], -outs[1]).astype(bf16)


def enter_body(groups, me_ref, x_ref, dr_ref, gb_ref, *refs):
    width = x_ref.shape[1]
    grads = refs[:groups]
    wl = refs[groups : groups + 2]
    (dx_ref, sum_ref, w1, sems) = refs[groups + 2 :]

    @pl.when(pl.program_id(0) == 0)
    def _():
        me = me_ref[0]
        copies = fetch_start(wl, w1, me, sems.at[0], 0, 3 * width)
        sum_ref[...] = jnp.zeros_like(sum_ref)
        for c in copies:
            c.wait()

    gb = gb_ref[...]
    _, hat, rstd = normed(x_ref[...].astype(f32), gb[0:1], gb[2:3])
    part = width // groups
    dh = jnp.zeros(x_ref.shape, f32)
    for g in range(groups):
        for i in range(3):
            dh = dh + mm_t(grads[g][:, pl.ds(i * part, part)], w1[:, pl.ds(i * width + g * part, part)])
    dx_ref[...] = dr_ref[...] + normed_back(dh, hat, rstd, gb[0:1])
    sum_ref[0:1] += jnp.sum(dh * hat, axis=0, keepdims=True)
    sum_ref[1:2] += jnp.sum(dh, axis=0, keepdims=True)


def whole(*_):
    return pl.BlockSpec(memory_space=pl.ANY)


def smem():
    return pl.BlockSpec(memory_space=pltpu.SMEM)


def rows_spec(size, cols, back=None):
    if back is None:
        return pl.BlockSpec((size, cols), lambda i: (i, 0))
    return pl.BlockSpec((size, cols), lambda i: (back - 1 - i, 0))


def full_spec(shape):
    zeros = (0,) * len(shape)
    return pl.BlockSpec(shape, lambda i: zeros)


def sds(shape, kind):
    return jax.ShapeDtypeStruct(shape, kind)


def cparams():
    return pltpu.CompilerParams(
        dimension_semantics=("arbitrary",), vmem_limit_bytes=58 * 1024 * 1024
    )


def cost(micros):
    return pl.CostEstimate(
        flops=int(micros * 5e8), transcendentals=0, bytes_accessed=int(micros * 1e6)
    )


def dma(*shape):
    return pltpu.SemaphoreType.DMA(shape)


def shards(n_seq, depth, inputs, resets, norm_gains, norm_biases, w_qkv, w_feat, w_out, w_fc, w_proj, cotangent):
    tokens, width = inputs.shape[1], inputs.shape[2]
    hidden = w_fc.shape[1]
    head_dim = w_feat.shape[1] // 2
    heads = width // head_dim
    pairs = heads // 2
    rows = w_qkv.shape[0]
    nblk = tokens // BT
    x, dy = inputs[0], cotangent[0]
    me = lax.axis_index("seq")
    me_arr = me.reshape(1).astype(jnp.int32)

    marks = resets[0].reshape(nblk, BT).astype(bf16)
    flag = jnp.where(jnp.max(resets) == 0, 1.0, 0.0).astype(bf16)
    upper = jnp.triu(jnp.ones((BT, BT), bf16))
    inner = jnp.dot(marks, upper, preferred_element_type=f32)
    ends = jnp.cumsum(inner[:, -1])
    cend = jnp.concatenate([jnp.zeros((1,), f32), ends])
    counts = inner + cend[:-1, None]
    cnt_col = counts.reshape(tokens, 1)
    cnt_row = counts.reshape(1, tokens)

    norms = jnp.concatenate(
        [norm_gains, norm_biases, jnp.broadcast_to(flag, (rows, 1)), jnp.zeros((rows, 123), bf16)],
        axis=1,
    )
    first = stream_rows(stream_send(jnp.concatenate([w_qkv, w_feat, norms], axis=1), depth), depth)
    first = Spread(first, n_seq, False).near()
    up = jnp.concatenate([w_fc, w_out], axis=1)
    first.far_halves()
    up = stream_send(after(up, first.block), depth)
    first_blocks = first.cores()
    up = stream_rows([after(a, first_blocks[0]) for a in up], depth)
    up = Spread(up, n_seq, True).near(first_blocks[0])
    proj_pieces = stream_send(after(w_proj, first_blocks[1], up.block), depth)
    me_first = after(me_arr, up.block)

    packed = (pairs + 1, 128, 128)
    full = (heads, 128, 128)
    h_one, keys, vals, phi_k, state, gb, feat_all = pl.pallas_call(
        functools.partial(keys_body, n_seq, pairs),
        name="keys",
        cost_estimate=cost(22),
        grid=(tokens // TK,),
        in_specs=[smem(), smem(), rows_spec(TK, width), rows_spec(TK, 1)] + [whole()] * 2,
        out_specs=[rows_spec(TK, width)] * 3
        + [rows_spec(TK, 2 * width), full_spec(packed), full_spec((8, width)), full_spec((width, 128))],
        out_shape=[sds((tokens, width), bf16)] * 3
        + [sds((tokens, 2 * width), bf16), sds(packed, bf16), sds((8, width), f32), sds((width, 128), bf16)],
        scratch_shapes=[
            pltpu.VMEM((width, 2 * width + 256), bf16),
            pltpu.VMEM((pairs, 128, 256), bf16),
            pltpu.VMEM(full, f32),
            dma(2, n_seq),
        ],
        compiler_params=cparams(),
    )(me_first, cend, x, cnt_col, *first_blocks)
    level = lax.axis_index("stream")
    flags = gb[4].reshape(n_seq, depth, rows)[:, :, 0]
    keeps = lax.dynamic_index_in_dim(flags, level, 1, False)
    spread = Spread(state, n_seq, False).near_all()
    up.far_halves(gb)
    proj = Spread(stream_rows([after(a, gb) for a in proj_pieces], depth), n_seq, False).near()
    part_blk = nblk // 2
    local = []
    for part in range(2):
        base = part * part_blk

        def here(size, cols):
            return pl.BlockSpec((size, cols), lambda i: (base + i, 0))

        blocks_out = [
            sds((tokens, width), bf16), sds((tokens, 2 * width), bf16), sds((tokens, width), f32),
            sds((tokens, width), f32), sds((nblk,) + full, bf16),
        ]
        if part:
            me_two = after(me_arr, up_blocks[0], *[proj.found[b] for b in proj.bits], *spread.found.values())
        else:
            me_two = after(me_arr, proj.block, state, after(up.found[up.bits[0]], gb))
        local = pl.pallas_call(
            functools.partial(local_body, base, pairs),
            name="local",
            cost_estimate=cost(15),
            grid=(part_blk,),
            in_specs=[
                smem(), smem(), here(BT, width), here(BT, 2 * width), here(BT, width), here(BT, 1),
                pl.BlockSpec((1, BT), lambda i: (0, base + i)), full_spec((width, 128)),
            ]
            + [whole()] * 2
            + ([full_spec(full)] + [whole()] * 5 if part else []),
            out_specs=[
                here(BT, width), here(BT, 2 * width), here(BT, width), here(BT, width),
                pl.BlockSpec((1,) + full, lambda i: (base + i, 0, 0, 0)), full_spec(full),
            ],
            out_shape=blocks_out + [sds(full, f32)],
            scratch_shapes=[
                pltpu.VMEM((width, width), bf16),
                pltpu.VMEM((pairs, 128, 256), bf16),
                dma(n_seq),
            ],
            input_output_aliases={11 + i: i for i in range(5)} if part else {},
            compiler_params=cparams(),
        )(
            me_two, cend, h_one, phi_k, vals, cnt_col, cnt_row, feat_all, *first_blocks,
            *([local[5]] + list(local[:5]) if part else []),
        )
        if part == 0:
            event = local[5]
            proj.far(event)
            up_blocks = up.cores(event)
    queries, phi_q, num, den, srel, event = local
    states = spread.cores(event)
    proj_blocks = proj.cores(event)

    y, att, h_two, act, d_fc, d_att, d_mid, dd, s_in, g_state, sums = pl.pallas_call(
        functools.partial(middle_body, n_seq, pairs),
        name="middle",
        cost_estimate=cost(43),
        grid=(tokens // TM,),
        in_specs=[
            smem(), smem(), rows_spec(TM, width), rows_spec(TM, width), rows_spec(TM, width),
            rows_spec(TM, width), rows_spec(TM, 2 * width), rows_spec(TM, 1), full_spec((8, width)),
        ]
        + [whole()] * 6,
        out_specs=[
            rows_spec(TM, width), rows_spec(TM, width), rows_spec(TM, width), rows_spec(TM, hidden),
            rows_spec(TM, hidden), rows_spec(TM, width), rows_spec(TM, width), rows_spec(TM, 2 * width),
            full_spec(full), full_spec(packed), full_spec((8, width)),
        ],
        out_shape=[
            sds((tokens, width), bf16), sds((tokens, width), bf16), sds((tokens, width), bf16),
            sds((tokens, hidden), bf16), sds((tokens, hidden), bf16), sds((tokens, width), bf16),
            sds((tokens, width), f32), sds((tokens, 2 * width), bf16), sds(full, bf16), sds(packed, bf16),
            sds((8, width), f32),
        ],
        scratch_shapes=[
            pltpu.VMEM((width, width), bf16),
            pltpu.VMEM((width, hidden), bf16),
            pltpu.VMEM((hidden, width), bf16),
            pltpu.VMEM((TM, width), f32),
            pltpu.VMEM(full, f32),
            pltpu.VMEM((2, n_seq // 2) + packed, bf16),
            dma(4, n_seq),
        ],
        compiler_params=cparams(),
    )(
        me_arr, keeps, x, dy, num, den, phi_q, cnt_col, gb,
        *up_blocks, *proj_blocks, *states,
    )

    spread = Spread(g_state, n_seq, True).near_all()
    norm_two = jnp.stack([sums[3], sums[4]], axis=1).astype(bf16)
    norm_two = jnp.concatenate([norm_two, jnp.zeros((width, 126), bf16)], axis=1)
    nbits = n_seq.bit_length() - 1
    g_fc = mm_f(h_two, d_fc).astype(bf16)
    g_out = mm_f(att, d_att).astype(bf16)
    red_fc = Reduce([g_fc, g_out, norm_two], n_seq, depth, [0] + list(range(1, nbits))[::-1]).send()
    g_states = spread.cores(red_fc.out)
    g_proj = mm_f(after(act, red_fc.out, g_states[0]), dy).astype(bf16)
    red_proj = Reduce([g_proj], n_seq, depth).send()
    red_fc.add(red_proj.out).send()
    red_proj.add(red_fc.out).send()
    me_back = after(me_arr, red_proj.out, red_fc.out)
    squares = sum(
        jnp.sum(stack[:, pairs, :3, 126:].astype(f32), axis=(0, 2)) for stack in g_states
    )
    branch_rms = jnp.sqrt(squares / (tokens * n_seq * width)).reshape(1, 3)

    groups = 2
    some = pairs // groups
    part = some * 128
    d_qkv, g_feat = [], []
    for g in range(groups):

        def spec(cols):
            return pl.BlockSpec((BT, cols), lambda i: (nblk - 1 - i, g))

        def one_group(shape):
            return pl.BlockSpec(shape, lambda i: (g,) + (0,) * (len(shape) - 1))

        one = (2 * some, 128, 128)
        d_one, g_one = pl.pallas_call(
            functools.partial(back_body, g * some, some, pairs),
            name="back",
            cost_estimate=cost(19),
            grid=(nblk,),
            in_specs=[
                smem(), smem(), smem(), spec(part), spec(part), spec(part), spec(2 * part), spec(2 * part),
                spec(2 * part), pl.BlockSpec((1,) + one, lambda i: (nblk - 1 - i, g, 0, 0)), one_group(one),
                rows_spec(BT, 1, nblk), pl.BlockSpec((1, BT), lambda i: (0, nblk - 1 - i)),
                one_group((part, 128)),
            ]
            + [whole()] * 2,
            out_specs=[rows_spec(BT, 3 * part, nblk), full_spec((part, 128))],
            out_shape=[sds((tokens, 3 * part), bf16), sds((part, 128), bf16)],
            scratch_shapes=[
                pltpu.VMEM((some, 128, 256), bf16),
                pltpu.VMEM((some, 128, 256), bf16),
                pltpu.VMEM(one, f32),
                pltpu.VMEM((some, 128, 256), f32),
                pltpu.VMEM((some, 128, 256), f32),
                pltpu.VMEM((2, n_seq // 2) + packed, bf16),
                dma(n_seq),
            ],
            compiler_params=cparams(),
        )(
            me_back, keeps, cend, queries, keys, vals, phi_q, phi_k, dd, srel, s_in, cnt_col, cnt_row,
            feat_all, *g_states,
        )
        d_qkv.append(d_one)
        g_feat.append(g_one)
        if g == 0:
            red_proj.add(d_one).send()
            me_back = after(me_arr, red_proj.out)

    last = d_qkv[-1]
    g_qkv = [mm_f(h_one, d).astype(bf16) for d in d_qkv]
    red_two = Reduce(g_qkv + [jnp.concatenate(g_feat, axis=0)], n_seq, depth).send()
    red_fc.add(red_two.out).send()
    red_proj.add(red_fc.out).send_stream()
    me_late = after(me_arr, red_proj.out, red_fc.out)
    dx, sums_one = pl.pallas_call(
        functools.partial(enter_body, groups),
        name="enter",
        cost_estimate=cost(11),
        grid=(tokens // TM,),
        in_specs=[smem(), rows_spec(TM, width), rows_spec(TM, width), full_spec((8, width))]
        + [rows_spec(TM, 3 * part)] * groups
        + [whole()] * 2,
        out_specs=[rows_spec(TM, width), full_spec((8, width))],
        out_shape=[sds((tokens, width), f32), sds((8, width), f32)],
        scratch_shapes=[pltpu.VMEM((width, 3 * width), bf16), dma(2, n_seq)],
        compiler_params=cparams(),
    )(me_late, x, d_mid, gb, *d_qkv, *first_blocks)
    norm_one = jnp.stack([sums_one[0], sums_one[1]], axis=1).astype(bf16)
    norm_one = jnp.concatenate([norm_one, jnp.zeros((width, 126), bf16)], axis=1)
    red_norm = Reduce([norm_one], n_seq, depth).send()
    red_a, red_b = red_two.add(dx).cut((groups * 3 * part + 256) // 2)
    red_a.send()
    red_norm.add(red_a.out)
    red_b.cur = [beside(red_b.cur + red_norm.cur)]
    red_b.send()
    red_fc.add(red_a.out, red_b.out).send_stream()
    grad_proj = red_proj.done(red_fc.out)
    while red_a.order:
        red_a.add().send()
        red_b.add().send()
    tail = Reduce(red_a.add().cur + red_b.add().cur, n_seq, depth, [], []).send_stream()
    grad_up = red_fc.done(tail.out)
    tail = tail.done()
    grads = [tail[:, g * 3 * part : (g + 1) * 3 * part] for g in range(groups)]
    grad_feat = tail[:, groups * 3 * part : groups * 3 * part + 128]
    norm_one = tail[:, groups * 3 * part + 128 :]
    grad_fc = grad_up[:, :hidden]
    grad_out = grad_up[:, hidden:]
    grad_qkv = jnp.concatenate(
        [grads[g][:, i * part : (i + 1) * part] for i in range(3) for g in range(groups)], axis=1
    )
    return (
        y[None],
        dx[None],
        jnp.concatenate([norm_one[:, 0:1], grad_out[:, width : width + 1]], axis=1),
        jnp.concatenate([norm_one[:, 1:2], grad_out[:, width + 1 : width + 2]], axis=1),
        grad_qkv,
        grad_feat,
        grad_out[:, :width],
        grad_fc,
        grad_proj,
        branch_rms,
    )


def solution(mesh):
    both = P(("seq", "stream"), None)
    acts = P("stream", "seq", None)
    placed = (acts, P("stream", "seq"), both, both, both, both, both, both, both, acts)
    return jax.shard_map(
        functools.partial(shards, mesh.shape["seq"], mesh.shape["stream"]),
        mesh=mesh,
        in_specs=placed,
        out_specs=(acts, acts, both, both, both, both, both, both, both, P("stream", None)),
        check_vma=False,
    )
```

```python
import functools

import jax
import jax.numpy as jnp
from jax import lax
from jax.experimental import pallas as pl
from jax.experimental.pallas import tpu as pltpu
from jax.sharding import PartitionSpec as P

BT = 256
GF = 6
TK = 512
TM = 256
epsilon = 1e-05
f32 = jnp.float32
bf16 = jnp.bfloat16
GC = 0.7978845608028654
GA = 0.044715


def mm(a, b):
    return jnp.dot(a, b, preferred_element_type=f32)


def mm_t(a, b):
    return lax.dot_general(a, b, (((1,), (1,)), ((), ())), preferred_element_type=f32)


def mm_f(a, b):
    return lax.dot_general(a, b, (((0,), (0,)), ((), ())), preferred_element_type=f32)


def xor_send(arr, size, mask):
    return lax.ppermute(arr, "seq", [(i, i ^ mask) for i in range(size)])


def after(arr, *deps):
    return lax.optimization_barrier((arr,) + deps)[0]


def stream_send(shard, depth):
    return [shard] + [
        lax.ppermute(shard, "stream", [(i, (i + d) % depth) for i in range(depth)])
        for d in range(1, depth)
    ]


def stream_rows(pieces, depth):
    shard = pieces[0]
    ring = pieces[::-1]
    place = lax.axis_index("stream")
    rows = shard.shape[0]
    both = jnp.concatenate(ring + ring, axis=0)
    return lax.dynamic_slice_in_dim(both, (depth - 1 - place) * rows, depth * rows, 0)


class Spread:
    def __init__(self, block, size, flip):
        self.size = size
        bits = [1 << b for b in range(1, size.bit_length() - 1)]
        self.bits = bits[::-1] if flip else bits
        self.block = block
        self.found = {0: block}

    def near(self, *deps):
        block = after(self.block, *deps) if deps else self.block
        for bit in self.bits:
            self.found[bit] = xor_send(block, self.size, bit)
        return self

    def near_all(self):
        for r in range(2, self.size, 2):
            self.found[r] = xor_send(self.block, self.size, r)
        return self

    def far(self, *deps):
        for bit in self.bits:
            for r in list(self.found):
                if r ^ bit not in self.found and r < 2 * max(self.bits):
                    src = self.found[r]
                    self.found[r ^ bit] = xor_send(after(src, *deps) if deps else src, self.size, bit)
        return self

    def far_halves(self, *deps):
        one, two = self.bits[:2]
        half = self.block.shape[1] // 256 * 128
        srcs = (self.found[one], self.found[two])
        if deps:
            srcs = lax.optimization_barrier(srcs + deps)[:2]
        self.cuts = [srcs[0][:, :half], srcs[1][:, half:]]
        left = xor_send(self.cuts[0], self.size, two)
        right = xor_send(self.cuts[1], self.size, one)
        self.found[one ^ two] = jnp.concatenate([left, right], axis=1)
        return self.far(*deps)

    def cores(self, *deps):
        parts = [self.found[2 * r] for r in range(self.size // 2)]
        if deps:
            parts = lax.optimization_barrier(tuple(parts) + deps)[: len(parts)]
        stack = jnp.stack(parts)
        return [stack, xor_send(stack, self.size, 1)]


def beside(parts):
    return parts[0] if len(parts) == 1 else jnp.concatenate(parts, axis=-1)


class Reduce:
    def __init__(self, grads, size, depth, order=None, rest=None):
        self.size, self.depth = size, depth
        nbits = size.bit_length() - 1
        self.rest = list(range(nbits))[::-1] if rest is None else list(rest)
        self.order = list(range(nbits)) if order is None else list(order)
        self.cur = [
            g.reshape([2] * len(self.rest) + [g.shape[0] // 2 ** len(self.rest), g.shape[1]])
            if g.ndim == 2
            else g
            for g in grads
        ]

    def send(self):
        place = lax.axis_index("seq")
        bit = self.order.pop(0)
        axis = self.rest.index(bit)
        own = (place >> bit) & 1
        self.out = beside([lax.dynamic_index_in_dim(c, 1 - own, axis, False) for c in self.cur])
        self.kept = [lax.dynamic_index_in_dim(c, own, axis, False) for c in self.cur]
        self.flight = xor_send(self.out, self.size, 1 << bit)
        self.rest.pop(axis)
        return self

    def add(self, *deps):
        got = after(self.flight, *deps) if deps else self.flight
        self.cur = [(beside(self.kept).astype(f32) + got.astype(f32)).astype(bf16)]
        return self

    def cut(self, at):
        (cur,) = self.cur
        parts = [
            Reduce([cur[..., :at]], self.size, self.depth, self.order, self.rest),
            Reduce([cur[..., at:]], self.size, self.depth, self.order[::-1], self.rest),
        ]
        return parts

    def send_stream(self):
        while self.order:
            self.send().add()
        depth = self.depth
        level = lax.axis_index("stream")
        cur = beside(self.cur)
        self.out = cur
        cur = cur.reshape(depth, cur.shape[0] // depth, cur.shape[1])
        self.total = lax.dynamic_index_in_dim(cur, level, 0, False).astype(f32)
        self.flights = []
        for d in range(1, depth):
            piece = lax.dynamic_index_in_dim(cur, (level + d) % depth, 0, False)
            self.flights.append(
                lax.ppermute(piece, "stream", [(i, (i + d) % depth) for i in range(depth)])
            )
        return self

    def done(self, *deps):
        total = self.total
        for f in self.flights:
            total = total + (after(f, *deps) if deps else f).astype(f32)
        return total


def lanes(shape):
    return lax.broadcasted_iota(jnp.int32, shape, len(shape) - 1)


def block_ones(width, part):
    r = lax.broadcasted_iota(jnp.int32, (width, width), 0) // part
    c = lax.broadcasted_iota(jnp.int32, (width, width), 1) // part
    return jnp.where(r == c, 1.0, 0.0).astype(bf16)


def fetch_start(stacks, dest, me, sems, col=0, width=None, at=0):
    half = stacks[0].shape[0]
    rows = dest.shape[0] // (2 * half)
    width = width or stacks[0].shape[2]
    copies = []
    for c, ref in enumerate(stacks):
        for r in range(half):
            off = pl.multiple_of((me ^ (2 * r + c)) * rows, 8)
            copy = pltpu.make_async_copy(
                ref.at[r, :, pl.ds(col, width)],
                dest.at[pl.ds(off, rows), pl.ds(at, width)],
                sems.at[2 * r + c],
            )
            copy.start()
            copies.append(copy)
    return copies


def pair_maps(feat_ref, dest, pairs, which):
    width = 128
    lane = lanes((width, width))
    row = lax.broadcasted_iota(jnp.int32, (width, width), 0)
    for p in range(pairs):
        both = feat_ref[pl.ds(p * width, width), :].astype(f32)
        half = width // 2
        other = pltpu.roll(both, half, 1)
        if which == 0:
            signed = jnp.where(lane < half, both, -other)
        else:
            signed = jnp.where(lane < half, other, -both)
        dest[p, :, pl.ds(0, width)] = jnp.where(row < half, signed, 0.0).astype(bf16)
        dest[p, :, pl.ds(width, width)] = jnp.where(row >= half, signed, 0.0).astype(bf16)


def features(logits_of, ones):
    halves = [one[:, j * 128 : (j + 1) * 128] for one in logits_of for j in range(2)]
    low = lanes(halves[0].shape) < 64
    tops = [
        (
            jnp.max(jnp.where(low, one, -jnp.inf), axis=1, keepdims=True),
            jnp.max(jnp.where(low, -jnp.inf, one), axis=1, keepdims=True),
        )
        for one in halves
    ]
    exps = [jnp.exp(one - jnp.where(low, *top)) for one, top in zip(halves, tops)]
    exps = [jnp.concatenate(exps[2 * i : 2 * i + 2], axis=1) for i in range(len(logits_of))]
    sums = [mm(e.astype(bf16), ones) for e in exps]
    return [(e / t).astype(bf16) for e, t in zip(exps, sums)]


def augmented(two):
    low = lanes(two.shape) < 64
    one = jnp.ones_like(two)
    return jnp.where(low, two, one), jnp.where(low, one, two)


def pack_states(get, dest, pairs, zsum):
    shape = (128, 128)
    lane = lanes(shape)
    low = lane < 64
    zt = jnp.zeros(shape, f32)
    for p in range(pairs):
        a, b = get(2 * p), get(2 * p + 1)
        dest[p] = jnp.where(low, a, b).astype(bf16)
        if zsum:
            za = jnp.sum(jnp.where(low, 0.0, a), axis=1, keepdims=True)
            zb = jnp.sum(jnp.where(low, b, 0.0), axis=1, keepdims=True)
        else:
            za, zb = a, b
        zt = jnp.where(lane == 64 + 2 * p, za, zt)
        zt = jnp.where(lane == 2 * p + 1, zb, zt)
    dest[pairs] = zt.astype(bf16)


def unpack_states(me, keep_ref, blocks, put, base, count, pairs, back):
    shape = (128, 128)
    lane = lanes(shape)
    low = lane < 64
    size = 2 * blocks.shape[1]
    coefs = [None]
    for r in range(1, size):
        j = me ^ r
        c = jnp.where(j > me if back else j < me, 1.0, 0.0)
        for i in range(size):
            between = ((i > me) & (i < j)) if back else ((i > j) & (i < me))
            c = c * jnp.where(between, keep_ref[i], 1.0)
        coefs.append(c)

    def total(i):
        acc = jnp.zeros(shape, f32)
        for r in range(1, size):
            acc = acc + coefs[r] * blocks[r % 2, r // 2, i].astype(f32)
        return acc

    zt = total(pairs)
    for q in range(count):
        p = base + q
        two = total(p)
        za = jnp.sum(jnp.where(lane == 64 + 2 * p, zt, 0.0), axis=1, keepdims=True)
        zb = jnp.sum(jnp.where(lane == 2 * p + 1, zt, 0.0), axis=1, keepdims=True)
        if back:
            put(2 * q, jnp.where(low, two, jnp.where(lane == 64, za, 0.0)))
            put(2 * q + 1, jnp.where(low, jnp.where(lane == 0, zb, 0.0), two))
        else:
            put(2 * q, jnp.where(low, two, za))
            put(2 * q + 1, jnp.where(low, zb, two))


def normed(values, gain, bias):
    mean = jnp.mean(values, axis=1, keepdims=True)
    cent = values - mean
    rstd = lax.rsqrt(jnp.mean(cent * cent, axis=1, keepdims=True) + epsilon)
    hat = cent * rstd
    return hat * gain + bias, hat, rstd


def normed_back(grad, hat, rstd, gain):
    dhat = grad * gain
    return rstd * (
        dhat
        - jnp.mean(dhat, axis=1, keepdims=True)
        - hat * jnp.mean(dhat * hat, axis=1, keepdims=True)
    )


def keys_body(n_seq, pairs, me_ref, cend_ref, x_ref, cnt_ref, *refs):
    width = x_ref.shape[1]
    wl = refs[:2]
    (h_ref, k_ref, v_ref, phi_ref, st_ref, gb_ref, feat_ref, w1, maps, state, sems) = refs[2:]
    step = pl.program_id(0)

    @pl.when(step == 0)
    def _():
        me = me_ref[0]
        copies = fetch_start(wl, w1, me, sems.at[0], width, 2 * width + 256)
        for c in copies:
            c.wait()
        gb_ref[...] = w1[:, pl.ds(2 * width + 128, 128)].astype(f32).T[:8]
        feat_ref[...] = w1[:, pl.ds(2 * width, 128)]
        pair_maps(feat_ref, maps, pairs, 1)
        state[...] = jnp.zeros_like(state)

    gb = gb_ref[...]
    out, _, _ = normed(x_ref[...].astype(f32), gb[0:1], gb[2:3])
    h1 = out.astype(bf16)
    h_ref[...] = h1
    keys = mm(h1, w1[:, pl.ds(0, width)]).astype(bf16)
    vals = mm(h1, w1[:, pl.ds(width, width)]).astype(bf16)
    k_ref[...] = keys
    v_ref[...] = vals
    ones = block_ones(256, 64)
    last = cend_ref[cend_ref.shape[0] - 1]
    used = jnp.where(cnt_ref[...] == last, 1.0, 0.0).astype(bf16)
    for g in range(0, pairs, GF):
        group = range(g, min(g + GF, pairs))
        phis = features([mm(keys[:, p * 128 : (p + 1) * 128], maps[p]) for p in group], ones)
        for p, phi in zip(group, phis):
            phi_ref[:, pl.ds(p * 256, 256)] = phi
            va, vb = augmented(vals[:, p * 128 : (p + 1) * 128])
            state[2 * p] += mm_f(phi[:, :128], va * used)
            state[2 * p + 1] += mm_f(phi[:, 128:], vb * used)

    @pl.when(step == pl.num_programs(0) - 1)
    def _():
        pack_states(lambda h: state[h], st_ref, pairs, False)


def local_body(base, pairs, me_ref, cend_ref, h_ref, phik_ref, v_ref, cnt_ref, row_ref, feat_ref, *refs):
    wq = refs[:2]
    (q_ref, phiq_ref, num_ref, den_ref, srel_ref, state, w1, maps, sems) = refs[-9:]
    step = pl.program_id(0)
    width = h_ref.shape[1]

    @pl.when(step == 0)
    def _():
        copies = fetch_start(wq, w1, me_ref[0], sems, 0, width)
        pair_maps(feat_ref, maps, pairs, 0)
        if base:
            state[...] = refs[2][...]
        else:
            state[...] = jnp.zeros_like(state)
        for c in copies:
            c.wait()

    queries = mm(h_ref[...], w1[...]).astype(bf16)
    q_ref[...] = queries
    ones = block_ones(256, 64)
    size = h_ref.shape[0]
    cnt = cnt_ref[...]
    first, last = cend_ref[base + step], cend_ref[base + step + 1]
    row_id = lax.broadcasted_iota(jnp.int32, (size, size), 0)
    mask = (row_id >= lanes((size, size))) & (cnt == row_ref[...])
    before = jnp.where(cnt == first, 1.0, 0.0)
    after = jnp.where(cnt == last, 1.0, 0.0).astype(bf16)
    keep = jnp.where(first == last, 1.0, 0.0)
    low = lanes((size, 128)) < 64
    for g in range(0, pairs, GF):
        group = range(g, min(g + GF, pairs))
        phis = features([mm(queries[:, p * 128 : (p + 1) * 128], maps[p]) for p in group], ones)
        for p, phi in zip(group, phis):
            phiq_ref[:, pl.ds(p * 256, 256)] = phi
        pqs = [phi[:, j * 128 : (j + 1) * 128] for phi in phis for j in range(2)]
        heads = [2 * p + j for p in group for j in range(2)]
        pks = [phik_ref[:, pl.ds(h * 128, 128)] for h in heads]
        scores = [jnp.where(mask, mm_t(pq, pk), 0.0).astype(bf16) for pq, pk in zip(pqs, pks)]
        val_of = [v for p in group for v in augmented(v_ref[:, p * 128 : (p + 1) * 128])]
        res = []
        for h, pq, pk, sc, val in zip(heads, pqs, pks, scores, val_of):
            st = state[h]
            st_b = st.astype(bf16)
            srel_ref[0, h] = st_b
            res.append(mm(sc, val) + before * mm(pq, st_b))
            state[h] = keep * st + mm_f(pk, val * after)
        for i, p in enumerate(group):
            two = pl.ds(p * 128, 128)
            num_ref[:, two] = jnp.where(low, res[2 * i], res[2 * i + 1])
            den_ref[:, two] = pltpu.roll(jnp.where(low, res[2 * i + 1], res[2 * i]), 64, 1)


def middle_body(
    n_seq, pairs, me_ref, keep_ref, x_ref, dy_ref, num_ref, den_ref, phiq_ref, cnt_ref, gb_ref, *refs
):
    width = x_ref.shape[1]
    wf, wp, sts = (refs[2 * i : 2 * i + 2] for i in range(3))
    (
        y_ref, o_ref, h_ref, a_ref, df_ref, dat_ref, dr_ref, dd_ref, sin_ref, gst_ref, sum_ref,
        w_out, w_fc, w_proj, rden, state, stv, sems,
    ) = refs[6:]
    step = pl.program_id(0)
    chunk = 768
    hidden = w_fc.shape[1]
    size = x_ref.shape[0]

    @pl.when(step == 0)
    def _():
        me = me_ref[0]
        st_copies = []
        for c in range(2):
            st_copies.append(pltpu.make_async_copy(sts[c], stv.at[c], sems.at[3, c]))
            st_copies[c].start()
        copies = fetch_start(wf, w_out, me, sems.at[0], hidden, width)
        copies += fetch_start(wf, w_fc, me, sems.at[1], 0, hidden)
        copies += fetch_start(wp, w_proj, me, sems.at[2])
        for c in st_copies:
            c.wait()

        def put(h, value):
            sin_ref[h] = value.astype(bf16)

        unpack_states(me, keep_ref, stv, put, 0, pairs, pairs, False)
        state[...] = jnp.zeros_like(state)
        sum_ref[...] = jnp.zeros_like(sum_ref)
        for c in copies:
            c.wait()

    gb = gb_ref[...]
    low = lanes((size, 128)) < 64
    start = jnp.where(cnt_ref[...] == 0.0, 1.0, 0.0)
    start_b = start.astype(bf16)
    res = [mm(phiq_ref[:, pl.ds(h * 128, 128)], sin_ref[h]) for h in range(2 * pairs)]
    for p in range(pairs):
        two = pl.ds(p * 128, 128)
        ra, rb = res[2 * p], res[2 * p + 1]
        num = num_ref[:, two] + start * jnp.where(low, ra, rb)
        den = den_ref[:, two] + start * pltpu.roll(jnp.where(low, rb, ra), 64, 1)
        inv = 1.0 / den
        rden[:, two] = inv
        o_ref[:, two] = (num * inv).astype(bf16)
    x = x_ref[...].astype(f32)
    attn = mm(o_ref[...], w_out[...])
    mid = x + attn
    out, hat, rstd = normed(mid, gb[1:2], gb[3:4])
    h2 = out.astype(bf16)
    h_ref[...] = h2
    dy_b = dy_ref[...]
    branch = jnp.zeros((size, width), f32)
    dh2 = jnp.zeros((size, width), f32)
    for c in range(w_fc.shape[1] // chunk):
        cols = pl.ds(c * chunk, chunk)
        fc = mm(h2, w_fc[:, cols])
        square = fc * fc
        tan = jnp.tanh(fc * (GC + GC * GA * square))
        half = 0.5 + 0.5 * tan
        act = (fc * half).astype(bf16)
        a_ref[:, cols] = act
        branch = branch + mm(act, w_proj[cols, :])
        slope = half + fc * (1.0 - half) * half * (2.0 * GC + 6.0 * GC * GA * square)
        dfc = (mm_t(dy_b, w_proj[cols, :]) * slope).astype(bf16)
        df_ref[:, cols] = dfc
        dh2 = dh2 + mm_t(dfc, w_fc[:, cols])
    y = mid + branch
    y_ref[...] = y.astype(bf16)
    sum_ref[0:1] += jnp.sum(attn * attn, axis=0, keepdims=True)
    sum_ref[1:2] += jnp.sum(branch * branch, axis=0, keepdims=True)
    sum_ref[2:3] += jnp.sum(y * y, axis=0, keepdims=True)
    sum_ref[3:4] += jnp.sum(dh2 * hat, axis=0, keepdims=True)
    sum_ref[4:5] += jnp.sum(dh2, axis=0, keepdims=True)
    dr = dy_b.astype(f32) + normed_back(dh2, hat, rstd, gb[1:2])
    dr_ref[...] = dr
    dat = dr.astype(bf16)
    dat_ref[...] = dat
    d_o = mm_t(dat, w_out[...])
    ones = block_ones(256, 64)
    lane = lanes((size, 128))
    quads = range(pairs // 2)
    fours = [pl.ds(q * 256, 256) for q in quads]
    d_os = [d_o[:, q * 256 : (q + 1) * 256] for q in quads]
    prods = [d * o_ref[:, c].astype(f32) for d, c in zip(d_os, fours)]
    his = [a.astype(bf16) for a in prods]
    los = [(a - hi.astype(f32)).astype(bf16) for a, hi in zip(prods, his)]
    ddens = [-(mm(hi, ones) + mm(lo, ones)) * rden[:, c] for hi, lo, c in zip(his, los, fours)]
    dnums = [(d * rden[:, c]).astype(bf16) for d, c in zip(d_os, fours)]
    near = lane & 63
    for p in range(pairs):
        sub = slice((p % 2) * 128, (p % 2 + 1) * 128)
        dd = pltpu.roll(ddens[p // 2][:, sub], 64, 1)
        dhi = dd.astype(bf16)
        dlo = (dd - dhi.astype(f32)).astype(bf16)
        aux = jnp.where(near == 0, dhi.astype(f32), jnp.where(near == 1, dlo.astype(f32), 0.0)).astype(bf16)
        dn = dnums[p // 2][:, sub]
        dd_ref[:, pl.ds(p * 256, 128)] = jnp.where(low, dn, aux)
        dd_ref[:, pl.ds(p * 256 + 128, 128)] = jnp.where(low, aux, dn)
    for h in range(2 * pairs):
        own = pl.ds(h * 128, 128)
        state[h] += mm_f(phiq_ref[:, own], dd_ref[:, own] * start_b)

    @pl.when(step == pl.num_programs(0) - 1)
    def _():
        pack_states(lambda h: state[h], gst_ref, pairs, True)
        total = jnp.sum(sum_ref[...], axis=1, keepdims=True)
        high = total.astype(bf16).astype(f32)
        place = lanes((8, 128))
        tile = jnp.where(place == 126, high, jnp.where(place == 127, total - high, 0.0))
        tile = jnp.concatenate([tile, jnp.zeros_like(tile)], axis=0)
        top = gst_ref[pairs, pl.ds(0, 16), :].astype(f32)
        gst_ref[pairs, pl.ds(0, 16), :] = (top + tile).astype(bf16)


def back_body(
    base, pairs, all_pairs, me_ref, keep_ref, cend_ref, q_ref, k_ref, v_ref, phiq_ref, phik_ref, dd_ref, srel_ref, sin_ref,
    cnt_ref, row_ref, feat_ref, *refs
):
    sts = refs[:2]
    (dqkv_ref, gfeat_ref, mapq, mapk, state, gq, gk, stv, sems) = refs[2:]
    step = pl.program_id(0)
    nblk = pl.num_programs(0)
    here = nblk - 1 - step

    @pl.when(step == 0)
    def _():
        copies = []
        for c in range(2):
            copies.append(pltpu.make_async_copy(sts[c], stv.at[c], sems.at[c]))
            copies[c].start()
        pair_maps(feat_ref, mapq, pairs, 0)
        pair_maps(feat_ref, mapk, pairs, 1)
        gq[...] = jnp.zeros_like(gq)
        gk[...] = jnp.zeros_like(gk)
        for c in copies:
            c.wait()

        def put(h, value):
            state[h] = value

        unpack_states(me_ref[0], keep_ref, stv, put, base, pairs, all_pairs, True)

    size = q_ref.shape[0]
    width = q_ref.shape[1]
    cnt = cnt_ref[...]
    first, last = cend_ref[here], cend_ref[here + 1]
    row_id = lax.broadcasted_iota(jnp.int32, (size, size), 0)
    col_id = lanes((size, size))
    same = cnt == row_ref[...]
    mask = (row_id >= col_id) & same
    mask_t = (col_id >= row_id) & same
    before = jnp.where(cnt == first, 1.0, 0.0).astype(bf16)
    after = jnp.where(cnt == last, 1.0, 0.0).astype(bf16)
    keep = jnp.where(first == last, 1.0, 0.0)
    opened = jnp.where(first == 0.0, 1.0, 0.0)
    ones = block_ones(256, 64)
    low = lanes((size, 128)) < 64
    heads = range(2 * pairs)
    cols = [pl.ds(h * 128, 128) for h in heads]
    vals = [v for p in range(pairs) for v in augmented(v_ref[:, pl.ds(p * 128, 128)])]
    scores_t = [
        jnp.where(mask_t, mm_t(phik_ref[:, c], phiq_ref[:, c]), 0.0).astype(bf16) for c in cols
    ]
    dsc = [jnp.where(mask, mm_t(dd_ref[:, c], v), 0.0).astype(bf16) for c, v in zip(cols, vals)]
    dsc_t = [jnp.where(mask_t, mm_t(v, dd_ref[:, c]), 0.0).astype(bf16) for c, v in zip(cols, vals)]
    sts = [
        (srel_ref[0, h].astype(f32) + opened * sin_ref[h].astype(f32)).astype(bf16) for h in heads
    ]
    dsts = [state[h].astype(bf16) for h in heads]
    ddws = [dd_ref[:, c] * before for c in cols]
    dphi_q = [mm(dsc[h], phik_ref[:, cols[h]]) + mm_t(ddws[h], sts[h]) for h in heads]
    dphi_k = [mm(dsc_t[h], phiq_ref[:, cols[h]]) + mm_t(vals[h] * after, dsts[h]) for h in heads]
    dvs = [mm(scores_t[h], dd_ref[:, cols[h]]) + mm(phik_ref[:, cols[h]] * after, dsts[h]) for h in heads]
    for h in heads:
        state[h] = keep * state[h] + mm_f(phiq_ref[:, cols[h]], ddws[h])
    for p in range(pairs):
        dqkv_ref[:, pl.ds(2 * width + p * 128, 128)] = jnp.where(low, dvs[2 * p], dvs[2 * p + 1]).astype(bf16)
    for phi_ref, dphi, rows_ref, maps, acc, base_col in (
        (phiq_ref, dphi_q, q_ref, mapq, gq, 0),
        (phik_ref, dphi_k, k_ref, mapk, gk, width),
    ):
        phis = [phi_ref[:, pl.ds(p * 256, 256)].astype(f32) for p in range(pairs)]
        dphis = [jnp.concatenate(dphi[2 * p : 2 * p + 2], axis=1) for p in range(pairs)]
        totals = [mm((phi * d).astype(bf16), ones) for phi, d in zip(phis, dphis)]
        dlogs = [(phi * (d - t)).astype(bf16) for phi, d, t in zip(phis, dphis, totals)]
        for p in range(pairs):
            two = pl.ds(p * 128, 128)
            dqkv_ref[:, pl.ds(base_col + p * 128, 128)] = mm_t(dlogs[p], maps[p]).astype(bf16)
            acc[p] += mm_f(rows_ref[:, two], dlogs[p])

    @pl.when(step == nblk - 1)
    def _():
        lane = lanes((128, 128))
        row = lax.broadcasted_iota(jnp.int32, (128, 128), 0)
        for p in range(pairs):
            outs = []
            for acc in (gq, gk):
                one = jnp.where(row < 64, acc[p, :, :128], acc[p, :, 128:])
                outs.append(one - pltpu.roll(one, 64, 1))
            gfeat_ref[pl.ds(p * 128, 128), :] = jnp.where(lane < 64, outs[0], -outs[1]).astype(bf16)


def enter_body(groups, me_ref, x_ref, dr_ref, gb_ref, *refs):
    width = x_ref.shape[1]
    grads = refs[:groups]
    wl = refs[groups : groups + 2]
    (dx_ref, sum_ref, w1, sems) = refs[groups + 2 :]

    @pl.when(pl.program_id(0) == 0)
    def _():
        me = me_ref[0]
        copies = fetch_start(wl, w1, me, sems.at[0], 0, 3 * width)
        sum_ref[...] = jnp.zeros_like(sum_ref)
        for c in copies:
            c.wait()

    gb = gb_ref[...]
    _, hat, rstd = normed(x_ref[...].astype(f32), gb[0:1], gb[2:3])
    part = width // groups
    dh = jnp.zeros(x_ref.shape, f32)
    for g in range(groups):
        for i in range(3):
            dh = dh + mm_t(grads[g][:, pl.ds(i * part, part)], w1[:, pl.ds(i * width + g * part, part)])
    dx_ref[...] = dr_ref[...] + normed_back(dh, hat, rstd, gb[0:1])
    sum_ref[0:1] += jnp.sum(dh * hat, axis=0, keepdims=True)
    sum_ref[1:2] += jnp.sum(dh, axis=0, keepdims=True)


def whole(*_):
    return pl.BlockSpec(memory_space=pl.ANY)


def smem():
    return pl.BlockSpec(memory_space=pltpu.SMEM)


def rows_spec(size, cols, back=None):
    if back is None:
        return pl.BlockSpec((size, cols), lambda i: (i, 0))
    return pl.BlockSpec((size, cols), lambda i: (back - 1 - i, 0))


def full_spec(shape):
    zeros = (0,) * len(shape)
    return pl.BlockSpec(shape, lambda i: zeros)


def sds(shape, kind):
    return jax.ShapeDtypeStruct(shape, kind)


def cparams():
    return pltpu.CompilerParams(
        dimension_semantics=("arbitrary",), vmem_limit_bytes=58 * 1024 * 1024
    )


def cost(micros):
    return pl.CostEstimate(
        flops=int(micros * 5e8), transcendentals=0, bytes_accessed=int(micros * 1e6)
    )


def dma(*shape):
    return pltpu.SemaphoreType.DMA(shape)


def shards(n_seq, depth, inputs, resets, norm_gains, norm_biases, w_qkv, w_feat, w_out, w_fc, w_proj, cotangent):
    tokens, width = inputs.shape[1], inputs.shape[2]
    hidden = w_fc.shape[1]
    head_dim = w_feat.shape[1] // 2
    heads = width // head_dim
    pairs = heads // 2
    rows = w_qkv.shape[0]
    nblk = tokens // BT
    x, dy = inputs[0], cotangent[0]
    me = lax.axis_index("seq")
    me_arr = me.reshape(1).astype(jnp.int32)

    marks = resets[0].reshape(nblk, BT).astype(bf16)
    flag = jnp.where(jnp.max(resets) == 0, 1.0, 0.0).astype(bf16)
    upper = jnp.triu(jnp.ones((BT, BT), bf16))
    inner = jnp.dot(marks, upper, preferred_element_type=f32)
    ends = jnp.cumsum(inner[:, -1])
    cend = jnp.concatenate([jnp.zeros((1,), f32), ends])
    counts = inner + cend[:-1, None]
    cnt_col = counts.reshape(tokens, 1)
    cnt_row = counts.reshape(1, tokens)

    norms = jnp.concatenate(
        [norm_gains, norm_biases, jnp.broadcast_to(flag, (rows, 1)), jnp.zeros((rows, 123), bf16)],
        axis=1,
    )
    first = stream_rows(stream_send(jnp.concatenate([w_qkv, w_feat, norms], axis=1), depth), depth)
    first = Spread(first, n_seq, False).near()
    up = jnp.concatenate([w_fc, w_out], axis=1)
    first.far_halves()
    up = stream_send(after(up, first.block), depth)
    first_blocks = first.cores()
    up = stream_rows([after(a, first_blocks[0]) for a in up], depth)
    up = Spread(up, n_seq, True).near(first_blocks[0])
    proj_pieces = stream_send(after(w_proj, first_blocks[1], up.block), depth)
    me_first = after(me_arr, up.block)

    packed = (pairs + 1, 128, 128)
    full = (heads, 128, 128)
    h_one, keys, vals, phi_k, state, gb, feat_all = pl.pallas_call(
        functools.partial(keys_body, n_seq, pairs),
        name="keys",
        cost_estimate=cost(22),
        grid=(tokens // TK,),
        in_specs=[smem(), smem(), rows_spec(TK, width), rows_spec(TK, 1)] + [whole()] * 2,
        out_specs=[rows_spec(TK, width)] * 3
        + [rows_spec(TK, 2 * width), full_spec(packed), full_spec((8, width)), full_spec((width, 128))],
        out_shape=[sds((tokens, width), bf16)] * 3
        + [sds((tokens, 2 * width), bf16), sds(packed, bf16), sds((8, width), f32), sds((width, 128), bf16)],
        scratch_shapes=[
            pltpu.VMEM((width, 2 * width + 256), bf16),
            pltpu.VMEM((pairs, 128, 256), bf16),
            pltpu.VMEM(full, f32),
            dma(2, n_seq),
        ],
        compiler_params=cparams(),
    )(me_first, cend, x, cnt_col, *first_blocks)
    level = lax.axis_index("stream")
    flags = gb[4].reshape(n_seq, depth, rows)[:, :, 0]
    keeps = lax.dynamic_index_in_dim(flags, level, 1, False)
    spread = Spread(state, n_seq, False).near_all()
    up.far_halves(gb)
    proj = Spread(stream_rows([after(a, gb) for a in proj_pieces], depth), n_seq, False).near()
    part_blk = nblk // 2
    local = []
    for part in range(2):
        base = part * part_blk

        def here(size, cols):
            return pl.BlockSpec((size, cols), lambda i: (base + i, 0))

        blocks_out = [
            sds((tokens, width), bf16), sds((tokens, 2 * width), bf16), sds((tokens, width), f32),
            sds((tokens, width), f32), sds((nblk,) + full, bf16),
        ]
        if part:
            me_two = after(me_arr, up_blocks[0], *[proj.found[b] for b in proj.bits], *spread.found.values())
        else:
            me_two = after(me_arr, proj.block, state, after(up.found[up.bits[0]], gb))
        local = pl.pallas_call(
            functools.partial(local_body, base, pairs),
            name="local",
            cost_estimate=cost(15),
            grid=(part_blk,),
            in_specs=[
                smem(), smem(), here(BT, width), here(BT, 2 * width), here(BT, width), here(BT, 1),
                pl.BlockSpec((1, BT), lambda i: (0, base + i)), full_spec((width, 128)),
            ]
            + [whole()] * 2
            + ([full_spec(full)] + [whole()] * 5 if part else []),
            out_specs=[
                here(BT, width), here(BT, 2 * width), here(BT, width), here(BT, width),
                pl.BlockSpec((1,) + full, lambda i: (base + i, 0, 0, 0)), full_spec(full),
            ],
            out_shape=blocks_out + [sds(full, f32)],
            scratch_shapes=[
                pltpu.VMEM((width, width), bf16),
                pltpu.VMEM((pairs, 128, 256), bf16),
                dma(n_seq),
            ],
            input_output_aliases={11 + i: i for i in range(5)} if part else {},
            compiler_params=cparams(),
        )(
            me_two, cend, h_one, phi_k, vals, cnt_col, cnt_row, feat_all, *first_blocks,
            *([local[5]] + list(local[:5]) if part else []),
        )
        if part == 0:
            event = local[5]
            proj.far(event)
            up_blocks = up.cores(event)
    queries, phi_q, num, den, srel, event = local
    states = spread.cores(event)
    proj_blocks = proj.cores(event)

    y, att, h_two, act, d_fc, d_att, d_mid, dd, s_in, g_state, sums = pl.pallas_call(
        functools.partial(middle_body, n_seq, pairs),
        name="middle",
        cost_estimate=cost(43),
        grid=(tokens // TM,),
        in_specs=[
            smem(), smem(), rows_spec(TM, width), rows_spec(TM, width), rows_spec(TM, width),
            rows_spec(TM, width), rows_spec(TM, 2 * width), rows_spec(TM, 1), full_spec((8, width)),
        ]
        + [whole()] * 6,
        out_specs=[
            rows_spec(TM, width), rows_spec(TM, width), rows_spec(TM, width), rows_spec(TM, hidden),
            rows_spec(TM, hidden), rows_spec(TM, width), rows_spec(TM, width), rows_spec(TM, 2 * width),
            full_spec(full), full_spec(packed), full_spec((8, width)),
        ],
        out_shape=[
            sds((tokens, width), bf16), sds((tokens, width), bf16), sds((tokens, width), bf16),
            sds((tokens, hidden), bf16), sds((tokens, hidden), bf16), sds((tokens, width), bf16),
            sds((tokens, width), f32), sds((tokens, 2 * width), bf16), sds(full, bf16), sds(packed, bf16),
            sds((8, width), f32),
        ],
        scratch_shapes=[
            pltpu.VMEM((width, width), bf16),
            pltpu.VMEM((width, hidden), bf16),
            pltpu.VMEM((hidden, width), bf16),
            pltpu.VMEM((TM, width), f32),
            pltpu.VMEM(full, f32),
            pltpu.VMEM((2, n_seq // 2) + packed, bf16),
            dma(4, n_seq),
        ],
        compiler_params=cparams(),
    )(
        me_arr, keeps, x, dy, num, den, phi_q, cnt_col, gb,
        *up_blocks, *proj_blocks, *states,
    )

    spread = Spread(g_state, n_seq, True).near_all()
    norm_two = jnp.stack([sums[3], sums[4]], axis=1).astype(bf16)
    norm_two = jnp.concatenate([norm_two, jnp.zeros((width, 126), bf16)], axis=1)
    nbits = n_seq.bit_length() - 1
    g_fc = mm_f(h_two, d_fc).astype(bf16)
    g_out = mm_f(att, d_att).astype(bf16)
    red_fc = Reduce([g_fc, g_out, norm_two], n_seq, depth, [0] + list(range(1, nbits))[::-1]).send()
    g_states = spread.cores(red_fc.out)
    g_proj = mm_f(after(act, red_fc.out, g_states[0]), dy).astype(bf16)
    red_proj = Reduce([g_proj], n_seq, depth).send()
    red_fc.add(red_proj.out).send()
    red_proj.add(red_fc.out).send()
    me_back = after(me_arr, red_proj.out, red_fc.out)
    groups = 2
    some = pairs // groups
    part = some * 128
    d_qkv, g_feat = [], []
    for g in range(groups):

        def spec(cols):
            return pl.BlockSpec((BT, cols), lambda i: (nblk - 1 - i, g))

        def one_group(shape):
            return pl.BlockSpec(shape, lambda i: (g,) + (0,) * (len(shape) - 1))

        one = (2 * some, 128, 128)
        d_one, g_one = pl.pallas_call(
            functools.partial(back_body, g * some, some, pairs),
            name="back",
            cost_estimate=cost(19),
            grid=(nblk,),
            in_specs=[
                smem(), smem(), smem(), spec(part), spec(part), spec(part), spec(2 * part), spec(2 * part),
                spec(2 * part), pl.BlockSpec((1,) + one, lambda i: (nblk - 1 - i, g, 0, 0)), one_group(one),
                rows_spec(BT, 1, nblk), pl.BlockSpec((1, BT), lambda i: (0, nblk - 1 - i)),
                one_group((part, 128)),
            ]
            + [whole()] * 2,
            out_specs=[rows_spec(BT, 3 * part, nblk), full_spec((part, 128))],
            out_shape=[sds((tokens, 3 * part), bf16), sds((part, 128), bf16)],
            scratch_shapes=[
                pltpu.VMEM((some, 128, 256), bf16),
                pltpu.VMEM((some, 128, 256), bf16),
                pltpu.VMEM(one, f32),
                pltpu.VMEM((some, 128, 256), f32),
                pltpu.VMEM((some, 128, 256), f32),
                pltpu.VMEM((2, n_seq // 2) + packed, bf16),
                dma(n_seq),
            ],
            compiler_params=cparams(),
        )(
            me_back, keeps, cend, queries, keys, vals, phi_q, phi_k, dd, srel, s_in, cnt_col, cnt_row,
            feat_all, *g_states,
        )
        d_qkv.append(d_one)
        g_feat.append(g_one)
        if g == 0:
            red_proj.add(d_one).send()
            me_back = after(me_arr, red_proj.out)

    last = d_qkv[-1]
    g_qkv = [mm_f(h_one, d).astype(bf16) for d in d_qkv]
    red_two = Reduce(g_qkv + [jnp.concatenate(g_feat, axis=0)], n_seq, depth).send()
    red_fc.add(red_two.out).send()
    red_proj.add(red_fc.out).send_stream()
    me_late = after(me_arr, red_proj.out, red_fc.out)
    dx, sums_one = pl.pallas_call(
        functools.partial(enter_body, groups),
        name="enter",
        cost_estimate=cost(11),
        grid=(tokens // TM,),
        in_specs=[smem(), rows_spec(TM, width), rows_spec(TM, width), full_spec((8, width))]
        + [rows_spec(TM, 3 * part)] * groups
        + [whole()] * 2,
        out_specs=[rows_spec(TM, width), full_spec((8, width))],
        out_shape=[sds((tokens, width), f32), sds((8, width), f32)],
        scratch_shapes=[pltpu.VMEM((width, 3 * width), bf16), dma(2, n_seq)],
        compiler_params=cparams(),
    )(me_late, x, d_mid, gb, *d_qkv, *first_blocks)
    norm_one = jnp.stack([sums_one[0], sums_one[1]], axis=1).astype(bf16)
    norm_one = jnp.concatenate([norm_one, jnp.zeros((width, 126), bf16)], axis=1)
    red_norm = Reduce([norm_one], n_seq, depth).send()
    grad_proj = red_proj.done(dx)
    red_a, red_b = red_two.add(grad_proj).cut((groups * 3 * part + 256) // 2)
    red_a.send()
    red_norm.add(red_a.out)
    red_b.cur = [beside(red_b.cur + red_norm.cur)]
    red_b.send()
    red_fc.add(red_a.out, red_b.out).send_stream()
    while red_a.order:
        red_a.add().send()
        red_b.add().send()
    tail = Reduce(red_a.add().cur + red_b.add().cur, n_seq, depth, [], []).send_stream()
    grad_up = red_fc.done(tail.out)
    squares = sum(
        jnp.sum(after(stack[:, pairs, :3, 126:], tail.out).astype(f32), axis=(0, 2))
        for stack in g_states
    )
    branch_rms = jnp.sqrt(squares / (tokens * n_seq * width)).reshape(1, 3)
    tail = tail.done()
    grads = [tail[:, g * 3 * part : (g + 1) * 3 * part] for g in range(groups)]
    grad_feat = tail[:, groups * 3 * part : groups * 3 * part + 128]
    norm_one = tail[:, groups * 3 * part + 128 :]
    grad_fc = grad_up[:, :hidden]
    grad_out = grad_up[:, hidden:]
    grad_qkv = jnp.concatenate(
        [grads[g][:, i * part : (i + 1) * part] for i in range(3) for g in range(groups)], axis=1
    )
    return (
        y[None],
        dx[None],
        jnp.concatenate([norm_one[:, 0:1], grad_out[:, width : width + 1]], axis=1),
        jnp.concatenate([norm_one[:, 1:2], grad_out[:, width + 1 : width + 2]], axis=1),
        grad_qkv,
        grad_feat,
        grad_out[:, :width],
        grad_fc,
        grad_proj,
        branch_rms,
    )


def solution(mesh):
    both = P(("seq", "stream"), None)
    acts = P("stream", "seq", None)
    placed = (acts, P("stream", "seq"), both, both, both, both, both, both, both, acts)
    return jax.shard_map(
        functools.partial(shards, mesh.shape["seq"], mesh.shape["stream"]),
        mesh=mesh,
        in_specs=placed,
        out_specs=(acts, acts, both, both, both, both, both, both, both, P("stream", None)),
        check_vma=False,
    )
```

```python
import functools

import jax
import jax.numpy as jnp
from jax import lax
from jax.experimental import pallas as pl
from jax.experimental.pallas import tpu as pltpu
from jax.sharding import PartitionSpec as P

BT = 256
GF = 6
TK = 512
TM = 256
epsilon = 1e-05
f32 = jnp.float32
bf16 = jnp.bfloat16
GC = 0.7978845608028654
GA = 0.044715


def mm(a, b):
    return jnp.dot(a, b, preferred_element_type=f32)


def mm_t(a, b):
    return lax.dot_general(a, b, (((1,), (1,)), ((), ())), preferred_element_type=f32)


def mm_f(a, b):
    return lax.dot_general(a, b, (((0,), (0,)), ((), ())), preferred_element_type=f32)


def xor_send(arr, size, mask):
    return lax.ppermute(arr, "seq", [(i, i ^ mask) for i in range(size)])


def after(arr, *deps):
    return lax.optimization_barrier((arr,) + deps)[0]


def stream_send(shard, depth):
    return [shard] + [
        lax.ppermute(shard, "stream", [(i, (i + d) % depth) for i in range(depth)])
        for d in range(1, depth)
    ]


def stream_rows(pieces, depth):
    shard = pieces[0]
    ring = pieces[::-1]
    place = lax.axis_index("stream")
    rows = shard.shape[0]
    both = jnp.concatenate(ring + ring, axis=0)
    return lax.dynamic_slice_in_dim(both, (depth - 1 - place) * rows, depth * rows, 0)


class Spread:
    def __init__(self, block, size, flip):
        self.size = size
        bits = [1 << b for b in range(1, size.bit_length() - 1)]
        self.bits = bits[::-1] if flip else bits
        self.block = block
        self.found = {0: block}

    def near(self, *deps):
        block = after(self.block, *deps) if deps else self.block
        for bit in self.bits:
            self.found[bit] = xor_send(block, self.size, bit)
        return self

    def near_all(self):
        for r in range(2, self.size, 2):
            self.found[r] = xor_send(self.block, self.size, r)
        return self

    def far(self, *deps):
        for bit in self.bits:
            for r in list(self.found):
                if r ^ bit not in self.found and r < 2 * max(self.bits):
                    src = self.found[r]
                    self.found[r ^ bit] = xor_send(after(src, *deps) if deps else src, self.size, bit)
        return self

    def far_halves(self, *deps):
        one, two = self.bits[:2]
        half = self.block.shape[1] // 256 * 128
        srcs = (self.found[one], self.found[two])
        if deps:
            srcs = lax.optimization_barrier(srcs + deps)[:2]
        self.cuts = [srcs[0][:, :half], srcs[1][:, half:]]
        left = xor_send(self.cuts[0], self.size, two)
        right = xor_send(self.cuts[1], self.size, one)
        self.found[one ^ two] = jnp.concatenate([left, right], axis=1)
        return self.far(*deps)

    def cores(self, *deps):
        parts = [self.found[2 * r] for r in range(self.size // 2)]
        if deps:
            parts = lax.optimization_barrier(tuple(parts) + deps)[: len(parts)]
        stack = jnp.stack(parts)
        return [stack, xor_send(stack, self.size, 1)]


def beside(parts):
    return parts[0] if len(parts) == 1 else jnp.concatenate(parts, axis=-1)


class Reduce:
    def __init__(self, grads, size, depth, order=None, rest=None):
        self.size, self.depth = size, depth
        nbits = size.bit_length() - 1
        self.rest = list(range(nbits))[::-1] if rest is None else list(rest)
        self.order = list(range(nbits)) if order is None else list(order)
        self.cur = [
            g.reshape([2] * len(self.rest) + [g.shape[0] // 2 ** len(self.rest), g.shape[1]])
            if g.ndim == 2
            else g
            for g in grads
        ]

    def send(self):
        place = lax.axis_index("seq")
        bit = self.order.pop(0)
        axis = self.rest.index(bit)
        own = (place >> bit) & 1
        self.out = beside([lax.dynamic_index_in_dim(c, 1 - own, axis, False) for c in self.cur])
        self.kept = [lax.dynamic_index_in_dim(c, own, axis, False) for c in self.cur]
        self.flight = xor_send(self.out, self.size, 1 << bit)
        self.rest.pop(axis)
        return self

    def add(self, *deps):
        got = after(self.flight, *deps) if deps else self.flight
        self.cur = [(beside(self.kept).astype(f32) + got.astype(f32)).astype(bf16)]
        return self

    def cut(self, at):
        (cur,) = self.cur
        parts = [
            Reduce([cur[..., :at]], self.size, self.depth, self.order, self.rest),
            Reduce([cur[..., at:]], self.size, self.depth, self.order[::-1], self.rest),
        ]
        return parts

    def send_stream(self):
        while self.order:
            self.send().add()
        depth = self.depth
        level = lax.axis_index("stream")
        cur = beside(self.cur)
        self.out = cur
        cur = cur.reshape(depth, cur.shape[0] // depth, cur.shape[1])
        self.total = lax.dynamic_index_in_dim(cur, level, 0, False).astype(f32)
        self.flights = []
        for d in range(1, depth):
            piece = lax.dynamic_index_in_dim(cur, (level + d) % depth, 0, False)
            self.flights.append(
                lax.ppermute(piece, "stream", [(i, (i + d) % depth) for i in range(depth)])
            )
        return self

    def done(self, *deps):
        total = self.total
        for f in self.flights:
            total = total + (after(f, *deps) if deps else f).astype(f32)
        return total


def lanes(shape):
    return lax.broadcasted_iota(jnp.int32, shape, len(shape) - 1)


def block_ones(width, part):
    r = lax.broadcasted_iota(jnp.int32, (width, width), 0) // part
    c = lax.broadcasted_iota(jnp.int32, (width, width), 1) // part
    return jnp.where(r == c, 1.0, 0.0).astype(bf16)


def fetch_start(stacks, dest, me, sems, col=0, width=None, at=0):
    half = stacks[0].shape[0]
    rows = dest.shape[0] // (2 * half)
    width = width or stacks[0].shape[2]
    copies = []
    for c, ref in enumerate(stacks):
        for r in range(half):
            off = pl.multiple_of((me ^ (2 * r + c)) * rows, 8)
            copy = pltpu.make_async_copy(
                ref.at[r, :, pl.ds(col, width)],
                dest.at[pl.ds(off, rows), pl.ds(at, width)],
                sems.at[2 * r + c],
            )
            copy.start()
            copies.append(copy)
    return copies


def pair_maps(feat_ref, dest, pairs, which):
    width = 128
    lane = lanes((width, width))
    row = lax.broadcasted_iota(jnp.int32, (width, width), 0)
    for p in range(pairs):
        both = feat_ref[pl.ds(p * width, width), :].astype(f32)
        half = width // 2
        other = pltpu.roll(both, half, 1)
        if which == 0:
            signed = jnp.where(lane < half, both, -other)
        else:
            signed = jnp.where(lane < half, other, -both)
        dest[p, :, pl.ds(0, width)] = jnp.where(row < half, signed, 0.0).astype(bf16)
        dest[p, :, pl.ds(width, width)] = jnp.where(row >= half, signed, 0.0).astype(bf16)


def features(logits_of, ones):
    halves = [one[:, j * 128 : (j + 1) * 128] for one in logits_of for j in range(2)]
    low = lanes(halves[0].shape) < 64
    tops = [
        (
            jnp.max(jnp.where(low, one, -jnp.inf), axis=1, keepdims=True),
            jnp.max(jnp.where(low, -jnp.inf, one), axis=1, keepdims=True),
        )
        for one in halves
    ]
    exps = [jnp.exp(one - jnp.where(low, *top)) for one, top in zip(halves, tops)]
    exps = [jnp.concatenate(exps[2 * i : 2 * i + 2], axis=1) for i in range(len(logits_of))]
    sums = [mm(e.astype(bf16), ones) for e in exps]
    return [(e / t).astype(bf16) for e, t in zip(exps, sums)]


def augmented(two):
    low = lanes(two.shape) < 64
    one = jnp.ones_like(two)
    return jnp.where(low, two, one), jnp.where(low, one, two)


def pack_states(get, dest, pairs, zsum):
    shape = (128, 128)
    lane = lanes(shape)
    low = lane < 64
    zt = jnp.zeros(shape, f32)
    for p in range(pairs):
        a, b = get(2 * p), get(2 * p + 1)
        dest[p] = jnp.where(low, a, b).astype(bf16)
        if zsum:
            za = jnp.sum(jnp.where(low, 0.0, a), axis=1, keepdims=True)
            zb = jnp.sum(jnp.where(low, b, 0.0), axis=1, keepdims=True)
        else:
            za, zb = a, b
        zt = jnp.where(lane == 64 + 2 * p, za, zt)
        zt = jnp.where(lane == 2 * p + 1, zb, zt)
    dest[pairs] = zt.astype(bf16)


def unpack_states(me, keep_ref, blocks, put, base, count, pairs, back):
    shape = (128, 128)
    lane = lanes(shape)
    low = lane < 64
    size = 2 * blocks.shape[1]
    coefs = [None]
    for r in range(1, size):
        j = me ^ r
        c = jnp.where(j > me if back else j < me, 1.0, 0.0)
        for i in range(size):
            between = ((i > me) & (i < j)) if back else ((i > j) & (i < me))
            c = c * jnp.where(between, keep_ref[i], 1.0)
        coefs.append(c)

    def total(i):
        acc = jnp.zeros(shape, f32)
        for r in range(1, size):
            acc = acc + coefs[r] * blocks[r % 2, r // 2, i].astype(f32)
        return acc

    zt = total(pairs)
    for q in range(count):
        p = base + q
        two = total(p)
        za = jnp.sum(jnp.where(lane == 64 + 2 * p, zt, 0.0), axis=1, keepdims=True)
        zb = jnp.sum(jnp.where(lane == 2 * p + 1, zt, 0.0), axis=1, keepdims=True)
        if back:
            put(2 * q, jnp.where(low, two, jnp.where(lane == 64, za, 0.0)))
            put(2 * q + 1, jnp.where(low, jnp.where(lane == 0, zb, 0.0), two))
        else:
            put(2 * q, jnp.where(low, two, za))
            put(2 * q + 1, jnp.where(low, zb, two))


def normed(values, gain, bias):
    mean = jnp.mean(values, axis=1, keepdims=True)
    cent = values - mean
    rstd = lax.rsqrt(jnp.mean(cent * cent, axis=1, keepdims=True) + epsilon)
    hat = cent * rstd
    return hat * gain + bias, hat, rstd


def normed_back(grad, hat, rstd, gain):
    dhat = grad * gain
    return rstd * (
        dhat
        - jnp.mean(dhat, axis=1, keepdims=True)
        - hat * jnp.mean(dhat * hat, axis=1, keepdims=True)
    )


def keys_body(n_seq, pairs, me_ref, cend_ref, x_ref, cnt_ref, *refs):
    width = x_ref.shape[1]
    wl = refs[:2]
    (h_ref, k_ref, v_ref, phi_ref, st_ref, gb_ref, feat_ref, w1, maps, state, sems) = refs[2:]
    step = pl.program_id(0)

    @pl.when(step == 0)
    def _():
        me = me_ref[0]
        copies = fetch_start(wl, w1, me, sems.at[0], width, 2 * width + 256)
        for c in copies:
            c.wait()
        gb_ref[...] = w1[:, pl.ds(2 * width + 128, 128)].astype(f32).T[:8]
        feat_ref[...] = w1[:, pl.ds(2 * width, 128)]
        pair_maps(feat_ref, maps, pairs, 1)
        state[...] = jnp.zeros_like(state)

    gb = gb_ref[...]
    out, _, _ = normed(x_ref[...].astype(f32), gb[0:1], gb[2:3])
    h1 = out.astype(bf16)
    h_ref[...] = h1
    keys = mm(h1, w1[:, pl.ds(0, width)]).astype(bf16)
    vals = mm(h1, w1[:, pl.ds(width, width)]).astype(bf16)
    k_ref[...] = keys
    v_ref[...] = vals
    ones = block_ones(256, 64)
    last = cend_ref[cend_ref.shape[0] - 1]
    used = jnp.where(cnt_ref[...] == last, 1.0, 0.0).astype(bf16)
    for g in range(0, pairs, GF):
        group = range(g, min(g + GF, pairs))
        phis = features([mm(keys[:, p * 128 : (p + 1) * 128], maps[p]) for p in group], ones)
        for p, phi in zip(group, phis):
            phi_ref[:, pl.ds(p * 256, 256)] = phi
            va, vb = augmented(vals[:, p * 128 : (p + 1) * 128])
            state[2 * p] += mm_f(phi[:, :128], va * used)
            state[2 * p + 1] += mm_f(phi[:, 128:], vb * used)

    @pl.when(step == pl.num_programs(0) - 1)
    def _():
        pack_states(lambda h: state[h], st_ref, pairs, False)


def local_body(base, pairs, me_ref, cend_ref, h_ref, phik_ref, v_ref, cnt_ref, row_ref, feat_ref, *refs):
    wq = refs[:2]
    (q_ref, phiq_ref, num_ref, den_ref, srel_ref, state, w1, maps, sems) = refs[-9:]
    step = pl.program_id(0)
    width = h_ref.shape[1]

    @pl.when(step == 0)
    def _():
        copies = fetch_start(wq, w1, me_ref[0], sems, 0, width)
        pair_maps(feat_ref, maps, pairs, 0)
        if base:
            state[...] = refs[2][...]
        else:
            state[...] = jnp.zeros_like(state)
        for c in copies:
            c.wait()

    queries = mm(h_ref[...], w1[...]).astype(bf16)
    q_ref[...] = queries
    ones = block_ones(256, 64)
    size = h_ref.shape[0]
    cnt = cnt_ref[...]
    first, last = cend_ref[base + step], cend_ref[base + step + 1]
    row_id = lax.broadcasted_iota(jnp.int32, (size, size), 0)
    mask = (row_id >= lanes((size, size))) & (cnt == row_ref[...])
    before = jnp.where(cnt == first, 1.0, 0.0).astype(bf16)
    after = jnp.where(cnt == last, 1.0, 0.0).astype(bf16)
    keep = jnp.where(first == last, 1.0, 0.0)
    low = lanes((size, 128)) < 64
    for g in range(0, pairs, GF):
        group = range(g, min(g + GF, pairs))
        phis = features([mm(queries[:, p * 128 : (p + 1) * 128], maps[p]) for p in group], ones)
        for p, phi in zip(group, phis):
            phiq_ref[:, pl.ds(p * 256, 256)] = phi
        pqs = [phi[:, j * 128 : (j + 1) * 128] for phi in phis for j in range(2)]
        heads = [2 * p + j for p in group for j in range(2)]
        pks = [phik_ref[:, pl.ds(h * 128, 128)] for h in heads]
        scores = [jnp.where(mask, mm_t(pq, pk), 0.0).astype(bf16) for pq, pk in zip(pqs, pks)]
        val_of = [v for p in group for v in augmented(v_ref[:, p * 128 : (p + 1) * 128])]
        res = []
        for h, pq, pk, sc, val in zip(heads, pqs, pks, scores, val_of):
            st = state[h]
            st_b = st.astype(bf16)
            srel_ref[0, h] = st_b
            res.append(mm(sc, val) + mm(pq * before, st_b))
            state[h] = keep * st + mm_f(pk, val * after)
        for i, p in enumerate(group):
            two = pl.ds(p * 128, 128)
            num_ref[:, two] = jnp.where(low, res[2 * i], res[2 * i + 1])
            den_ref[:, two] = pltpu.roll(jnp.where(low, res[2 * i + 1], res[2 * i]), 64, 1)


def middle_body(
    n_seq, pairs, me_ref, keep_ref, x_ref, dy_ref, num_ref, den_ref, phiq_ref, cnt_ref, gb_ref, *refs
):
    width = x_ref.shape[1]
    wf, wp, sts = (refs[2 * i : 2 * i + 2] for i in range(3))
    (
        y_ref, o_ref, h_ref, a_ref, df_ref, dat_ref, dr_ref, dd_ref, sin_ref, gst_ref, sum_ref,
        w_out, w_fc, w_proj, rden, state, stv, sems,
    ) = refs[6:]
    step = pl.program_id(0)
    chunk = 768
    hidden = w_fc.shape[1]
    size = x_ref.shape[0]

    @pl.when(step == 0)
    def _():
        me = me_ref[0]
        st_copies = []
        for c in range(2):
            st_copies.append(pltpu.make_async_copy(sts[c], stv.at[c], sems.at[3, c]))
            st_copies[c].start()
        copies = fetch_start(wf, w_out, me, sems.at[0], hidden, width)
        copies += fetch_start(wf, w_fc, me, sems.at[1], 0, hidden)
        copies += fetch_start(wp, w_proj, me, sems.at[2])
        for c in st_copies:
            c.wait()

        def put(h, value):
            sin_ref[h] = value.astype(bf16)

        unpack_states(me, keep_ref, stv, put, 0, pairs, pairs, False)
        state[...] = jnp.zeros_like(state)
        sum_ref[...] = jnp.zeros_like(sum_ref)
        for c in copies:
            c.wait()

    gb = gb_ref[...]
    low = lanes((size, 128)) < 64
    start = jnp.where(cnt_ref[...] == 0.0, 1.0, 0.0)
    start_b = start.astype(bf16)
    res = [mm(phiq_ref[:, pl.ds(h * 128, 128)], sin_ref[h]) for h in range(2 * pairs)]
    for p in range(pairs):
        two = pl.ds(p * 128, 128)
        ra, rb = res[2 * p], res[2 * p + 1]
        num = num_ref[:, two] + start * jnp.where(low, ra, rb)
        den = den_ref[:, two] + start * pltpu.roll(jnp.where(low, rb, ra), 64, 1)
        inv = 1.0 / den
        rden[:, two] = inv
        o_ref[:, two] = (num * inv).astype(bf16)
    x = x_ref[...].astype(f32)
    attn = mm(o_ref[...], w_out[...])
    mid = x + attn
    out, hat, rstd = normed(mid, gb[1:2], gb[3:4])
    h2 = out.astype(bf16)
    h_ref[...] = h2
    dy_b = dy_ref[...]
    branch = jnp.zeros((size, width), f32)
    dh2 = jnp.zeros((size, width), f32)
    for c in range(w_fc.shape[1] // chunk):
        cols = pl.ds(c * chunk, chunk)
        fc = mm(h2, w_fc[:, cols])
        square = fc * fc
        tan = jnp.tanh(fc * (GC + GC * GA * square))
        half = 0.5 + 0.5 * tan
        act = (fc * half).astype(bf16)
        a_ref[:, cols] = act
        branch = branch + mm(act, w_proj[cols, :])
        slope = half + fc * (1.0 - half) * half * (2.0 * GC + 6.0 * GC * GA * square)
        dfc = (mm_t(dy_b, w_proj[cols, :]) * slope).astype(bf16)
        df_ref[:, cols] = dfc
        dh2 = dh2 + mm_t(dfc, w_fc[:, cols])
    y = mid + branch
    y_ref[...] = y.astype(bf16)
    sum_ref[0:1] += jnp.sum(attn * attn, axis=0, keepdims=True)
    sum_ref[1:2] += jnp.sum(branch * branch, axis=0, keepdims=True)
    sum_ref[2:3] += jnp.sum(y * y, axis=0, keepdims=True)
    sum_ref[3:4] += jnp.sum(dh2 * hat, axis=0, keepdims=True)
    sum_ref[4:5] += jnp.sum(dh2, axis=0, keepdims=True)
    dr = dy_b.astype(f32) + normed_back(dh2, hat, rstd, gb[1:2])
    dr_ref[...] = dr
    dat = dr.astype(bf16)
    dat_ref[...] = dat
    d_o = mm_t(dat, w_out[...])
    ones = block_ones(256, 64)
    lane = lanes((size, 128))
    quads = range(pairs // 2)
    fours = [pl.ds(q * 256, 256) for q in quads]
    d_os = [d_o[:, q * 256 : (q + 1) * 256] for q in quads]
    prods = [d * o_ref[:, c].astype(f32) for d, c in zip(d_os, fours)]
    his = [a.astype(bf16) for a in prods]
    los = [(a - hi.astype(f32)).astype(bf16) for a, hi in zip(prods, his)]
    ddens = [-(mm(hi, ones) + mm(lo, ones)) * rden[:, c] for hi, lo, c in zip(his, los, fours)]
    dnums = [(d * rden[:, c]).astype(bf16) for d, c in zip(d_os, fours)]
    near = lane & 63
    for p in range(pairs):
        sub = slice((p % 2) * 128, (p % 2 + 1) * 128)
        dd = pltpu.roll(ddens[p // 2][:, sub], 64, 1)
        dhi = dd.astype(bf16)
        dlo = (dd - dhi.astype(f32)).astype(bf16)
        aux = jnp.where(near == 0, dhi.astype(f32), jnp.where(near == 1, dlo.astype(f32), 0.0)).astype(bf16)
        dn = dnums[p // 2][:, sub]
        dd_ref[:, pl.ds(p * 256, 128)] = jnp.where(low, dn, aux)
        dd_ref[:, pl.ds(p * 256 + 128, 128)] = jnp.where(low, aux, dn)
    for h in range(2 * pairs):
        own = pl.ds(h * 128, 128)
        state[h] += mm_f(phiq_ref[:, own], dd_ref[:, own] * start_b)

    @pl.when(step == pl.num_programs(0) - 1)
    def _():
        pack_states(lambda h: state[h], gst_ref, pairs, True)
        total = jnp.sum(sum_ref[...], axis=1, keepdims=True)
        high = total.astype(bf16).astype(f32)
        place = lanes((8, 128))
        tile = jnp.where(place == 126, high, jnp.where(place == 127, total - high, 0.0))
        tile = jnp.concatenate([tile, jnp.zeros_like(tile)], axis=0)
        top = gst_ref[pairs, pl.ds(0, 16), :].astype(f32)
        gst_ref[pairs, pl.ds(0, 16), :] = (top + tile).astype(bf16)


def back_body(
    base, pairs, all_pairs, me_ref, keep_ref, cend_ref, q_ref, k_ref, v_ref, phiq_ref, phik_ref, dd_ref, srel_ref, sin_ref,
    cnt_ref, row_ref, feat_ref, *refs
):
    sts = refs[:2]
    (dqkv_ref, gfeat_ref, mapq, mapk, state, gq, gk, stv, sems) = refs[2:]
    step = pl.program_id(0)
    nblk = pl.num_programs(0)
    here = nblk - 1 - step

    @pl.when(step == 0)
    def _():
        copies = []
        for c in range(2):
            copies.append(pltpu.make_async_copy(sts[c], stv.at[c], sems.at[c]))
            copies[c].start()
        pair_maps(feat_ref, mapq, pairs, 0)
        pair_maps(feat_ref, mapk, pairs, 1)
        gq[...] = jnp.zeros_like(gq)
        gk[...] = jnp.zeros_like(gk)
        for c in copies:
            c.wait()

        def put(h, value):
            state[h] = value

        unpack_states(me_ref[0], keep_ref, stv, put, base, pairs, all_pairs, True)

    size = q_ref.shape[0]
    width = q_ref.shape[1]
    cnt = cnt_ref[...]
    first, last = cend_ref[here], cend_ref[here + 1]
    row_id = lax.broadcasted_iota(jnp.int32, (size, size), 0)
    col_id = lanes((size, size))
    same = cnt == row_ref[...]
    mask = (row_id >= col_id) & same
    mask_t = (col_id >= row_id) & same
    before = jnp.where(cnt == first, 1.0, 0.0).astype(bf16)
    after = jnp.where(cnt == last, 1.0, 0.0).astype(bf16)
    keep = jnp.where(first == last, 1.0, 0.0)
    opened = jnp.where(first == 0.0, 1.0, 0.0)
    ones = block_ones(256, 64)
    low = lanes((size, 128)) < 64
    heads = range(2 * pairs)
    cols = [pl.ds(h * 128, 128) for h in heads]
    vals = [v for p in range(pairs) for v in augmented(v_ref[:, pl.ds(p * 128, 128)])]
    scores_t = [
        jnp.where(mask_t, mm_t(phik_ref[:, c], phiq_ref[:, c]), 0.0).astype(bf16) for c in cols
    ]
    dsc = [jnp.where(mask, mm_t(dd_ref[:, c], v), 0.0).astype(bf16) for c, v in zip(cols, vals)]
    dsc_t = [jnp.where(mask_t, mm_t(v, dd_ref[:, c]), 0.0).astype(bf16) for c, v in zip(cols, vals)]
    sts = [
        (srel_ref[0, h].astype(f32) + opened * sin_ref[h].astype(f32)).astype(bf16) for h in heads
    ]
    dsts = [state[h].astype(bf16) for h in heads]
    ddws = [dd_ref[:, c] * before for c in cols]
    dphi_q = [mm(dsc[h], phik_ref[:, cols[h]]) + mm_t(ddws[h], sts[h]) for h in heads]
    dphi_k = [mm(dsc_t[h], phiq_ref[:, cols[h]]) + mm_t(vals[h] * after, dsts[h]) for h in heads]
    dvs = [mm(scores_t[h], dd_ref[:, cols[h]]) + mm(phik_ref[:, cols[h]] * after, dsts[h]) for h in heads]
    for h in heads:
        state[h] = keep * state[h] + mm_f(phiq_ref[:, cols[h]], ddws[h])
    for p in range(pairs):
        dqkv_ref[:, pl.ds(2 * width + p * 128, 128)] = jnp.where(low, dvs[2 * p], dvs[2 * p + 1]).astype(bf16)
    for phi_ref, dphi, rows_ref, maps, acc, base_col in (
        (phiq_ref, dphi_q, q_ref, mapq, gq, 0),
        (phik_ref, dphi_k, k_ref, mapk, gk, width),
    ):
        phis = [phi_ref[:, pl.ds(p * 256, 256)].astype(f32) for p in range(pairs)]
        dphis = [jnp.concatenate(dphi[2 * p : 2 * p + 2], axis=1) for p in range(pairs)]
        totals = [mm((phi * d).astype(bf16), ones) for phi, d in zip(phis, dphis)]
        dlogs = [(phi * (d - t)).astype(bf16) for phi, d, t in zip(phis, dphis, totals)]
        for p in range(pairs):
            two = pl.ds(p * 128, 128)
            dqkv_ref[:, pl.ds(base_col + p * 128, 128)] = mm_t(dlogs[p], maps[p]).astype(bf16)
            acc[p] += mm_f(rows_ref[:, two], dlogs[p])

    @pl.when(step == nblk - 1)
    def _():
        lane = lanes((128, 128))
        row = lax.broadcasted_iota(jnp.int32, (128, 128), 0)
        for p in range(pairs):
            outs = []
            for acc in (gq, gk):
                one = jnp.where(row < 64, acc[p, :, :128], acc[p, :, 128:])
                outs.append(one - pltpu.roll(one, 64, 1))
            gfeat_ref[pl.ds(p * 128, 128), :] = jnp.where(lane < 64, outs[0], -outs[1]).astype(bf16)


def enter_body(groups, me_ref, x_ref, dr_ref, gb_ref, *refs):
    width = x_ref.shape[1]
    grads = refs[:groups]
    wl = refs[groups : groups + 2]
    (dx_ref, sum_ref, w1, sems) = refs[groups + 2 :]

    @pl.when(pl.program_id(0) == 0)
    def _():
        me = me_ref[0]
        copies = fetch_start(wl, w1, me, sems.at[0], 0, 3 * width)
        sum_ref[...] = jnp.zeros_like(sum_ref)
        for c in copies:
            c.wait()

    gb = gb_ref[...]
    _, hat, rstd = normed(x_ref[...].astype(f32), gb[0:1], gb[2:3])
    part = width // groups
    dh = jnp.zeros(x_ref.shape, f32)
    for g in range(groups):
        for i in range(3):
            dh = dh + mm_t(grads[g][:, pl.ds(i * part, part)], w1[:, pl.ds(i * width + g * part, part)])
    dx_ref[...] = dr_ref[...] + normed_back(dh, hat, rstd, gb[0:1])
    sum_ref[0:1] += jnp.sum(dh * hat, axis=0, keepdims=True)
    sum_ref[1:2] += jnp.sum(dh, axis=0, keepdims=True)


def whole(*_):
    return pl.BlockSpec(memory_space=pl.ANY)


def smem():
    return pl.BlockSpec(memory_space=pltpu.SMEM)


def rows_spec(size, cols, back=None):
    if back is None:
        return pl.BlockSpec((size, cols), lambda i: (i, 0))
    return pl.BlockSpec((size, cols), lambda i: (back - 1 - i, 0))


def full_spec(shape):
    zeros = (0,) * len(shape)
    return pl.BlockSpec(shape, lambda i: zeros)


def sds(shape, kind):
    return jax.ShapeDtypeStruct(shape, kind)


def cparams():
    return pltpu.CompilerParams(
        dimension_semantics=("arbitrary",), vmem_limit_bytes=58 * 1024 * 1024
    )


def cost(micros):
    return pl.CostEstimate(
        flops=int(micros * 5e8), transcendentals=0, bytes_accessed=int(micros * 1e6)
    )


def dma(*shape):
    return pltpu.SemaphoreType.DMA(shape)


def shards(n_seq, depth, inputs, resets, norm_gains, norm_biases, w_qkv, w_feat, w_out, w_fc, w_proj, cotangent):
    tokens, width = inputs.shape[1], inputs.shape[2]
    hidden = w_fc.shape[1]
    head_dim = w_feat.shape[1] // 2
    heads = width // head_dim
    pairs = heads // 2
    rows = w_qkv.shape[0]
    nblk = tokens // BT
    x, dy = inputs[0], cotangent[0]
    me = lax.axis_index("seq")
    me_arr = me.reshape(1).astype(jnp.int32)

    marks = resets[0].reshape(nblk, BT).astype(bf16)
    flag = jnp.where(jnp.max(resets) == 0, 1.0, 0.0).astype(bf16)
    upper = jnp.triu(jnp.ones((BT, BT), bf16))
    inner = jnp.dot(marks, upper, preferred_element_type=f32)
    ends = jnp.cumsum(inner[:, -1])
    cend = jnp.concatenate([jnp.zeros((1,), f32), ends])
    counts = inner + cend[:-1, None]
    cnt_col = counts.reshape(tokens, 1)
    cnt_row = counts.reshape(1, tokens)

    norms = jnp.concatenate(
        [norm_gains, norm_biases, jnp.broadcast_to(flag, (rows, 1)), jnp.zeros((rows, 123), bf16)],
        axis=1,
    )
    first = stream_rows(stream_send(jnp.concatenate([w_qkv, w_feat, norms], axis=1), depth), depth)
    first = Spread(first, n_seq, False).near()
    up = jnp.concatenate([w_fc, w_out], axis=1)
    first.far_halves()
    up = stream_send(after(up, first.block), depth)
    first_blocks = first.cores()
    up = stream_rows([after(a, first_blocks[0]) for a in up], depth)
    up = Spread(up, n_seq, True).near(first_blocks[0])
    proj_pieces = stream_send(after(w_proj, first_blocks[1], up.block), depth)
    me_first = after(me_arr, up.block)

    packed = (pairs + 1, 128, 128)
    full = (heads, 128, 128)
    h_one, keys, vals, phi_k, state, gb, feat_all = pl.pallas_call(
        functools.partial(keys_body, n_seq, pairs),
        name="keys",
        cost_estimate=cost(22),
        grid=(tokens // TK,),
        in_specs=[smem(), smem(), rows_spec(TK, width), rows_spec(TK, 1)] + [whole()] * 2,
        out_specs=[rows_spec(TK, width)] * 3
        + [rows_spec(TK, 2 * width), full_spec(packed), full_spec((8, width)), full_spec((width, 128))],
        out_shape=[sds((tokens, width), bf16)] * 3
        + [sds((tokens, 2 * width), bf16), sds(packed, bf16), sds((8, width), f32), sds((width, 128), bf16)],
        scratch_shapes=[
            pltpu.VMEM((width, 2 * width + 256), bf16),
            pltpu.VMEM((pairs, 128, 256), bf16),
            pltpu.VMEM(full, f32),
            dma(2, n_seq),
        ],
        compiler_params=cparams(),
    )(me_first, cend, x, cnt_col, *first_blocks)
    level = lax.axis_index("stream")
    flags = gb[4].reshape(n_seq, depth, rows)[:, :, 0]
    keeps = lax.dynamic_index_in_dim(flags, level, 1, False)
    spread = Spread(state, n_seq, False).near_all()
    up.far_halves(gb)
    proj = Spread(stream_rows([after(a, gb) for a in proj_pieces], depth), n_seq, False).near()
    part_blk = nblk // 2
    local = []
    for part in range(2):
        base = part * part_blk

        def here(size, cols):
            return pl.BlockSpec((size, cols), lambda i: (base + i, 0))

        blocks_out = [
            sds((tokens, width), bf16), sds((tokens, 2 * width), bf16), sds((tokens, width), f32),
            sds((tokens, width), f32), sds((nblk,) + full, bf16),
        ]
        if part:
            me_two = after(me_arr, up_blocks[0], *[proj.found[b] for b in proj.bits], *spread.found.values())
        else:
            me_two = after(me_arr, proj.block, state, after(up.found[up.bits[0]], gb))
        local = pl.pallas_call(
            functools.partial(local_body, base, pairs),
            name="local",
            cost_estimate=cost(15),
            grid=(part_blk,),
            in_specs=[
                smem(), smem(), here(BT, width), here(BT, 2 * width), here(BT, width), here(BT, 1),
                pl.BlockSpec((1, BT), lambda i: (0, base + i)), full_spec((width, 128)),
            ]
            + [whole()] * 2
            + ([full_spec(full)] + [whole()] * 5 if part else []),
            out_specs=[
                here(BT, width), here(BT, 2 * width), here(BT, width), here(BT, width),
                pl.BlockSpec((1,) + full, lambda i: (base + i, 0, 0, 0)), full_spec(full),
            ],
            out_shape=blocks_out + [sds(full, f32)],
            scratch_shapes=[
                pltpu.VMEM((width, width), bf16),
                pltpu.VMEM((pairs, 128, 256), bf16),
                dma(n_seq),
            ],
            input_output_aliases={11 + i: i for i in range(5)} if part else {},
            compiler_params=cparams(),
        )(
            me_two, cend, h_one, phi_k, vals, cnt_col, cnt_row, feat_all, *first_blocks,
            *([local[5]] + list(local[:5]) if part else []),
        )
        if part == 0:
            event = local[5]
            proj.far(event)
            up_blocks = up.cores(event)
    queries, phi_q, num, den, srel, event = local
    states = spread.cores(event)
    proj_blocks = proj.cores(event)

    y, att, h_two, act, d_fc, d_att, d_mid, dd, s_in, g_state, sums = pl.pallas_call(
        functools.partial(middle_body, n_seq, pairs),
        name="middle",
        cost_estimate=cost(43),
        grid=(tokens // TM,),
        in_specs=[
            smem(), smem(), rows_spec(TM, width), rows_spec(TM, width), rows_spec(TM, width),
            rows_spec(TM, width), rows_spec(TM, 2 * width), rows_spec(TM, 1), full_spec((8, width)),
        ]
        + [whole()] * 6,
        out_specs=[
            rows_spec(TM, width), rows_spec(TM, width), rows_spec(TM, width), rows_spec(TM, hidden),
            rows_spec(TM, hidden), rows_spec(TM, width), rows_spec(TM, width), rows_spec(TM, 2 * width),
            full_spec(full), full_spec(packed), full_spec((8, width)),
        ],
        out_shape=[
            sds((tokens, width), bf16), sds((tokens, width), bf16), sds((tokens, width), bf16),
            sds((tokens, hidden), bf16), sds((tokens, hidden), bf16), sds((tokens, width), bf16),
            sds((tokens, width), f32), sds((tokens, 2 * width), bf16), sds(full, bf16), sds(packed, bf16),
            sds((8, width), f32),
        ],
        scratch_shapes=[
            pltpu.VMEM((width, width), bf16),
            pltpu.VMEM((width, hidden), bf16),
            pltpu.VMEM((hidden, width), bf16),
            pltpu.VMEM((TM, width), f32),
            pltpu.VMEM(full, f32),
            pltpu.VMEM((2, n_seq // 2) + packed, bf16),
            dma(4, n_seq),
        ],
        compiler_params=cparams(),
    )(
        me_arr, keeps, x, dy, num, den, phi_q, cnt_col, gb,
        *up_blocks, *proj_blocks, *states,
    )

    spread = Spread(g_state, n_seq, True).near_all()
    norm_two = jnp.stack([sums[3], sums[4]], axis=1).astype(bf16)
    norm_two = jnp.concatenate([norm_two, jnp.zeros((width, 126), bf16)], axis=1)
    nbits = n_seq.bit_length() - 1
    g_fc = mm_f(h_two, d_fc).astype(bf16)
    g_out = mm_f(att, d_att).astype(bf16)
    red_fc = Reduce([g_fc, g_out, norm_two], n_seq, depth, [0] + list(range(1, nbits))[::-1]).send()
    g_states = spread.cores(red_fc.out)
    g_proj = mm_f(after(act, red_fc.out, g_states[0]), dy).astype(bf16)
    red_proj = Reduce([g_proj], n_seq, depth).send()
    red_fc.add(red_proj.out).send()
    red_proj.add(red_fc.out).send()
    me_back = after(me_arr, red_proj.out, red_fc.out)
    groups = 2
    some = pairs // groups
    part = some * 128
    d_qkv, g_feat = [], []
    for g in range(groups):

        def spec(cols):
            return pl.BlockSpec((BT, cols), lambda i: (nblk - 1 - i, g))

        def one_group(shape):
            return pl.BlockSpec(shape, lambda i: (g,) + (0,) * (len(shape) - 1))

        one = (2 * some, 128, 128)
        d_one, g_one = pl.pallas_call(
            functools.partial(back_body, g * some, some, pairs),
            name="back",
            cost_estimate=cost(19),
            grid=(nblk,),
            in_specs=[
                smem(), smem(), smem(), spec(part), spec(part), spec(part), spec(2 * part), spec(2 * part),
                spec(2 * part), pl.BlockSpec((1,) + one, lambda i: (nblk - 1 - i, g, 0, 0)), one_group(one),
                rows_spec(BT, 1, nblk), pl.BlockSpec((1, BT), lambda i: (0, nblk - 1 - i)),
                one_group((part, 128)),
            ]
            + [whole()] * 2,
            out_specs=[rows_spec(BT, 3 * part, nblk), full_spec((part, 128))],
            out_shape=[sds((tokens, 3 * part), bf16), sds((part, 128), bf16)],
            scratch_shapes=[
                pltpu.VMEM((some, 128, 256), bf16),
                pltpu.VMEM((some, 128, 256), bf16),
                pltpu.VMEM(one, f32),
                pltpu.VMEM((some, 128, 256), f32),
                pltpu.VMEM((some, 128, 256), f32),
                pltpu.VMEM((2, n_seq // 2) + packed, bf16),
                dma(n_seq),
            ],
            compiler_params=cparams(),
        )(
            me_back, keeps, cend, queries, keys, vals, phi_q, phi_k, dd, srel, s_in, cnt_col, cnt_row,
            feat_all, *g_states,
        )
        d_qkv.append(d_one)
        g_feat.append(g_one)
        if g == 0:
            red_proj.add(d_one).send()
            me_back = after(me_arr, red_proj.out)

    last = d_qkv[-1]
    g_qkv = [mm_f(h_one, d).astype(bf16) for d in d_qkv]
    red_two = Reduce(g_qkv + [jnp.concatenate(g_feat, axis=0)], n_seq, depth).send()
    red_fc.add(red_two.out).send()
    red_proj.add(red_fc.out).send_stream()
    me_late = after(me_arr, red_proj.out, red_fc.out)
    dx, sums_one = pl.pallas_call(
        functools.partial(enter_body, groups),
        name="enter",
        cost_estimate=cost(11),
        grid=(tokens // TM,),
        in_specs=[smem(), rows_spec(TM, width), rows_spec(TM, width), full_spec((8, width))]
        + [rows_spec(TM, 3 * part)] * groups
        + [whole()] * 2,
        out_specs=[rows_spec(TM, width), full_spec((8, width))],
        out_shape=[sds((tokens, width), f32), sds((8, width), f32)],
        scratch_shapes=[pltpu.VMEM((width, 3 * width), bf16), dma(2, n_seq)],
        compiler_params=cparams(),
    )(me_late, x, d_mid, gb, *d_qkv, *first_blocks)
    norm_one = jnp.stack([sums_one[0], sums_one[1]], axis=1).astype(bf16)
    norm_one = jnp.concatenate([norm_one, jnp.zeros((width, 126), bf16)], axis=1)
    red_norm = Reduce([norm_one], n_seq, depth).send()
    grad_proj = red_proj.done(dx)
    red_a, red_b = red_two.add(grad_proj).cut((groups * 3 * part + 256) // 2)
    red_a.send()
    red_norm.add(red_a.out)
    red_b.cur = [beside(red_b.cur + red_norm.cur)]
    red_b.send()
    red_fc.add(red_a.out, red_b.out).send_stream()
    while red_a.order:
        red_a.add().send()
        red_b.add().send()
    tail = Reduce(red_a.add().cur + red_b.add().cur, n_seq, depth, [], []).send_stream()
    grad_up = red_fc.done(tail.out)
    squares = sum(
        jnp.sum(after(stack[:, pairs, :3, 126:], tail.out).astype(f32), axis=(0, 2))
        for stack in g_states
    )
    branch_rms = jnp.sqrt(squares / (tokens * n_seq * width)).reshape(1, 3)
    tail = tail.done()
    grads = [tail[:, g * 3 * part : (g + 1) * 3 * part] for g in range(groups)]
    grad_feat = tail[:, groups * 3 * part : groups * 3 * part + 128]
    norm_one = tail[:, groups * 3 * part + 128 :]
    grad_fc = grad_up[:, :hidden]
    grad_out = grad_up[:, hidden:]
    grad_qkv = jnp.concatenate(
        [grads[g][:, i * part : (i + 1) * part] for i in range(3) for g in range(groups)], axis=1
    )
    return (
        y[None],
        dx[None],
        jnp.concatenate([norm_one[:, 0:1], grad_out[:, width : width + 1]], axis=1),
        jnp.concatenate([norm_one[:, 1:2], grad_out[:, width + 1 : width + 2]], axis=1),
        grad_qkv,
        grad_feat,
        grad_out[:, :width],
        grad_fc,
        grad_proj,
        branch_rms,
    )


def solution(mesh):
    both = P(("seq", "stream"), None)
    acts = P("stream", "seq", None)
    placed = (acts, P("stream", "seq"), both, both, both, both, both, both, both, acts)
    return jax.shard_map(
        functools.partial(shards, mesh.shape["seq"], mesh.shape["stream"]),
        mesh=mesh,
        in_specs=placed,
        out_specs=(acts, acts, both, both, both, both, both, both, both, P("stream", None)),
        check_vma=False,
    )
```
